32 devices in a mesh: wide: 16 (over z, y, core), narrow: 2 (over x).
Axes of the slice: x: 2, y: 2, z: 4, core: 2. Of those that a mesh axis runs over, the one named last changes fastest.
Arguments:
- block_in: bfloat16 [32768, 768], P(('wide', 'narrow')), may hold values from -6 to 6
- out_grad: bfloat16 [32768, 768], P(('wide', 'narrow')), may hold values from -6 to 6
- seq_lens: int32 [16, 4], P('wide'), may hold values from 0 to 2048, as said below
- qkv_weight: bfloat16 [768, 2304], P(None, 'narrow'), may hold values from -0.21875 to 0.21875
- qkv_bias: bfloat16 [2304], P('narrow'), may hold values from -0.5 to 0.5
- out_weight: bfloat16 [768, 768], P('narrow'), may hold values from -0.875 to 0.875
- out_bias: bfloat16 [768], replicated, may hold values from -0.5 to 0.5
- up_weight: bfloat16 [768, 3072], P(None, 'narrow'), may hold values from -0.21875 to 0.21875
- up_bias: bfloat16 [3072], P('narrow'), may hold values from -0.5 to 0.5
- down_weight: bfloat16 [3072, 768], P('narrow'), may hold values from -0.109375 to 0.109375
- down_bias: bfloat16 [768], replicated, may hold values from -0.5 to 0.5
- attn_gain: bfloat16 [768], replicated, may hold values from 0.5 to 1.5
- attn_shift: bfloat16 [768], replicated, may hold values from -0.5 to 0.5
- ffn_gain: bfloat16 [768], replicated, may hold values from 0.5 to 1.5
- ffn_shift: bfloat16 [768], replicated, may hold values from -0.5 to 0.5
Outputs:
- block_out: bfloat16 [32768, 768], P(('wide', 'narrow'))
- in_grad: bfloat16 [32768, 768], P(('wide', 'narrow'))
- grad_qkv_weight: float32 [768, 2304], P(None, 'narrow')
- grad_qkv_bias: float32 [2304], P('narrow')
- grad_out_weight: float32 [768, 768], P('narrow')
- grad_out_bias: float32 [768], replicated
- grad_up_weight: float32 [768, 3072], P(None, 'narrow')
- grad_up_bias: float32 [3072], P('narrow')
- grad_down_weight: float32 [3072, 768], P('narrow')
- grad_down_bias: float32 [768], replicated
- grad_attn_gain: float32 [768], replicated
- grad_attn_shift: float32 [768], replicated
- grad_ffn_gain: float32 [768], replicated
- grad_ffn_shift: float32 [768], replicated
The draws below stay inside these ranges and needn't reach their ends.
Inputs may be any that keep to these rules, and one draw needn't show every extreme that they name: `seq_lens`: each row is either 2048 followed by zeros or 512 in every slot; both kinds occur in every draw.
All inputs are finite; a program needn't handle non-finite values.
Results may differ from the reference program's by a relative error of at most 0.011.
Values may be sent and summed in bfloat16 or wider, within the bound.
No kernel may reach another device: no remote copies, remote signals or barrier semaphores. Data moves between devices by JAX's collectives and lax.ppermute only.
A program may use at most 256 MiB of HBM per device.

```python
import jax
import jax.numpy as jnp
from jax import lax

D = 768
H = 12
HD = 64
ROT = 16
FF = 3072
SEQ_LEN = 2048
SEQ_SLOTS = 4
SHORT_LEN = 512
GROUPS = 16
TOKENS = 32768


def draw_seq_lens(key, part):
    kind_key, long_key, short_key = jax.random.split(key, 3)
    group_kind = jax.random.randint(kind_key, (GROUPS,), 0, 2)
    long_at = jax.random.randint(long_key, (), 0, GROUPS)
    short_at = (long_at + jax.random.randint(short_key, (), 1, GROUPS)) % GROUPS
    group_index = jnp.arange(GROUPS)
    group_kind = jnp.where(group_index == long_at, 1, group_kind)
    group_kind = jnp.where(group_index == short_at, 0, group_kind)
    slot_index = jnp.arange(SEQ_SLOTS)
    long_row = jnp.where(slot_index == 0, SEQ_LEN, 0)
    short_row = jnp.full((SEQ_SLOTS,), SHORT_LEN)
    return jnp.where(group_kind[:, None] == 1, long_row[None, :], short_row[None, :]).astype(jnp.int32)


def block_scale(own_key, shape, cuts, least, largest):
    def one(position, blocks):
        steps = jax.random.uniform(jax.random.fold_in(jax.random.fold_in(own_key, 6), position), (blocks,), jnp.float32, least / len(cuts), largest / len(cuts))
        return jnp.repeat(jnp.exp(steps), shape[position] // blocks).reshape((-1,) + (1,) * (len(shape) - position - 1))

    factor_of = one(*cuts[0])
    for cut in cuts[1:]:
        factor_of = factor_of * one(*cut)
    return factor_of


def centred(key, shape, scale, bound, cuts=(), held_as=jnp.bfloat16):
    entries = jax.random.normal(key, shape, jnp.float32) * scale
    if len(cuts) > 0:
        entries = block_scale(key, shape, cuts, -0.22, 0.18) * entries
    return jnp.clip(entries, min=-bound, max=bound).astype(held_as)


def setup_inputs(seed: int = 0) -> dict:
    streams_of = jax.random.split(jax.random.key(seed), 16)
    block_in = centred(streams_of[0], (TOKENS, D), 1.0, 6.0, ((0, 32),))
    out_grad = centred(streams_of[1], (TOKENS, D), 1.0, 6.0, ((0, 32),))
    seq_lens = draw_seq_lens(jax.random.fold_in(streams_of[15], 71), 0)
    qkv_weight = centred(streams_of[3], (D, 3 * D), D ** -0.5, 0.21875, ((1, 2),))
    qkv_bias = jnp.clip(jax.random.uniform(streams_of[4], (3 * D,), jnp.float32, -0.5, 0.5) * block_scale(streams_of[4], (3 * D,), ((0, 2),), -0.4, 0.0), -0.5, 0.5).astype(jnp.bfloat16)
    out_weight = centred(streams_of[5], (D, D), (D // 16) ** -0.5, 0.875, ((0, 2),))
    out_bias = jnp.clip(jax.random.uniform(streams_of[6], (D,), jnp.float32, -0.5, 0.5), -0.5, 0.5).astype(jnp.bfloat16)
    up_weight = centred(streams_of[7], (D, FF), D ** -0.5, 0.21875, ((1, 2),))
    up_bias = jnp.clip(jax.random.uniform(streams_of[8], (FF,), jnp.float32, -0.5, 0.5) * block_scale(streams_of[8], (FF,), ((0, 2),), -0.4, 0.0), -0.5, 0.5).astype(jnp.bfloat16)
    down_weight = centred(streams_of[9], (FF, D), FF ** -0.5, 0.109375, ((0, 2),))
    down_bias = jnp.clip(jax.random.uniform(streams_of[10], (D,), jnp.float32, -0.5, 0.5), -0.5, 0.5).astype(jnp.bfloat16)
    attn_gain = jnp.clip(1.0 + 0.1 * jax.random.normal(streams_of[11], (D,), jnp.float32), 0.5, 1.5).astype(jnp.bfloat16)
    attn_shift = jnp.clip(jax.random.uniform(streams_of[12], (D,), jnp.float32, -0.5, 0.5), -0.5, 0.5).astype(jnp.bfloat16)
    ffn_gain = jnp.clip(1.0 + 0.1 * jax.random.normal(streams_of[13], (D,), jnp.float32), 0.5, 1.5).astype(jnp.bfloat16)
    ffn_shift = jnp.clip(jax.random.uniform(streams_of[14], (D,), jnp.float32, -0.5, 0.5), -0.5, 0.5).astype(jnp.bfloat16)
    return dict(block_in=block_in, out_grad=out_grad, seq_lens=seq_lens, qkv_weight=qkv_weight, qkv_bias=qkv_bias, out_weight=out_weight, out_bias=out_bias, up_weight=up_weight, up_bias=up_bias, down_weight=down_weight, down_bias=down_bias, attn_gain=attn_gain, attn_shift=attn_shift, ffn_gain=ffn_gain, ffn_shift=ffn_shift)


EPS = 1e-05
NEG = -1e+30
HIGH = lax.Precision.HIGHEST

@jax.custom_vjp
def low(v):
    return lax.optimization_barrier(v.astype(jnp.bfloat16)).astype(jnp.float32)

@jax.custom_vjp
def low_back(v):
    return v

def low_keep(v):
    return (low(v), None)

def low_pass(kept, grad):
    return (grad,)

def back_keep(v):
    return (v, None)

def back_low(kept, grad):
    return (low(grad),)
low.defvjp(low_keep, low_pass)
low_back.defvjp(back_keep, back_low)

def norm_rows(rows, gain, shift):
    center = lax.optimization_barrier(jnp.mean(rows, axis=-1, keepdims=True))
    offset = rows - center
    spread = lax.optimization_barrier(jnp.mean(offset * offset, axis=-1, keepdims=True))
    return offset * lax.rsqrt(spread + EPS) * gain + shift

def rotate(heads_rows, place):
    half = ROT // 2
    freq = 1.0 / 10000.0 ** (jnp.arange(half, dtype=jnp.float32) * 2.0 / ROT)
    angle = place[:, None].astype(jnp.float32) * freq[None, :]
    cosine = jnp.cos(angle)[:, None, :]
    sine = jnp.sin(angle)[:, None, :]
    first = heads_rows[..., :half]
    second = heads_rows[..., half:ROT]
    return jnp.concatenate([first * cosine - second * sine, second * cosine + first * sine, heads_rows[..., ROT:]], axis=-1)

def positions(lens_row, group_rows):
    ends = jnp.cumsum(lens_row).astype(jnp.int32)
    starts = ends - lens_row
    token_index = jnp.arange(group_rows, dtype=jnp.int32)
    segment = lax.optimization_barrier(jnp.sum((token_index[:, None] >= ends[None, :]).astype(jnp.int32), axis=1))
    chosen = segment[:, None] == jnp.arange(lens_row.shape[0], dtype=jnp.int32)[None, :]
    begin = lax.optimization_barrier(jnp.sum(jnp.where(chosen, starts[None, :], 0), axis=1)).astype(jnp.int32)
    return (segment, token_index - begin)

def group_layer(rows, lens_row, weights):
    weight_qkv, bias_qkv, weight_out, bias_out, weight_up, bias_up, weight_down, bias_down, gain_attn, shift_attn, gain_ffn, shift_ffn = weights
    group_rows = rows.shape[0]
    segment, place = positions(lens_row, group_rows)
    first_in = low(norm_rows(rows, gain_attn, shift_attn))
    second_in = low(norm_rows(rows, gain_ffn, shift_ffn))
    packed = low_back(jnp.dot(first_in, weight_qkv, precision=HIGH) + bias_qkv).reshape(group_rows, H, 3 * HD)
    queries = low(rotate(packed[..., :HD], place))
    keys_all = low(rotate(packed[..., HD:2 * HD], place))
    values = low(packed[..., 2 * HD:])
    scores = low_back(jnp.einsum('qhd,khd->hqk', queries, keys_all, precision=HIGH) * 0.125)
    token_index = jnp.arange(group_rows, dtype=jnp.int32)
    allowed = (segment[:, None] == segment[None, :]) & (token_index[None, :] <= token_index[:, None])
    scores = jnp.where(allowed[None], scores, NEG)
    top = lax.optimization_barrier(jnp.max(scores, axis=-1, keepdims=True))
    expo = jnp.exp(scores - top)
    probs = expo / lax.optimization_barrier(jnp.sum(expo, axis=-1, keepdims=True))
    context = jnp.einsum('hqk,khd->qhd', low(probs), values, precision=HIGH).reshape(group_rows, D)
    context = low(low_back(context))
    attention = jnp.dot(context, weight_out, precision=HIGH) + bias_out
    hidden_pre = low_back(jnp.dot(second_in, weight_up, precision=HIGH) + bias_up)
    activated = low(jax.nn.gelu(hidden_pre, approximate=False))
    feedforward = jnp.dot(activated, weight_down, precision=HIGH) + bias_down
    return rows + attention + feedforward

def reference(block_in, out_grad, seq_lens, qkv_weight, qkv_bias, out_weight, out_bias, up_weight, up_bias, down_weight, down_bias, attn_gain, attn_shift, ffn_gain, ffn_shift):
    params = tuple((param.astype(jnp.float32) for param in (qkv_weight, qkv_bias, out_weight, out_bias, up_weight, up_bias, down_weight, down_bias, attn_gain, attn_shift, ffn_gain, ffn_shift)))

    def forward(inputs, weights):

        def scan_step(carry, item):
            rows, lens_row = item
            return (carry, jax.checkpoint(group_layer)(rows, lens_row, weights))
        _, outputs = lax.scan(scan_step, jnp.zeros((), jnp.float32), (inputs.reshape(GROUPS, SEQ_LEN, D), seq_lens))
        return outputs.reshape(GROUPS * SEQ_LEN, D)
    outputs, backward = jax.vjp(forward, block_in.astype(jnp.float32), params)
    in_grad, grads = backward(out_grad.astype(jnp.float32))
    return (outputs.astype(jnp.bfloat16), in_grad.astype(jnp.bfloat16), grads[0], grads[1], grads[2], grads[3], grads[4], grads[5], grads[6], grads[7], grads[8], grads[9], grads[10], grads[11])
```

```python
import functools

import jax
import jax.numpy as jnp
import numpy as np
from jax import lax
from jax.experimental import pallas as pl
from jax.experimental.pallas import tpu as pltpu
from jax.sharding import PartitionSpec as P

HD = 64
ROT = 16
EPS = 1e-05
NEG = -1e30
SCALE = 0.125
SHORT_LEN = 512
F32 = jnp.float32
BF = jnp.bfloat16
LANES = 128
BQ = 512
BS = 256
ROWS = 256
VMEM_LIMIT = 58 << 20


def nn(a, b):
    return lax.dot_general(a, b, (((1,), (0,)), ((), ())), preferred_element_type=F32)


def nt(a, b):
    return lax.dot_general(a, b, (((1,), (1,)), ((), ())), preferred_element_type=F32)


def tn(a, b):
    return lax.dot_general(a, b, (((0,), (0,)), ((), ())), preferred_element_type=F32)


def colsum(a):
    return jnp.sum(a, axis=0, keepdims=True)


def rope_table(rows):
    half = ROT // 2
    freq = np.float32(1.0) / np.float32(10000.0) ** (
        np.arange(half, dtype=np.float32) * np.float32(2.0) / np.float32(ROT)
    )
    angle = np.arange(rows, dtype=np.float32)[:, None] * freq.astype(np.float32)[None, :]
    table = np.zeros((rows, 2 * HD), np.float32)
    table[:, :HD] = 1.0
    table[:, :half] = table[:, half:ROT] = np.cos(angle)
    table[:, HD : HD + half] = -np.sin(angle)
    table[:, HD + half : HD + ROT] = np.sin(angle)
    return table


def rope(x, table, back):
    lane = lax.broadcasted_iota(jnp.int32, x.shape, 1)
    other = pltpu.roll(table, HD, 1)
    cosine = jnp.where(lane < HD, table, other)
    sine = jnp.where(lane < HD, other, table)
    partner = jnp.where(
        lane % HD < ROT // 2, pltpu.roll(x, LANES - ROT // 2, 1), pltpu.roll(x, ROT // 2, 1)
    )
    return x * cosine - partner * sine if back else x * cosine + partner * sine


def normalize(x):
    center = jnp.mean(x, axis=-1, keepdims=True)
    offset = x - center
    inverse = lax.rsqrt(jnp.mean(offset * offset, axis=-1, keepdims=True) + EPS)
    return offset * inverse, inverse


def once(shape):
    return pl.BlockSpec(shape, lambda i, m: (0,) * len(shape), pipeline_mode=pl.Buffered(1))


def params(**more):
    return pltpu.CompilerParams(
        vmem_limit_bytes=VMEM_LIMIT, dimension_semantics=("arbitrary",), **more
    )


def front_kernel(carry, meta, *refs):
    (x_ref, g_ref, qkv_w, qkv_b, up_w, up_b, down_w, out_w, ag, ash, fg, fsh, tab_ref), refs = (
        refs[:13],
        refs[13:],
    )
    if carry:
        (_, _, up_in, down_in), refs = refs[:4], refs[4:]
    (qkv_ref, gc_ref, ffn_ref, s_ref, gup_ref, gdown_ref, vec_ref, vech_ref), refs = (
        refs[:8],
        refs[8:],
    )
    up_acc, down_acc = refs if carry else (gup_ref, gdown_ref)
    i = pl.program_id(0)
    rows = x_ref.shape[0]
    x = x_ref[...].astype(F32)
    g = g_ref[...]
    normed, _ = normalize(x)
    first = (normed * ag[...].astype(F32) + ash[...].astype(F32)).astype(BF)
    second = (normed * fg[...].astype(F32) + fsh[...].astype(F32)).astype(BF)

    @pl.when(i == 0)
    def _():
        if carry:
            up_acc[...] = up_in[...]
            down_acc[...] = down_in[...]
        else:
            up_acc[...] = jnp.zeros_like(up_acc)
            down_acc[...] = jnp.zeros_like(down_acc)
        vec_ref[...] = jnp.zeros_like(vec_ref)
        vech_ref[...] = jnp.zeros_like(vech_ref)

    packed = nn(first, qkv_w[...]) + qkv_b[...].astype(F32)
    third = packed.shape[1] // 3
    table = tab_ref[...]
    for c in range(0, third, LANES):
        q = rope(packed[:, c : c + LANES], table, False).astype(BF)
        qkv_ref[:, c : c + LANES] = (q.astype(F32) * SCALE).astype(BF)
        qkv_ref[:, third + c : third + c + LANES] = rope(
            packed[:, third + c : third + c + LANES], table, False
        ).astype(BF)
    qkv_ref[:, 2 * third :] = packed[:, 2 * third :].astype(BF)
    gc_ref[...] = nt(g, out_w[...]).astype(BF)

    hidden = nn(second, up_w[...]) + up_b[...].astype(F32)
    phi = 0.5 * (1.0 + lax.erf(hidden * np.float32(0.5**0.5)))
    density = jnp.exp(-0.5 * hidden * hidden) * np.float32(1.0 / np.sqrt(2.0 * np.pi))
    act = (hidden * phi).astype(BF)
    ffn_ref[...] = nn(act, down_w[...])
    gh_full = nt(g, down_w[...]) * (phi + hidden * density)
    gh = gh_full.astype(BF)
    gs = nt(gh, up_w[...])
    s_ref[...] = gs * fg[...].astype(F32)
    vec_ref[0:1, :] += colsum(gs * normed)
    vec_ref[1:2, :] += colsum(gs)
    vec_ref[2:3, :] += colsum(g.astype(F32))
    vech_ref[0:1, :] += colsum(gh.astype(F32))
    up_acc[...] += tn(second, gh)
    down_acc[...] += tn(act, g)
    if carry:

        @pl.when(i == pl.num_programs(0) - 1)
        def _():
            gup_ref[...] = up_acc[...].astype(BF)
            gdown_ref[...] = down_acc[...].astype(BF)


def front(meta, x, g, weights, table, group_rows, carry=None):
    qkv_w, qkv_b, up_w, up_b, down_w, out_w, ag, ash, fg, fsh = weights
    count, d = x.shape
    steps = count // ROWS
    heads_cols = out_w.shape[0]
    hidden = up_w.shape[1]
    per_short = SHORT_LEN // ROWS
    here = lambda i, m: (i, 0)
    there = lambda i, m: (m[1] * steps + i, 0)
    tab = lambda i, m: (
        jnp.where(m[0] == 1, m[1] * steps + i, lax.rem(m[1] * steps + i, per_short)),
        0,
    )
    grads_type = F32 if carry is None else BF
    in_specs = [
        pl.BlockSpec((ROWS, d), here),
        pl.BlockSpec((ROWS, d), here),
        *[once(w.shape) for w in weights],
        pl.BlockSpec((ROWS, 2 * HD), tab),
    ]
    out_specs = [
        pl.BlockSpec((ROWS, 3 * heads_cols), there),
        pl.BlockSpec((ROWS, heads_cols), there),
        pl.BlockSpec((ROWS, d), here),
        pl.BlockSpec((ROWS, d), here),
        once((d, hidden)),
        once((hidden, d)),
        once((8, d)),
        once((8, hidden)),
    ]
    out_shape = [
        jax.ShapeDtypeStruct((group_rows, 3 * heads_cols), BF),
        jax.ShapeDtypeStruct((group_rows, heads_cols), BF),
        jax.ShapeDtypeStruct((count, d), F32),
        jax.ShapeDtypeStruct((count, d), F32),
        jax.ShapeDtypeStruct((d, hidden), grads_type),
        jax.ShapeDtypeStruct((hidden, d), grads_type),
        jax.ShapeDtypeStruct((8, d), F32),
        jax.ShapeDtypeStruct((8, hidden), F32),
    ]
    args = [meta, x, g, *weights, table]
    scratch, aliases = [], {}
    if carry is not None:
        qkv_prev, gc_prev, gup_prev, gdown_prev = carry
        in_specs += [
            pl.BlockSpec(memory_space=pl.ANY),
            pl.BlockSpec(memory_space=pl.ANY),
            once((d, hidden)),
            once((hidden, d)),
        ]
        aliases = {len(args): 0, len(args) + 1: 1}
        args += [qkv_prev, gc_prev, gup_prev, gdown_prev]
        scratch = [pltpu.VMEM((d, hidden), F32), pltpu.VMEM((hidden, d), F32)]
    flops = 2 * count * d * (6 * hidden + 3 * heads_cols + heads_cols)
    return pl.pallas_call(
        functools.partial(front_kernel, carry is not None),
        grid_spec=pltpu.PrefetchScalarGridSpec(
            num_scalar_prefetch=1,
            grid=(steps,),
            in_specs=in_specs,
            out_specs=out_specs,
            scratch_shapes=scratch,
        ),
        out_shape=out_shape,
        input_output_aliases=aliases,
        compiler_params=params(),
        cost_estimate=pl.CostEstimate(
            flops=flops, bytes_accessed=40 << 20, transcendentals=2 * count * hidden
        ),
        name="front_second" if carry is not None else "front_first",
    )(*args)


def attention_kernel(meta, q_ref, k_ref, v_ref, do_ref, tab_ref, *refs):
    ctx_ref, dq_ref, dk_ref, dv_ref, s_sc, e_sc, ds_sc, kt_sc, vt_sc, dk_sc, dv_sc = refs
    i = pl.program_id(1)
    qb = meta[2 + i]
    long = meta[0]
    rows = k_ref.shape[0]
    wide_cols, half_cols = 2 * BQ, 2 * BS
    ext = HD + 16

    @pl.when(i == 0)
    def _():
        dk_sc[...] = jnp.zeros_like(dk_sc)
        dv_sc[...] = jnp.zeros_like(dv_sc)
        kt_sc[...] = k_ref[...].T
        ones = jnp.ones((16, rows), BF)
        vt = v_ref[...].T
        for h in range(2):
            vt_sc[h * ext : h * ext + HD, :] = vt[h * HD : (h + 1) * HD]
            vt_sc[h * ext + HD : (h + 1) * ext, :] = ones

    def process(base, tiles):
        def keys(start, count):
            row = base + start * BS
            return pl.ds(row if isinstance(row, int) else pl.multiple_of(row, BS), count * BS)

        zeros_t = jnp.zeros((HD, BS), BF)
        zeros = jnp.zeros((BS, LANES), BF)
        lane = lax.broadcasted_iota(jnp.int32, (BS, LANES), 1)

        def wide(t):
            return jnp.concatenate(
                [
                    jnp.concatenate(pair, 0)
                    for a in range(0, BQ, BS)
                    for pair in ([t[:HD, a : a + BS], zeros_t], [zeros_t, t[HD:, a : a + BS]])
                ],
                1,
            )

        def tall(t):
            return jnp.concatenate(
                [
                    block
                    for a in range(0, BQ, BS)
                    for block in (
                        jnp.where(lane < HD, t[a : a + BS], zeros),
                        jnp.where(lane < HD, zeros, t[a : a + BS]),
                    )
                ],
                0,
            )

        queries = q_ref[...]
        q_wide, q_tall = wide(queries.T), tall(queries)
        key_index = lax.broadcasted_iota(jnp.int32, (BS, half_cols), 0)
        query_index = lax.broadcasted_iota(jnp.int32, (BS, half_cols), 1) % BS
        causal = key_index <= query_index
        first_col = lambda t: half_cols if t == tiles - 1 else 0
        top = jnp.full((8, wide_cols), NEG, F32)
        for t in range(tiles):
            lo = first_col(t)
            s = nn(k_ref[keys(t, 1), :], q_wide[:, lo:])
            if t == tiles - 1:
                s = jnp.where(causal, s, NEG)
            if t == tiles - 2:
                s = jnp.concatenate(
                    [jnp.where(causal, s[:, :half_cols], NEG), s[:, half_cols:]], 1
                )
            s_sc[t * BS : (t + 1) * BS, lo:] = s
            part = jnp.max(s.reshape(BS // 8, 8, wide_cols - lo), axis=0)
            if lo:
                top = jnp.concatenate([top[:, :lo], jnp.maximum(top[:, lo:], part)], 1)
            else:
                top = jnp.maximum(top, part)
        top = jnp.max(top, axis=0, keepdims=True)
        for t in range(tiles):
            lo = first_col(t)
            block = slice(t * BS, (t + 1) * BS)
            e_sc[block, lo:] = jnp.exp(s_sc[block, lo:] - top[:, lo:]).astype(BF)
        grad_t = do_ref[...].astype(F32).T
        ctx_parts, grad_parts, weighted = [[], []], [[], []], []
        for a in range(2):
            count = tiles - 1 + a
            for h in range(2):
                c = a * half_cols + h * BS
                r = nn(vt_sc[h * ext : (h + 1) * ext, keys(0, count)], e_sc[: count * BS, c : c + BS])
                over_total = 1.0 / r[HD : HD + 1]
                ctx = r[:HD] * over_total
                grad = (grad_t[h * HD : (h + 1) * HD, a * BS : (a + 1) * BS] * over_total).astype(BF)
                weighted.append(colsum(ctx * grad.astype(F32)))
                ctx_parts[a].append(ctx)
                grad_parts[a].append(grad)
        full = lambda parts: jnp.concatenate([jnp.concatenate(part, 0) for part in parts], 1)
        ctx_ref[...] = full(ctx_parts).T.astype(BF)
        grad_full = full(grad_parts)
        g_wide, g_tall = wide(grad_full), tall(grad_full.T)
        weighted = jnp.concatenate(weighted, 1)
        for t in range(tiles):
            lo = first_col(t)
            block = slice(t * BS, (t + 1) * BS)
            e = e_sc[block, lo:]
            gp = nn(v_ref[keys(t, 1), :], g_wide[:, lo:])
            ds = (e.astype(F32) * (gp - weighted[:, lo:])).astype(BF)
            ds_sc[block, lo:] = ds
            dv_sc[keys(t, 1), :] += nn(e, g_tall[lo:])
            dk_sc[keys(t, 1), :] += nn(ds, q_tall[lo:])
        dq_parts = [[], []]
        for a in range(2):
            count = tiles - 1 + a
            for h in range(2):
                c = a * half_cols + h * BS
                dq_parts[a].append(
                    nn(kt_sc[h * HD : (h + 1) * HD, keys(0, count)], ds_sc[: count * BS, c : c + BS])
                )
        at = pl.multiple_of(jnp.where(long == 1, qb, 0) * BQ, BQ)
        dq_ref[...] = rope(full(dq_parts).T * SCALE, tab_ref[pl.ds(at, BQ), :], True).astype(BF)

    for c in range(rows // BQ):

        @pl.when((long == 1) & (qb == c))
        def _(c=c):
            process(0, (c + 1) * (BQ // BS))

    @pl.when(long == 0)
    def _():
        process(qb * BQ, BQ // BS)

    @pl.when(i == pl.num_programs(1) - 1)
    def _():
        dv_ref[...] = dv_sc[...].astype(BF)

        def finish(b, _):
            block = pl.ds(pl.multiple_of(b * BQ, BQ), BQ)
            at = pl.multiple_of(jnp.where(long == 1, b, 0) * BQ, BQ)
            dk_ref[block, :] = rope(dk_sc[block, :], tab_ref[pl.ds(at, BQ), :], True).astype(BF)
            return 0

        lax.fori_loop(0, rows // BQ, finish, 0)


def attention(meta, qkv, grad_ctx, table):
    rows, cols = grad_ctx.shape
    pairs, blocks = cols // LANES, rows // BQ
    at_query = lambda p, i, m: (m[2 + i], p)
    whole = lambda part: lambda p, i, m: (0, part * pairs + p)
    kept = jax.ShapeDtypeStruct((rows, cols), BF)
    area = rows * rows // 2 * cols
    return pl.pallas_call(
        attention_kernel,
        grid_spec=pltpu.PrefetchScalarGridSpec(
            num_scalar_prefetch=1,
            grid=(pairs, blocks),
            in_specs=[
                pl.BlockSpec((BQ, LANES), at_query),
                pl.BlockSpec((rows, LANES), whole(1)),
                pl.BlockSpec((rows, LANES), whole(2)),
                pl.BlockSpec((BQ, LANES), at_query),
                pl.BlockSpec((rows, LANES), lambda p, i, m: (0, 0), pipeline_mode=pl.Buffered(1)),
            ],
            out_specs=[
                pl.BlockSpec((BQ, LANES), at_query),
                pl.BlockSpec((BQ, LANES), at_query),
                pl.BlockSpec((rows, LANES), whole(0)),
                pl.BlockSpec((rows, LANES), whole(0)),
            ],
            scratch_shapes=[
                pltpu.VMEM((rows, 2 * BQ), F32),
                pltpu.VMEM((rows, 2 * BQ), BF),
                pltpu.VMEM((rows, 2 * BQ), BF),
                pltpu.VMEM((LANES, rows), BF),
                pltpu.VMEM((2 * (HD + 16), rows), BF),
                pltpu.VMEM((rows, LANES), F32),
                pltpu.VMEM((rows, LANES), F32),
            ],
        ),
        out_shape=[kept] * 4,
        compiler_params=pltpu.CompilerParams(
            vmem_limit_bytes=VMEM_LIMIT, dimension_semantics=("arbitrary", "arbitrary")
        ),
        cost_estimate=pl.CostEstimate(
            flops=4 * 12 * area, bytes_accessed=20 << 20, transcendentals=area // HD
        ),
        name="attention",
    )(meta, qkv, qkv, qkv, grad_ctx, table)


def back_kernel(carry, meta, *refs):
    (x_ref, ctx_ref, gq_ref, gk_ref, gv_ref, g_ref, ffn_ref, sf_ref, qkv_w, out_w, ag, ash), refs = (
        refs[:12],
        refs[12:],
    )
    if carry:
        (qkv_in, out_in), refs = refs[:2], refs[2:]
    (part_ref, s_ref, gqkv_ref, gout_ref, vec_ref, vecq_ref), refs = refs[:6], refs[6:]
    qkv_acc, out_acc = refs if carry else (gqkv_ref, gout_ref)
    i = pl.program_id(0)
    normed, _ = normalize(x_ref[...].astype(F32))
    gain = ag[...].astype(F32)
    first = (normed * gain + ash[...].astype(F32)).astype(BF)

    @pl.when(i == 0)
    def _():
        if carry:
            qkv_acc[...] = qkv_in[...]
            out_acc[...] = out_in[...]
        else:
            qkv_acc[...] = jnp.zeros_like(qkv_acc)
            out_acc[...] = jnp.zeros_like(out_acc)
        vec_ref[...] = jnp.zeros_like(vec_ref)
        vecq_ref[...] = jnp.zeros_like(vecq_ref)

    ctx = ctx_ref[...]
    part_ref[...] = (nn(ctx, out_w[...]) + ffn_ref[...]).astype(part_ref.dtype)
    packed = jnp.concatenate([gq_ref[...], gk_ref[...], gv_ref[...]], axis=1)
    grad_first = nt(packed, qkv_w[...])
    s_ref[...] = (grad_first * gain + sf_ref[...]).astype(s_ref.dtype)
    vec_ref[0:1, :] += colsum(grad_first * normed)
    vec_ref[1:2, :] += colsum(grad_first)
    vecq_ref[0:1, :] += colsum(packed.astype(F32))
    qkv_acc[...] += tn(first, packed)
    out_acc[...] += tn(ctx, g_ref[...])
    if carry:

        @pl.when(i == pl.num_programs(0) - 1)
        def _():
            gqkv_ref[...] = qkv_acc[...].astype(BF)
            gout_ref[...] = out_acc[...].astype(BF)


def back(meta, x, g, ctx, gq, gk, gv, ffn, sf, qkv_w, out_w, ag, ash, carry=None):
    count, d = x.shape
    steps = count // ROWS
    cols = out_w.shape[0]
    here = lambda i, m: (i, 0)
    there = lambda i, m: (m[1] * steps + i, 0)
    part_type, grads_type = (BF, F32) if carry is None else (F32, BF)
    in_specs = [
        pl.BlockSpec((ROWS, d), here),
        *[pl.BlockSpec((ROWS, cols), there) for _ in range(4)],
        *[pl.BlockSpec((ROWS, d), here) for _ in range(3)],
        once(qkv_w.shape),
        once(out_w.shape),
        once(ag.shape),
        once(ash.shape),
    ]
    args = [meta, x, ctx, gq, gk, gv, g, ffn, sf, qkv_w, out_w, ag, ash]
    scratch = []
    if carry is not None:
        in_specs += [once((d, 3 * cols)), once((cols, d))]
        args += list(carry)
        scratch = [pltpu.VMEM((d, 3 * cols), F32), pltpu.VMEM((cols, d), F32)]
    return pl.pallas_call(
        functools.partial(back_kernel, carry is not None),
        grid_spec=pltpu.PrefetchScalarGridSpec(
            num_scalar_prefetch=1,
            grid=(steps,),
            in_specs=in_specs,
            out_specs=[
                pl.BlockSpec((ROWS, d), here),
                pl.BlockSpec((ROWS, d), here),
                once((d, 3 * cols)),
                once((cols, d)),
                once((8, d)),
                once((8, 3 * cols)),
            ],
            scratch_shapes=scratch,
        ),
        out_shape=[
            jax.ShapeDtypeStruct((count, d), part_type),
            jax.ShapeDtypeStruct((count, d), part_type),
            jax.ShapeDtypeStruct((d, 3 * cols), grads_type),
            jax.ShapeDtypeStruct((cols, d), grads_type),
            jax.ShapeDtypeStruct((8, d), F32),
            jax.ShapeDtypeStruct((8, 3 * cols), F32),
        ],
        compiler_params=params(),
        cost_estimate=pl.CostEstimate(
            flops=2 * count * d * 8 * cols, bytes_accessed=24 << 20, transcendentals=0
        ),
        name="back_own" if carry is not None else "back_other",
    )(*args)


def finish_kernel(meta, x_ref, g_ref, own_ref, came_ref, o_ref):
    normed, inverse = normalize(x_ref[...].astype(F32))
    s = own_ref[...] + came_ref[...].astype(F32)
    back_rows = inverse * (
        s
        - jnp.mean(s, axis=-1, keepdims=True)
        - normed * jnp.mean(s * normed, axis=-1, keepdims=True)
    )
    o_ref[...] = (g_ref[...].astype(F32) + back_rows).astype(BF)


def finish(meta, x, g, own, came):
    count, d = x.shape
    here = pl.BlockSpec((ROWS, d), lambda i, m: (i, 0))
    return pl.pallas_call(
        finish_kernel,
        grid_spec=pltpu.PrefetchScalarGridSpec(
            num_scalar_prefetch=1, grid=(count // ROWS,), in_specs=[here] * 4, out_specs=here
        ),
        out_shape=jax.ShapeDtypeStruct((count, d), BF),
        compiler_params=params(),
        cost_estimate=pl.CostEstimate(flops=20 * count * d, bytes_accessed=14 * count * d, transcendentals=0),
        name="finish",
    )(meta, x, g, own, came)


def regroup(w, heads):
    lead = w.shape[:-1]
    return jnp.swapaxes(w.reshape(*lead, heads, 3, HD), -3, -2).reshape(w.shape)


def ungroup(w, heads):
    lead = w.shape[:-1]
    return jnp.swapaxes(w.reshape(*lead, 3, heads, HD), -3, -2).reshape(w.shape)


def per_device(
    block_in,
    out_grad,
    seq_lens,
    qkv_weight,
    qkv_bias,
    out_weight,
    out_bias,
    up_weight,
    up_bias,
    down_weight,
    down_bias,
    attn_gain,
    attn_shift,
    ffn_gain,
    ffn_shift,
):
    swap = [(0, 1), (1, 0)]
    other_in = lax.ppermute(block_in, "narrow", swap)
    other_grad = lax.ppermute(out_grad, "narrow", swap)
    half = block_in.shape[0]
    group_rows = 2 * half
    heads = out_weight.shape[0] // HD
    own = lax.axis_index("narrow").astype(jnp.int32)
    long = (seq_lens[0, 0] == group_rows).astype(jnp.int32)
    row = lambda v: v.reshape(1, -1)
    order = jnp.arange(group_rows // BQ, dtype=jnp.int32)
    meta_own = jnp.concatenate([jnp.stack([long, own]), order])
    meta_other = jnp.concatenate([jnp.stack([long, 1 - own]), order])
    table = jnp.asarray(rope_table(group_rows))
    qkv_w = regroup(qkv_weight, heads)
    weights = (
        qkv_w,
        row(regroup(qkv_bias, heads)),
        up_weight,
        row(up_bias),
        down_weight,
        out_weight,
        row(attn_gain),
        row(attn_shift),
        row(ffn_gain),
        row(ffn_shift),
    )
    qkv, gc, ffn_own, sf_own, gup, gdown, vec1, vech1 = front(
        meta_own, block_in, out_grad, weights, table, group_rows
    )
    qkv, gc, ffn_other, sf_other, gup, gdown, vec2, vech2 = front(
        meta_other, other_in, other_grad, weights, table, group_rows, (qkv, gc, gup, gdown)
    )
    gup, gdown = lax.psum((gup, gdown), "wide")
    ctx, gq, gk, gv = attention(meta_own, qkv, gc, table)
    ag, ash = row(attn_gain), row(attn_shift)
    send_part, send_s, gqkv, gout, vec3, vecq3 = back(
        meta_other, other_in, other_grad, ctx, gq, gk, gv, ffn_other, sf_other, qkv_w, out_weight, ag, ash
    )
    came_part = lax.ppermute(send_part, "narrow", swap)
    came_s = lax.ppermute(send_s, "narrow", swap)
    own_part, own_s, gqkv, gout, vec4, vecq4 = back(
        meta_own, block_in, out_grad, ctx, gq, gk, gv, ffn_own, sf_own, qkv_w, out_weight, ag, ash, (gqkv, gout)
    )
    gqkv, gout = lax.psum((gqkv, gout), "wide")
    block_out = (
        block_in.astype(F32)
        + own_part
        + came_part.astype(F32)
        + (out_bias.astype(F32) + down_bias.astype(F32))
    ).astype(BF)
    in_grad = finish(meta_own, block_in, out_grad, own_s, came_s)
    vec = jnp.concatenate([(vec1 + vec2)[:2], (vec3 + vec4)[:2], vec1[2:3]], 0)
    vec = lax.psum(vec, ("wide", "narrow"))
    gup_b, gqkv_b = lax.psum((vech1[0] + vech2[0], vecq3[0] + vecq4[0]), "wide")
    return (
        block_out,
        in_grad,
        ungroup(gqkv, heads).astype(F32),
        ungroup(gqkv_b, heads),
        gout.astype(F32),
        vec[4],
        gup.astype(F32),
        gup_b,
        gdown.astype(F32),
        vec[4],
        vec[2],
        vec[3],
        vec[0],
        vec[1],
    )


def solution(mesh):
    rows = P(("wide", "narrow"), None)
    placed = (
        rows,
        rows,
        P("wide", None),
        P(None, "narrow"),
        P("narrow"),
        P("narrow", None),
        P(),
        P(None, "narrow"),
        P("narrow"),
        P("narrow", None),
        P(),
        P(),
        P(),
        P(),
        P(),
    )
    return jax.shard_map(
        per_device,
        mesh=mesh,
        in_specs=placed,
        out_specs=(
            rows,
            rows,
            P(None, "narrow"),
            P("narrow"),
            P("narrow", None),
            P(),
            P(None, "narrow"),
            P("narrow"),
            P("narrow", None),
            P(),
            P(),
            P(),
            P(),
            P(),
        ),
        check_vma=False,
    )
```

```python
import functools

import jax
import jax.numpy as jnp
import numpy as np
from jax import lax
from jax.experimental import pallas as pl
from jax.experimental.pallas import tpu as pltpu
from jax.sharding import PartitionSpec as P

HD = 64
ROT = 16
EPS = 1e-05
NEG = -1e30
SCALE = 0.125
SHORT_LEN = 512
F32 = jnp.float32
BF = jnp.bfloat16
LANES = 128
BQ = 512
BS = 256
ROWS = 256
VMEM_LIMIT = 58 << 20
COST = pl.CostEstimate(flops=1 << 20, bytes_accessed=1 << 12, transcendentals=0)


def nn(a, b):
    return lax.dot_general(a, b, (((1,), (0,)), ((), ())), preferred_element_type=F32)


def nt(a, b):
    return lax.dot_general(a, b, (((1,), (1,)), ((), ())), preferred_element_type=F32)


def tn(a, b):
    return lax.dot_general(a, b, (((0,), (0,)), ((), ())), preferred_element_type=F32)


def colsum(a):
    return jnp.sum(a, axis=0, keepdims=True)


def rope_table(rows):
    half = ROT // 2
    freq = np.float32(1.0) / np.float32(10000.0) ** (
        np.arange(half, dtype=np.float32) * np.float32(2.0) / np.float32(ROT)
    )
    angle = np.arange(rows, dtype=np.float32)[:, None] * freq.astype(np.float32)[None, :]
    table = np.zeros((rows, 2 * HD), np.float32)
    table[:, :HD] = 1.0
    table[:, :half] = table[:, half:ROT] = np.cos(angle)
    table[:, HD : HD + half] = -np.sin(angle)
    table[:, HD + half : HD + ROT] = np.sin(angle)
    return table


def rope(x, table, back):
    lane = lax.broadcasted_iota(jnp.int32, x.shape, 1)
    other = pltpu.roll(table, HD, 1)
    cosine = jnp.where(lane < HD, table, other)
    sine = jnp.where(lane < HD, other, table)
    partner = jnp.where(
        lane % HD < ROT // 2, pltpu.roll(x, LANES - ROT // 2, 1), pltpu.roll(x, ROT // 2, 1)
    )
    return x * cosine - partner * sine if back else x * cosine + partner * sine


def normalize(x):
    center = jnp.mean(x, axis=-1, keepdims=True)
    offset = x - center
    inverse = lax.rsqrt(jnp.mean(offset * offset, axis=-1, keepdims=True) + EPS)
    return offset * inverse, inverse


def once(shape):
    return pl.BlockSpec(shape, lambda i, m: (0,) * len(shape), pipeline_mode=pl.Buffered(1))


def params(**more):
    return pltpu.CompilerParams(
        vmem_limit_bytes=VMEM_LIMIT, dimension_semantics=("arbitrary",), **more
    )


EXTRA = 16


def front_kernel(carry, meta, *refs):
    (x_ref, g_ref, qkv_w, qkv_b, up_w, up_b, down_w, out_w, ag, ash, fg, fsh, tab_ref), refs = (
        refs[:13],
        refs[13:],
    )
    if carry:
        (_, _, up_in, down_in, vec_in, vech_in), refs = refs[:6], refs[6:]
    (qkv_ref, gc_ref, ffn_ref, s_ref), refs = refs[:4], refs[4:]
    if carry:
        (packed_ref, up_acc, down_acc, vec_ref, vech_ref) = refs
    else:
        (up_acc, down_acc, vec_ref, vech_ref) = refs
    i = pl.program_id(0)
    rows = x_ref.shape[0]
    x = x_ref[...].astype(F32)
    g = g_ref[...]
    normed, _ = normalize(x)
    first = (normed * ag[...].astype(F32) + ash[...].astype(F32)).astype(BF)
    second = (normed * fg[...].astype(F32) + fsh[...].astype(F32)).astype(BF)

    @pl.when(i == 0)
    def _():
        if carry:
            up_acc[...] = up_in[...]
            down_acc[...] = down_in[...]
            vec_ref[...] = vec_in[...]
            vech_ref[...] = vech_in[...]
        else:
            up_acc[...] = jnp.zeros_like(up_acc)
            down_acc[...] = jnp.zeros_like(down_acc)
            vec_ref[...] = jnp.zeros_like(vec_ref)
            vech_ref[...] = jnp.zeros_like(vech_ref)

    packed = nn(first, qkv_w[...]) + qkv_b[...].astype(F32)
    third = packed.shape[1] // 3
    table = tab_ref[...]
    for c in range(0, third, LANES):
        q = rope(packed[:, c : c + LANES], table, False).astype(BF)
        qkv_ref[:, c : c + LANES] = (q.astype(F32) * SCALE).astype(BF)
        qkv_ref[:, third + c : third + c + LANES] = rope(
            packed[:, third + c : third + c + LANES], table, False
        ).astype(BF)
    qkv_ref[:, 2 * third :] = packed[:, 2 * third :].astype(BF)
    gc_ref[...] = nt(g, out_w[...]).astype(BF)

    hidden = nn(second, up_w[...]) + up_b[...].astype(F32)
    phi = 0.5 * (1.0 + lax.erf(hidden * np.float32(0.5**0.5)))
    density = jnp.exp(-0.5 * hidden * hidden) * np.float32(1.0 / np.sqrt(2.0 * np.pi))
    act = (hidden * phi).astype(BF)
    ffn_ref[...] = nn(act, down_w[...])
    gh_full = nt(g, down_w[...]) * (phi + hidden * density)
    gh = gh_full.astype(BF)
    gs = nt(gh, up_w[...])
    s_ref[...] = gs * fg[...].astype(F32)
    vec_ref[0:1, :] += colsum(gs * normed)
    vec_ref[1:2, :] += colsum(gs)
    if not carry:
        vec_ref[2:3, :] += colsum(g.astype(F32))
    vech_ref[0:1, :] += colsum(gh.astype(F32))
    up_acc[...] += tn(second, gh)
    down_acc[...] += tn(act, g)
    if carry:

        @pl.when(i == pl.num_programs(0) - 1)
        def _():
            d = up_acc.shape[0]
            hidden_rows = down_acc.shape[0]
            spare = [vec_ref[...]]
            for c in range(0, hidden_rows, d):
                packed_ref[c : c + d, :] = up_acc[:, c : c + d].astype(BF)
                spare.append(vech_ref[0:1, c : c + d])
            packed_ref[hidden_rows : 2 * hidden_rows, :] = down_acc[...].astype(BF)
            pad = EXTRA - vec_ref.shape[0] - (len(spare) - 1)
            spare.append(jnp.zeros((pad, d), F32))
            packed_ref[2 * hidden_rows :, :] = jnp.concatenate(spare, 0).astype(BF)


def front(meta, x, g, weights, table, group_rows, carry=None):
    qkv_w, qkv_b, up_w, up_b, down_w, out_w, ag, ash, fg, fsh = weights
    count, d = x.shape
    steps = count // ROWS
    heads_cols = out_w.shape[0]
    hidden = up_w.shape[1]
    per_short = SHORT_LEN // ROWS
    here = lambda i, m: (i, 0)
    there = lambda i, m: (m[1] * steps + i, 0)
    tab = lambda i, m: (
        jnp.where(m[0] == 1, m[1] * steps + i, lax.rem(m[1] * steps + i, per_short)),
        0,
    )
    in_specs = [
        pl.BlockSpec((ROWS, d), here),
        pl.BlockSpec((ROWS, d), here),
        *[once(w.shape) for w in weights],
        pl.BlockSpec((ROWS, 2 * HD), tab),
    ]
    out_specs = [
        pl.BlockSpec((ROWS, 3 * heads_cols), there),
        pl.BlockSpec((ROWS, heads_cols), there),
        pl.BlockSpec((ROWS, d), here),
        pl.BlockSpec((ROWS, d), here),
    ]
    out_shape = [
        jax.ShapeDtypeStruct((group_rows, 3 * heads_cols), BF),
        jax.ShapeDtypeStruct((group_rows, heads_cols), BF),
        jax.ShapeDtypeStruct((count, d), F32),
        jax.ShapeDtypeStruct((count, d), F32),
    ]
    sums = [(d, hidden), (hidden, d), (8, d), (8, hidden)]
    args = [meta, x, g, *weights, table]
    scratch, aliases = [], {}
    if carry is not None:
        in_specs += [pl.BlockSpec(memory_space=pl.ANY)] * 2 + [once(shape) for shape in sums]
        aliases = {len(args): 0, len(args) + 1: 1}
        args += list(carry)
        out_specs += [once((2 * hidden + EXTRA, d))]
        out_shape += [jax.ShapeDtypeStruct((2 * hidden + EXTRA, d), BF)]
        scratch = [pltpu.VMEM(shape, F32) for shape in sums]
    else:
        out_specs += [once(shape) for shape in sums]
        out_shape += [jax.ShapeDtypeStruct(shape, F32) for shape in sums]
    flops = 2 * count * d * (6 * hidden + 3 * heads_cols + heads_cols)
    return pl.pallas_call(
        functools.partial(front_kernel, carry is not None),
        grid_spec=pltpu.PrefetchScalarGridSpec(
            num_scalar_prefetch=1,
            grid=(steps,),
            in_specs=in_specs,
            out_specs=out_specs,
            scratch_shapes=scratch,
        ),
        out_shape=out_shape,
        input_output_aliases=aliases,
        compiler_params=params(),
        cost_estimate=pl.CostEstimate(
            flops=flops, bytes_accessed=40 << 20, transcendentals=2 * count * hidden
        ),
        name="front_second" if carry is not None else "front_first",
    )(*args)


def unpack_front(packed, d, hidden):
    assert hidden == 2 * d
    steps = 6
    part = d // steps
    chunk = hidden // steps

    def kernel(p0, p1, p2, e_ref, up_ref, down_ref, vec_ref):
        up_ref[:, :d] = p0[...].astype(F32)
        up_ref[:, d:] = p1[...].astype(F32)
        down_ref[...] = p2[...].astype(F32)
        vec_ref[...] = e_ref[...].astype(F32)

    return pl.pallas_call(
        kernel,
        grid=(steps,),
        in_specs=[
            pl.BlockSpec((part, d), lambda i: (i, 0)),
            pl.BlockSpec((part, d), lambda i: (steps + i, 0)),
            pl.BlockSpec((chunk, d), lambda i: (steps + i, 0)),
            pl.BlockSpec((EXTRA, d), lambda i: (2 * hidden // EXTRA, 0)),
        ],
        out_specs=[
            pl.BlockSpec((part, hidden), lambda i: (i, 0)),
            pl.BlockSpec((chunk, d), lambda i: (i, 0)),
            pl.BlockSpec((EXTRA, d), lambda i: (0, 0)),
        ],
        out_shape=[
            jax.ShapeDtypeStruct((d, hidden), F32),
            jax.ShapeDtypeStruct((hidden, d), F32),
            jax.ShapeDtypeStruct((EXTRA, d), F32),
        ],
        compiler_params=params(),
        cost_estimate=pl.CostEstimate(
            flops=2 * d * hidden, bytes_accessed=12 * d * hidden, transcendentals=0
        ),
        name="unpack_front",
    )(packed, packed, packed, packed)


def attention_kernel(meta, q_ref, k_ref, v_ref, do_ref, tab_ref, *refs):
    ctx_ref, dq_ref, dk_ref, dv_ref, s_sc, e_sc, ds_sc, kt_sc, vt_sc, dk_sc, dv_sc = refs
    i = pl.program_id(1)
    qb = meta[3 + i]
    long = meta[0]
    rows = k_ref.shape[0]
    wide_cols, half_cols = 2 * BQ, 2 * BS
    ext = HD + 16

    @pl.when(i == 0)
    def _():
        dk_sc[...] = jnp.zeros_like(dk_sc)
        dv_sc[...] = jnp.zeros_like(dv_sc)
        kt_sc[...] = k_ref[...].T
        ones = jnp.ones((16, rows), BF)
        vt = v_ref[...].T
        for h in range(2):
            vt_sc[h * ext : h * ext + HD, :] = vt[h * HD : (h + 1) * HD]
            vt_sc[h * ext + HD : (h + 1) * ext, :] = ones

    def process(base, tiles):
        def keys(start, count):
            row = base + start * BS
            return pl.ds(row if isinstance(row, int) else pl.multiple_of(row, BS), count * BS)

        zeros_t = jnp.zeros((HD, BS), BF)
        zeros = jnp.zeros((BS, LANES), BF)
        lane = lax.broadcasted_iota(jnp.int32, (BS, LANES), 1)

        def wide(t):
            return jnp.concatenate(
                [
                    jnp.concatenate(pair, 0)
                    for a in range(0, BQ, BS)
                    for pair in ([t[:HD, a : a + BS], zeros_t], [zeros_t, t[HD:, a : a + BS]])
                ],
                1,
            )

        def tall(t):
            return jnp.concatenate(
                [
                    block
                    for a in range(0, BQ, BS)
                    for block in (
                        jnp.where(lane < HD, t[a : a + BS], zeros),
                        jnp.where(lane < HD, zeros, t[a : a + BS]),
                    )
                ],
                0,
            )

        queries = q_ref[...]
        q_wide, q_tall = wide(queries.T), tall(queries)
        key_index = lax.broadcasted_iota(jnp.int32, (BS, half_cols), 0)
        query_index = lax.broadcasted_iota(jnp.int32, (BS, half_cols), 1) % BS
        causal = key_index <= query_index
        first_col = lambda t: half_cols if t == tiles - 1 else 0
        top = jnp.full((8, wide_cols), NEG, F32)
        for t in range(tiles):
            lo = first_col(t)
            s = nn(k_ref[keys(t, 1), :], q_wide[:, lo:])
            if t == tiles - 1:
                s = jnp.where(causal, s, NEG)
            if t == tiles - 2:
                s = jnp.concatenate(
                    [jnp.where(causal, s[:, :half_cols], NEG), s[:, half_cols:]], 1
                )
            s_sc[t * BS : (t + 1) * BS, lo:] = s
            part = jnp.max(s.reshape(BS // 8, 8, wide_cols - lo), axis=0)
            if lo:
                top = jnp.concatenate([top[:, :lo], jnp.maximum(top[:, lo:], part)], 1)
            else:
                top = jnp.maximum(top, part)
        top = jnp.max(top, axis=0, keepdims=True)
        for t in range(tiles):
            lo = first_col(t)
            block = slice(t * BS, (t + 1) * BS)
            e_sc[block, lo:] = jnp.exp(s_sc[block, lo:] - top[:, lo:]).astype(BF)
        grad_t = do_ref[...].astype(F32).T
        ctx_parts, grad_parts, weighted = [[], []], [[], []], []
        for a in range(2):
            count = tiles - 1 + a
            for h in range(2):
                c = a * half_cols + h * BS
                r = nn(vt_sc[h * ext : (h + 1) * ext, keys(0, count)], e_sc[: count * BS, c : c + BS])
                over_total = 1.0 / r[HD : HD + 1]
                ctx = r[:HD] * over_total
                grad = (grad_t[h * HD : (h + 1) * HD, a * BS : (a + 1) * BS] * over_total).astype(BF)
                weighted.append(colsum(ctx * grad.astype(F32)))
                ctx_parts[a].append(ctx)
                grad_parts[a].append(grad)
        full = lambda parts: jnp.concatenate([jnp.concatenate(part, 0) for part in parts], 1)
        ctx_ref[...] = full(ctx_parts).T.astype(BF)
        grad_full = full(grad_parts)
        g_wide, g_tall = wide(grad_full), tall(grad_full.T)
        weighted = jnp.concatenate(weighted, 1)
        for t in range(tiles):
            lo = first_col(t)
            block = slice(t * BS, (t + 1) * BS)
            e = e_sc[block, lo:]
            gp = nn(v_ref[keys(t, 1), :], g_wide[:, lo:])
            ds = (e.astype(F32) * (gp - weighted[:, lo:])).astype(BF)
            ds_sc[block, lo:] = ds
            dv_sc[keys(t, 1), :] += nn(e, g_tall[lo:])
            dk_sc[keys(t, 1), :] += nn(ds, q_tall[lo:])
        dq_parts = [[], []]
        for a in range(2):
            count = tiles - 1 + a
            for h in range(2):
                c = a * half_cols + h * BS
                dq_parts[a].append(
                    nn(kt_sc[h * HD : (h + 1) * HD, keys(0, count)], ds_sc[: count * BS, c : c + BS])
                )
        at = pl.multiple_of(jnp.where(long == 1, qb, 0) * BQ, BQ)
        dq_ref[...] = rope(full(dq_parts).T * SCALE, tab_ref[pl.ds(at, BQ), :], True).astype(BF)

    for c in range(rows // BQ):

        @pl.when((long == 1) & (qb == c))
        def _(c=c):
            process(0, (c + 1) * (BQ // BS))

    @pl.when(long == 0)
    def _():
        process(qb * BQ, BQ // BS)

    @pl.when(i == pl.num_programs(1) - 1)
    def _():
        dv_ref[...] = dv_sc[...].astype(BF)

        def finish(b, _):
            block = pl.ds(pl.multiple_of(b * BQ, BQ), BQ)
            at = pl.multiple_of(jnp.where(long == 1, b, 0) * BQ, BQ)
            dk_ref[block, :] = rope(dk_sc[block, :], tab_ref[pl.ds(at, BQ), :], True).astype(BF)
            return 0

        lax.fori_loop(0, rows // BQ, finish, 0)


def attention(meta, qkv, grad_ctx, table):
    rows, cols = grad_ctx.shape
    pairs, blocks = cols // LANES, rows // BQ
    at_query = lambda p, i, m: (m[3 + i], p)
    whole = lambda part: lambda p, i, m: (0, part * pairs + p)
    kept = jax.ShapeDtypeStruct((rows, cols), BF)
    return pl.pallas_call(
        attention_kernel,
        grid_spec=pltpu.PrefetchScalarGridSpec(
            num_scalar_prefetch=1,
            grid=(pairs, blocks),
            in_specs=[
                pl.BlockSpec((BQ, LANES), at_query),
                pl.BlockSpec((rows, LANES), whole(1)),
                pl.BlockSpec((rows, LANES), whole(2)),
                pl.BlockSpec((BQ, LANES), at_query),
                pl.BlockSpec((rows, LANES), lambda p, i, m: (0, 0), pipeline_mode=pl.Buffered(1)),
            ],
            out_specs=[
                pl.BlockSpec((BQ, LANES), at_query),
                pl.BlockSpec((BQ, LANES), at_query),
                pl.BlockSpec((rows, LANES), whole(0)),
                pl.BlockSpec((rows, LANES), whole(0)),
            ],
            scratch_shapes=[
                pltpu.VMEM((rows, 2 * BQ), F32),
                pltpu.VMEM((rows, 2 * BQ), BF),
                pltpu.VMEM((rows, 2 * BQ), BF),
                pltpu.VMEM((LANES, rows), BF),
                pltpu.VMEM((2 * (HD + 16), rows), BF),
                pltpu.VMEM((rows, LANES), F32),
                pltpu.VMEM((rows, LANES), F32),
            ],
        ),
        out_shape=[kept] * 4,
        compiler_params=pltpu.CompilerParams(
            vmem_limit_bytes=VMEM_LIMIT, dimension_semantics=("arbitrary", "arbitrary")
        ),
        cost_estimate=COST,
        name="attention",
    )(meta, qkv, qkv, qkv, grad_ctx, table)


def back_rows_kernel(meta, ctx_ref, gq_ref, gk_ref, gv_ref, ffn_ref, sf_ref, qkv_w, out_w, ag, part_ref, s_ref):
    part_ref[...] = (nn(ctx_ref[...], out_w[...]) + ffn_ref[...]).astype(part_ref.dtype)
    packed = jnp.concatenate([gq_ref[...], gk_ref[...], gv_ref[...]], axis=1)
    s_ref[...] = (nt(packed, qkv_w[...]) * ag[...].astype(F32) + sf_ref[...]).astype(s_ref.dtype)


def back_rows(meta, ctx, gq, gk, gv, ffn, sf, qkv_w, out_w, ag, kind):
    count, d = ffn.shape
    steps = count // ROWS
    cols = out_w.shape[0]
    here = pl.BlockSpec((ROWS, d), lambda i, m: (i, 0))
    there = pl.BlockSpec((ROWS, cols), lambda i, m: (m[1] * steps + i, 0))
    return pl.pallas_call(
        back_rows_kernel,
        grid_spec=pltpu.PrefetchScalarGridSpec(
            num_scalar_prefetch=1,
            grid=(steps,),
            in_specs=[there] * 4 + [here] * 2 + [once(qkv_w.shape), once(out_w.shape), once(ag.shape)],
            out_specs=[here, here],
        ),
        out_shape=[jax.ShapeDtypeStruct((count, d), kind)] * 2,
        compiler_params=params(),
        cost_estimate=COST,
        name="back_rows",
    )(meta, ctx, gq, gk, gv, ffn, sf, qkv_w, out_w, ag)


def bit_of(me, bit):
    return lax.rem(lax.div(me, bit), 2)


def back_weights_kernel(meta, *refs):
    (x0_ref, x1_ref, g0_ref, g1_ref, ctx_ref, gq_ref, gk_ref, gv_ref, ag, ash), refs = refs[:10], refs[10:]
    away_ref, kept_ref, qkv_acc, out_acc, bias_acc, all_sc = refs
    i = pl.program_id(0)
    steps = pl.num_programs(0)

    @pl.when(i == 0)
    def _():
        qkv_acc[...] = jnp.zeros_like(qkv_acc)
        out_acc[...] = jnp.zeros_like(out_acc)
        bias_acc[...] = jnp.zeros_like(bias_acc)

    own = i < steps // 2
    x = jnp.where(own, x0_ref[...].astype(F32), x1_ref[...].astype(F32))
    g = jnp.where(own, g0_ref[...], g1_ref[...])
    normed, _ = normalize(x)
    first = (normed * ag[...].astype(F32) + ash[...].astype(F32)).astype(BF)
    packed = jnp.concatenate([gq_ref[...], gk_ref[...], gv_ref[...]], axis=1)
    bias_acc[0:1, :] += colsum(packed.astype(F32))
    qkv_acc[...] += tn(first, packed)
    out_acc[...] += tn(ctx_ref[...], g)

    @pl.when(i == steps - 1)
    def _():
        d, width = qkv_acc.shape
        third = width // 3
        all_sc[:d, :width] = qkv_acc[...]
        all_sc[d:, :d] = out_acc[: 2 * third // 3, :]
        all_sc[d : d + third // 3, d:width] = out_acc[2 * third // 3 :, :third]
        all_sc[d + third // 3 :, d:width] = out_acc[2 * third // 3 :, third:]
        all_sc[:, width:] = jnp.zeros((all_sc.shape[0], LANES), F32)
        for c in range(0, width, LANES):
            all_sc[c // LANES : c // LANES + 1, width:] = bias_acc[0:1, c : c + LANES]
        quarter = all_sc.shape[0] // 4
        core = bit_of(meta[2], 1)
        for k in range(2):
            here = pl.multiple_of((2 * k + core) * quarter, quarter)
            there = pl.multiple_of((2 * k + 1 - core) * quarter, quarter)
            rows = slice(k * quarter, (k + 1) * quarter)
            kept_ref[rows, :] = all_sc[pl.ds(here, quarter), :]
            away_ref[rows, :] = all_sc[pl.ds(there, quarter), :].astype(BF)


def back_weights(meta, x_own, x_other, g_own, g_other, ctx, gq, gk, gv, ag, ash):
    half, d = x_own.shape
    steps = half // ROWS
    cols = ctx.shape[1]
    assert d == 2 * cols and cols % 3 == 0
    first = pl.BlockSpec((ROWS, d), lambda i, m: (jnp.minimum(i, steps - 1), 0))
    last = pl.BlockSpec((ROWS, d), lambda i, m: (jnp.maximum(i - steps, 0), 0))
    there = pl.BlockSpec(
        (ROWS, cols), lambda i, m: (lax.rem(m[1] * steps + i, 2 * steps), 0)
    )
    rows, width = d + 2 * cols // 3, 3 * cols + LANES
    return pl.pallas_call(
        back_weights_kernel,
        grid_spec=pltpu.PrefetchScalarGridSpec(
            num_scalar_prefetch=1,
            grid=(2 * steps,),
            in_specs=[first, last, first, last] + [there] * 4 + [once(ag.shape), once(ash.shape)],
            out_specs=[once((rows // 2, width))] * 2,
            scratch_shapes=[
                pltpu.VMEM((d, 3 * cols), F32),
                pltpu.VMEM((cols, d), F32),
                pltpu.VMEM((8, 3 * cols), F32),
                pltpu.VMEM((rows, width), F32),
            ],
        ),
        out_shape=[
            jax.ShapeDtypeStruct((rows // 2, width), BF),
            jax.ShapeDtypeStruct((rows // 2, width), F32),
        ],
        compiler_params=params(),
        cost_estimate=COST,
        name="back_weights",
    )(meta, x_own, x_other, g_own, g_other, ctx, gq, gk, gv, ag, ash)


def fold_kernel(bits, meta, *refs):
    ins, outs = refs[:4], refs[4:]
    for k, bit in enumerate(bits):
        kept, came = ins[2 * k], ins[2 * k + 1]
        if bit is None:
            outs[k][...] = (kept[...] + came[...].astype(F32)).astype(BF)
            continue
        away_ref, kept_ref = outs[2 * k], outs[2 * k + 1]
        half = kept_ref.shape[0]
        mine = bit_of(meta[2], bit)
        here = pl.ds(pl.multiple_of(mine * half, half), half)
        there = pl.ds(pl.multiple_of((1 - mine) * half, half), half)
        kept_ref[...] = kept[here, :] + came[here, :].astype(F32)
        away_ref[...] = (kept[there, :] + came[there, :].astype(F32)).astype(BF)


def spread_kernel(bits, join, meta, *refs):
    ins, outs = refs[:4], refs[4:]
    rows = ins[0].shape[0]
    for k, bit in enumerate(bits):
        out_ref, base = (outs[0], k * 2 * rows) if join else (outs[k], 0)
        mine = bit_of(meta[2], bit)
        out_ref[pl.ds(pl.multiple_of(base + mine * rows, rows), rows), :] = ins[2 * k][...]
        out_ref[pl.ds(pl.multiple_of(base + (1 - mine) * rows, rows), rows), :] = ins[2 * k + 1][...]


def small_call(kernel, meta, ins, in_specs, outs, name):
    whole = lambda shape: pl.BlockSpec(shape, lambda i, m: (0,) * len(shape))
    size = sum(int(np.prod(o[0])) for o in outs)
    return pl.pallas_call(
        kernel,
        grid_spec=pltpu.PrefetchScalarGridSpec(
            num_scalar_prefetch=1,
            grid=(1,),
            in_specs=[whole(a.shape) if s is None else s for a, s in zip(ins, in_specs)],
            out_specs=[whole(o[0]) for o in outs],
        ),
        out_shape=[jax.ShapeDtypeStruct(*o) for o in outs],
        compiler_params=params(),
        cost_estimate=pl.CostEstimate(flops=size, bytes_accessed=8 * size, transcendentals=0),
        name=name,
    )(meta, *ins)


def late_sum(meta, away, kept, orders, gates):
    gates = list(gates)

    def gated(step, values):
        if step < len(gates) and gates[step] is not None:
            values, gates[step] = lax.optimization_barrier((values, gates[step]))
        return values

    rows, width = kept.shape[0] // 2, kept.shape[1]
    came = swap_wide(away, 1)
    order_a, order_b = orders
    count = lax.axis_size("wide")
    if rows // (count // 2) < 16:
        parts = []
        for k, order in enumerate(orders):
            value = kept[k * rows : (k + 1) * rows] + came[k * rows : (k + 1) * rows].astype(F32)
            parts.append(gather_shares(scatter_sum(value, order[1:]), order[1:]))
        mine = jnp.concatenate(parts, 0)
        return mine, swap_wide(mine, 1), gates
    part = lambda k: pl.BlockSpec((rows, width), lambda i, m: (k, 0))
    ins, specs = [kept, came, kept, came], [part(0), part(0), part(1), part(1)]
    steps = len(order_a)
    for step in range(1, steps):
        rows //= 2
        shapes = [((rows, width), BF), ((rows, width), F32)] * 2
        bits = (order_a[step], order_b[step])
        away_a, kept_a, away_b, kept_b = small_call(
            functools.partial(fold_kernel, bits), meta, ins, specs, shapes, "fold"
        )
        ins = [kept_a, swap_wide(away_a, bits[0]), kept_b, swap_wide(away_b, bits[1])]
        specs = [None] * 4
        ins = gated(step, ins)
    share_a, share_b = small_call(
        functools.partial(fold_kernel, (None, None)), meta, ins, specs, [((rows, width), BF)] * 2, "fold"
    )
    for step in range(steps - 1, 0, -1):
        bits = (order_a[step], order_b[step])
        ins = [share_a, swap_wide(share_a, bits[0]), share_b, swap_wide(share_b, bits[1])]
        ins = gated(2 * steps - 1 - step, ins)
        last = step == 1
        shapes = [((4 * rows, width), BF)] if last else [((2 * rows, width), BF)] * 2
        got = small_call(functools.partial(spread_kernel, bits, last), meta, ins, specs, shapes, "spread")
        rows *= 2
        if not last:
            share_a, share_b = got
    return got[0], swap_wide(got[0], 1), gates


def unpack_late_kernel(meta, mine_ref, peer_ref, w_ref, ag, ash, gqkv_ref, gout_ref, bias_ref, vec_ref, all_sc):
    d, width = gqkv_ref.shape
    third = width // 3
    quarter = mine_ref.shape[0] // 2
    core = bit_of(meta[2], 1)
    for k in range(2):
        rows = slice(k * quarter, (k + 1) * quarter)
        here = pl.multiple_of((2 * k + core) * quarter, quarter)
        there = pl.multiple_of((2 * k + 1 - core) * quarter, quarter)
        all_sc[pl.ds(here, quarter), :] = mine_ref[rows, :].astype(F32)
        all_sc[pl.ds(there, quarter), :] = peer_ref[rows, :].astype(F32)
    gout_ref[: 2 * third // 3, :] = all_sc[d:, :d]
    gout_ref[2 * third // 3 :, :third] = all_sc[d : d + third // 3, d:width]
    gout_ref[2 * third // 3 :, third:] = all_sc[d + third // 3 :, d:width]
    lane = lax.broadcasted_iota(jnp.int32, (1, LANES), 1)

    def pick(read, block, to):
        start = block % 3 * third + block // 3 * HD
        tile = read(start // LANES * LANES)
        return tile if start % LANES == to * HD else pltpu.roll(tile, HD, 1)

    bias = jnp.concatenate([all_sc[c : c + 1, width:] for c in range(width // LANES)], 1)
    bias8 = jnp.broadcast_to(bias, (8, width))
    for t in range(width // LANES):
        to = slice(t * LANES, (t + 1) * LANES)
        read = lambda c: all_sc[:d, c : c + LANES]
        gqkv_ref[:, to] = jnp.where(lane < HD, pick(read, 2 * t, 0), pick(read, 2 * t + 1, 1))
        read = lambda c: bias8[:, c : c + LANES]
        bias_ref[:, to] = jnp.where(lane < HD, pick(read, 2 * t, 0), pick(read, 2 * t + 1, 1))
    left = jnp.zeros((d, LANES), F32)
    right = jnp.zeros((d, LANES), F32)
    for c in range(0, width, LANES):
        w = w_ref[:, c : c + LANES].astype(F32)
        left += w * all_sc[:d, c : c + LANES]
        right += w * bias[:, c : c + LANES]
    shift_sum = colsum(right.T)
    vec_ref[0:1, :] = (colsum(left.T) - ash[...].astype(F32) * shift_sum) / ag[...].astype(F32)
    vec_ref[1:2, :] = shift_sum
    vec_ref[2:, :] = jnp.zeros((vec_ref.shape[0] - 2, d), F32)


def unpack_late(meta, mine, peer, qkv_w, ag, ash):
    d, width = qkv_w.shape
    cols = width // 3
    whole = lambda shape: pl.BlockSpec(shape, lambda i, m: (0, 0))
    ins = [mine, peer, qkv_w, ag, ash]
    outs = [(d, width), (cols, d), (8, width), (8, d)]
    return pl.pallas_call(
        unpack_late_kernel,
        grid_spec=pltpu.PrefetchScalarGridSpec(
            num_scalar_prefetch=1,
            grid=(1,),
            in_specs=[whole(a.shape) for a in ins],
            out_specs=[whole(o) for o in outs],
            scratch_shapes=[pltpu.VMEM((2 * mine.shape[0], mine.shape[1]), F32)],
        ),
        out_shape=[jax.ShapeDtypeStruct(o, F32) for o in outs],
        compiler_params=params(),
        cost_estimate=pl.CostEstimate(flops=4 * d * width, bytes_accessed=8 * d * width, transcendentals=0),
        name="unpack_late",
    )(meta, *ins)


def finish_kernel(meta, x_ref, g_ref, own_ref, came_ref, o_ref):
    normed, inverse = normalize(x_ref[...].astype(F32))
    s = own_ref[...] + came_ref[...].astype(F32)
    back_rows = inverse * (
        s
        - jnp.mean(s, axis=-1, keepdims=True)
        - normed * jnp.mean(s * normed, axis=-1, keepdims=True)
    )
    o_ref[...] = (g_ref[...].astype(F32) + back_rows).astype(BF)


def finish(meta, x, g, own, came):
    count, d = x.shape
    here = pl.BlockSpec((ROWS, d), lambda i, m: (i, 0))
    return pl.pallas_call(
        finish_kernel,
        grid_spec=pltpu.PrefetchScalarGridSpec(
            num_scalar_prefetch=1, grid=(count // ROWS,), in_specs=[here] * 4, out_specs=here
        ),
        out_shape=jax.ShapeDtypeStruct((count, d), BF),
        compiler_params=params(),
        cost_estimate=pl.CostEstimate(flops=20 * count * d, bytes_accessed=14 * count * d, transcendentals=0),
        name="finish",
    )(meta, x, g, own, came)


def finish_out_kernel(x_ref, own_ref, came_ref, out_bias, down_bias, o_ref):
    bias = out_bias[...].astype(F32) + down_bias[...].astype(F32)
    o_ref[...] = (x_ref[...].astype(F32) + own_ref[...] + came_ref[...].astype(F32) + bias).astype(BF)


def finish_out(x, own, came, out_bias, down_bias):
    count, d = x.shape
    here = pl.BlockSpec((ROWS, d), lambda i: (i, 0))
    bias = pl.BlockSpec((1, d), lambda i: (0, 0))
    return pl.pallas_call(
        finish_out_kernel,
        grid=(count // ROWS,),
        in_specs=[here] * 3 + [bias] * 2,
        out_specs=here,
        out_shape=jax.ShapeDtypeStruct((count, d), BF),
        compiler_params=params(),
        cost_estimate=pl.CostEstimate(flops=4 * count * d, bytes_accessed=10 * count * d, transcendentals=0),
        name="finish_out",
    )(x, own, came, out_bias, down_bias)


def regroup(w, heads):
    lead = w.shape[:-1]
    return jnp.swapaxes(w.reshape(*lead, heads, 3, HD), -3, -2).reshape(w.shape)


def wide_orders(count):
    bits = [1 << k for k in range(count.bit_length() - 1)]
    return bits, bits[:1] + bits[2:] + bits[1:2]


def swap_wide(value, bit):
    count = lax.axis_size("wide")
    return lax.ppermute(value, "wide", [(k, k ^ bit) for k in range(count)])


def scatter_sum(value, order):
    me = lax.axis_index("wide")
    for bit in order:
        half = value.shape[0] // 2
        mine = jnp.where((me & bit) == 0, 0, 1)
        away = lax.dynamic_slice_in_dim(value, (1 - mine) * half, half, 0).astype(BF)
        kept = lax.dynamic_slice_in_dim(value, mine * half, half, 0)
        value = kept.astype(F32) + swap_wide(away, bit).astype(F32)
    return value


def gather_shares(value, order):
    me = lax.axis_index("wide")
    value = value.astype(BF)
    for bit in reversed(order):
        came = swap_wide(value, bit)
        low = (me & bit) == 0
        value = jnp.concatenate([jnp.where(low, value, came), jnp.where(low, came, value)], 0)
    return value


def per_device(
    block_in,
    out_grad,
    seq_lens,
    qkv_weight,
    qkv_bias,
    out_weight,
    out_bias,
    up_weight,
    up_bias,
    down_weight,
    down_bias,
    attn_gain,
    attn_shift,
    ffn_gain,
    ffn_shift,
):
    swap = [(0, 1), (1, 0)]
    other_in = lax.ppermute(block_in, "narrow", swap)
    other_grad = lax.ppermute(out_grad, "narrow", swap)
    half = block_in.shape[0]
    group_rows = 2 * half
    heads = out_weight.shape[0] // HD
    own = lax.axis_index("narrow").astype(jnp.int32)
    long = (seq_lens[0, 0] == group_rows).astype(jnp.int32)
    row = lambda v: v.reshape(1, -1)
    order = jnp.arange(group_rows // BQ, dtype=jnp.int32)
    me = lax.axis_index("wide").astype(jnp.int32)
    meta_own = jnp.concatenate([jnp.stack([long, own, me]), order])
    meta_other = jnp.concatenate([jnp.stack([long, 1 - own, me]), order])
    table = jnp.asarray(rope_table(group_rows))
    qkv_w = regroup(qkv_weight, heads)
    weights = (
        qkv_w,
        row(regroup(qkv_bias, heads)),
        up_weight,
        row(up_bias),
        down_weight,
        out_weight,
        row(attn_gain),
        row(attn_shift),
        row(ffn_gain),
        row(ffn_shift),
    )
    qkv, gc, ffn_own, sf_own, *carry = front(
        meta_own, block_in, out_grad, weights, table, group_rows
    )
    qkv, gc, ffn_other, sf_other, early = front(
        meta_other, other_in, other_grad, weights, table, group_rows, (qkv, gc, *carry)
    )
    ag, ash = row(attn_gain), row(attn_shift)
    early = lax.psum(early, "wide")
    ctx, gq, gk, gv = attention(meta_own, qkv, gc, table)
    send_part, send_s = back_rows(
        meta_other, ctx, gq, gk, gv, ffn_other, sf_other, qkv_w, out_weight, ag, BF
    )
    came_s = lax.ppermute(send_s, "narrow", swap)
    came_part = lax.ppermute(send_part, "narrow", swap)
    ctx, send_s = lax.optimization_barrier((ctx, send_s))
    away, kept = back_weights(
        meta_own, block_in, other_in, out_grad, other_grad, ctx, gq, gk, gv, ag, ash
    )
    away, ffn_own = lax.optimization_barrier((away, ffn_own))
    own_part, own_s = back_rows(
        meta_own, ctx, gq, gk, gv, ffn_own, sf_own, qkv_w, out_weight, ag, F32
    )
    mine, peer, gates = late_sum(
        meta_own, away, kept, wide_orders(lax.axis_size("wide")), [None, own_part, early, came_s, None, None, came_part]
    )
    _, own_part, early, came_s, _, _, came_part = gates
    d, hidden = up_weight.shape
    gqkv, gout, gqkv_b, late_vec = unpack_late(meta_own, mine, peer, qkv_w, ag, ash)
    gup, gdown, early_vec = unpack_front(early, d, hidden)
    gup_b = early_vec[8 : 8 + hidden // d].reshape(-1)
    vec = jnp.concatenate([early_vec[:3], late_vec[:2]], 0)
    vec = vec + lax.ppermute(vec, "narrow", swap)
    in_grad = finish(meta_own, block_in, out_grad, own_s, came_s)
    block_out = finish_out(block_in, own_part, came_part, row(out_bias), row(down_bias))
    return (
        block_out,
        in_grad,
        gqkv,
        gqkv_b[0],
        gout,
        vec[2],
        gup,
        gup_b,
        gdown,
        vec[2],
        vec[3],
        vec[4],
        vec[0],
        vec[1],
    )


def solution(mesh):
    rows = P(("wide", "narrow"), None)
    placed = (
        rows,
        rows,
        P("wide", None),
        P(None, "narrow"),
        P("narrow"),
        P("narrow", None),
        P(),
        P(None, "narrow"),
        P("narrow"),
        P("narrow", None),
        P(),
        P(),
        P(),
        P(),
        P(),
    )
    return jax.shard_map(
        per_device,
        mesh=mesh,
        in_specs=placed,
        out_specs=(
            rows,
            rows,
            P(None, "narrow"),
            P("narrow"),
            P("narrow", None),
            P(),
            P(None, "narrow"),
            P("narrow"),
            P("narrow", None),
            P(),
            P(),
            P(),
            P(),
            P(),
        ),
        check_vma=False,
    )
```

```python
import functools

import jax
import jax.numpy as jnp
import numpy as np
from jax import lax
from jax.experimental import pallas as pl
from jax.experimental.pallas import tpu as pltpu
from jax.sharding import PartitionSpec as P

HD = 64
ROT = 16
EPS = 1e-05
NEG = -1e30
SCALE = 0.125
SHORT_LEN = 512
F32 = jnp.float32
BF = jnp.bfloat16
LANES = 128
BQ = 512
BS = 256
ROWS = 256
SMALL_LIMIT = 8 << 20
COST = pl.CostEstimate(flops=1 << 20, bytes_accessed=1 << 12, transcendentals=0)


def nn(a, b):
    return lax.dot_general(a, b, (((1,), (0,)), ((), ())), preferred_element_type=F32)


def nt(a, b):
    return lax.dot_general(a, b, (((1,), (1,)), ((), ())), preferred_element_type=F32)


def tn(a, b):
    return lax.dot_general(a, b, (((0,), (0,)), ((), ())), preferred_element_type=F32)


def colsum(a):
    return jnp.sum(a, axis=0, keepdims=True)


def rope_table(rows):
    half = ROT // 2
    freq = np.float32(1.0) / np.float32(10000.0) ** (
        np.arange(half, dtype=np.float32) * np.float32(2.0) / np.float32(ROT)
    )
    angle = np.arange(rows, dtype=np.float32)[:, None] * freq.astype(np.float32)[None, :]
    table = np.zeros((rows, 2 * HD), np.float32)
    table[:, :HD] = 1.0
    table[:, :half] = table[:, half:ROT] = np.cos(angle)
    table[:, HD : HD + half] = -np.sin(angle)
    table[:, HD + half : HD + ROT] = np.sin(angle)
    return table


def rope(x, table, back):
    lane = lax.broadcasted_iota(jnp.int32, x.shape, 1)
    other = pltpu.roll(table, HD, 1)
    cosine = jnp.where(lane < HD, table, other)
    sine = jnp.where(lane < HD, other, table)
    partner = jnp.where(
        lane % HD < ROT // 2, pltpu.roll(x, LANES - ROT // 2, 1), pltpu.roll(x, ROT // 2, 1)
    )
    return x * cosine - partner * sine if back else x * cosine + partner * sine


def normalize(x):
    center = jnp.mean(x, axis=-1, keepdims=True)
    offset = x - center
    inverse = lax.rsqrt(jnp.mean(offset * offset, axis=-1, keepdims=True) + EPS)
    return offset * inverse, inverse


def once(shape):
    return pl.BlockSpec(shape, lambda i, m: (0,) * len(shape), pipeline_mode=pl.Buffered(1))


def params(mib):
    return pltpu.CompilerParams(vmem_limit_bytes=mib << 20, dimension_semantics=("arbitrary",))


EXTRA = 16
SMALLS = 32


def project(first, qkv_w, qkv_b, table, qkv_ref):
    packed = nn(first, qkv_w[...]) + qkv_b[...].astype(F32)
    third = packed.shape[1] // 3
    for c in range(0, third, LANES):
        q = rope(packed[:, c : c + LANES], table, False).astype(BF)
        qkv_ref[:, c : c + LANES] = (q.astype(F32) * SCALE).astype(BF)
        k = rope(packed[:, third + c : third + c + LANES], table, False)
        qkv_ref[:, third + c : third + c + LANES] = k.astype(BF)
    qkv_ref[:, 2 * third :] = packed[:, 2 * third :].astype(BF)


def gelu_parts(hidden):
    phi = 0.5 * (1.0 + lax.erf(hidden * np.float32(0.5**0.5)))
    density = jnp.exp(-0.5 * hidden * hidden) * np.float32(1.0 / np.sqrt(2.0 * np.pi))
    return hidden * phi, phi + hidden * density


def front_own_kernel(meta, *refs):
    (x_ref, g_ref, qkv_w, qkv_b, up_w, up_b, down_w, out_w, ag, ash, fg, fsh, tab_ref), refs = (
        refs[:13],
        refs[13:],
    )
    (qkv_ref, gc_ref, ffn_ref, s_ref, up_acc, down_acc, vec_ref, vech_ref) = refs
    normed, _ = normalize(x_ref[...].astype(F32))
    g = g_ref[...]
    first = (normed * ag[...].astype(F32) + ash[...].astype(F32)).astype(BF)
    second = (normed * fg[...].astype(F32) + fsh[...].astype(F32)).astype(BF)

    @pl.when(pl.program_id(0) == 0)
    def _():
        for ref in (up_acc, down_acc, vec_ref, vech_ref):
            ref[...] = jnp.zeros_like(ref)

    project(first, qkv_w, qkv_b, tab_ref[...], qkv_ref)
    gc_ref[...] = nt(g, out_w[...]).astype(BF)
    act, slope = gelu_parts(nn(second, up_w[...]) + up_b[...].astype(F32))
    act = act.astype(BF)
    ffn_ref[...] = nn(act, down_w[...])
    gh = (nt(g, down_w[...]) * slope).astype(BF)
    gs = nt(gh, up_w[...])
    s_ref[...] = gs * fg[...].astype(F32)
    vec_ref[0:1, :] += colsum(gs * normed)
    vec_ref[1:2, :] += colsum(gs)
    vec_ref[2:3, :] += colsum(g.astype(F32))
    vech_ref[0:1, :] += colsum(gh.astype(F32))
    up_acc[...] += tn(second, gh)
    down_acc[...] += tn(act, g)


def front_forward_kernel(meta, *refs):
    x_ref, qkv_w, qkv_b, up_w, up_b, down_w, ag, ash, fg, fsh, tab_ref, _ = refs[:12]
    qkv_ref, ffn_ref, act_ref, slope_ref = refs[12:]
    normed, _ = normalize(x_ref[...].astype(F32))
    first = (normed * ag[...].astype(F32) + ash[...].astype(F32)).astype(BF)
    second = (normed * fg[...].astype(F32) + fsh[...].astype(F32)).astype(BF)
    project(first, qkv_w, qkv_b, tab_ref[...], qkv_ref)
    act, slope = gelu_parts(nn(second, up_w[...]) + up_b[...].astype(F32))
    act = act.astype(BF)
    act_ref[...] = act
    slope_ref[...] = slope
    ffn_ref[...] = nn(act, down_w[...])


def front_backward_kernel(meta, *refs):
    x_ref, g_ref, act_ref, slope_ref, up_w, down_w, out_w, fg, fsh, _, *sums_in = refs[:14]
    gc_ref, s_ref, packed_ref, *sums = refs[14:]
    up_acc, down_acc, vec_ref, vech_ref = sums
    i = pl.program_id(0)

    @pl.when(i == 0)
    def _():
        for ref, before in zip(sums, sums_in):
            ref[...] = before[...]

    normed, _ = normalize(x_ref[...].astype(F32))
    second = (normed * fg[...].astype(F32) + fsh[...].astype(F32)).astype(BF)
    g = g_ref[...]
    gc_ref[...] = nt(g, out_w[...]).astype(BF)
    gh = (nt(g, down_w[...]) * slope_ref[...]).astype(BF)
    gs = nt(gh, up_w[...])
    s_ref[...] = gs * fg[...].astype(F32)
    vec_ref[0:1, :] += colsum(gs * normed)
    vec_ref[1:2, :] += colsum(gs)
    vech_ref[0:1, :] += colsum(gh.astype(F32))
    up_acc[...] += tn(second, gh)
    down_acc[...] += tn(act_ref[...], g)

    @pl.when(i == pl.num_programs(0) - 1)
    def _():
        d = up_acc.shape[0]
        hidden_rows = down_acc.shape[0]
        spare = [vec_ref[...]]
        for c in range(0, hidden_rows, d):
            packed_ref[c : c + d, :] = up_acc[:, c : c + d].astype(BF)
            spare.append(vech_ref[0:1, c : c + d])
        packed_ref[hidden_rows : 2 * hidden_rows, :] = down_acc[...].astype(BF)
        pad = EXTRA - vec_ref.shape[0] - (len(spare) - 1)
        spare.append(jnp.zeros((pad, d), F32))
        packed_ref[2 * hidden_rows :, :] = jnp.concatenate(spare, 0).astype(BF)


def front_call(kernel, name, mib, meta, x, ins, outs, aliases, flops, scratch=()):
    count = x.shape[0]
    steps = count // ROWS
    per_short = SHORT_LEN // ROWS

    def spec(shape, kind):
        if kind == "here":
            return pl.BlockSpec((ROWS, shape[1]), lambda i, m: (i, 0))
        if kind == "there":
            return pl.BlockSpec((ROWS, shape[1]), lambda i, m: (m[1] * steps + i, 0))
        if kind == "table":
            block = lambda i, m: m[1] * steps + i
            return pl.BlockSpec(
                (ROWS, shape[1]),
                lambda i, m: (jnp.where(m[0] == 1, block(i, m), lax.rem(block(i, m), per_short)), 0),
            )
        return pl.BlockSpec(memory_space=pl.ANY) if kind == "any" else once(shape)

    return pl.pallas_call(
        kernel,
        grid_spec=pltpu.PrefetchScalarGridSpec(
            num_scalar_prefetch=1,
            grid=(steps,),
            in_specs=[spec(a.shape, kind) for a, kind in ins],
            out_specs=[spec(shape, kind) for (shape, _), kind in outs],
            scratch_shapes=list(scratch),
        ),
        out_shape=[jax.ShapeDtypeStruct(*o) for o, _ in outs],
        input_output_aliases=aliases,
        compiler_params=params(mib),
        cost_estimate=pl.CostEstimate(
            flops=flops, bytes_accessed=16 << 20, transcendentals=0
        ),
        name=name,
    )(meta, *[a for a, _ in ins])


def sums_of(d, hidden):
    return [(d, hidden), (hidden, d), (8, d), (8, hidden)]


def front_own(meta, x, g, weights, table, group_rows):
    (count, d), cols, hidden = x.shape, weights[5].shape[0], weights[2].shape[1]
    return front_call(
        front_own_kernel,
        "front_own",
        44,
        meta,
        x,
        [(x, "here"), (g, "here"), *[(w, "once") for w in weights], (table, "table")],
        [
            (((group_rows, 3 * cols), BF), "there"),
            (((group_rows, cols), BF), "there"),
            (((count, d), F32), "here"),
            (((count, d), F32), "here"),
            *[((shape, F32), "once") for shape in sums_of(d, hidden)],
        ],
        {},
        2 * count * d * (6 * hidden + 4 * cols),
    )


def front_forward(meta, x, weights, table, qkv):
    qkv_w, qkv_b, up_w, up_b, down_w, out_w, ag, ash, fg, fsh = weights
    (count, d), hidden = x.shape, up_w.shape[1]
    once_in = [(w, "once") for w in (qkv_w, qkv_b, up_w, up_b, down_w, ag, ash, fg, fsh)]
    return front_call(
        front_forward_kernel,
        "front_forward",
        32,
        meta,
        x,
        [(x, "here"), *once_in, (table, "table"), (qkv, "any")],
        [
            ((qkv.shape, BF), "there"),
            (((count, d), F32), "here"),
            (((count, hidden), BF), "here"),
            (((count, hidden), F32), "here"),
        ],
        {12: 0},
        2 * count * d * (2 * hidden + qkv.shape[1]),
    )


def front_backward(meta, x, g, act, slope, weights, gc, sums):
    _, _, up_w, _, down_w, out_w, _, _, fg, fsh = weights
    (count, d), hidden = x.shape, up_w.shape[1]
    return front_call(
        front_backward_kernel,
        "front_backward",
        44,
        meta,
        x,
        [
            *[(a, "here") for a in (x, g, act, slope)],
            *[(w, "once") for w in (up_w, down_w, out_w, fg, fsh)],
            (gc, "any"),
            *[(a, "once") for a in sums],
        ],
        [
            ((gc.shape, BF), "there"),
            (((count, d), F32), "here"),
            (((2 * hidden + EXTRA, d), BF), "once"),
        ],
        {10: 0},
        2 * count * d * (4 * hidden + out_w.shape[0]),
        [pltpu.VMEM(shape, F32) for shape in sums_of(d, hidden)],
    )


def unpack_front(packed, d, hidden):
    assert hidden == 2 * d
    steps = 6
    part = d // steps
    chunk = hidden // steps

    def kernel(p0, p1, p2, e_ref, up_ref, down_ref, vec_ref):
        up_ref[:, :d] = p0[...].astype(F32)
        up_ref[:, d:] = p1[...].astype(F32)
        down_ref[...] = p2[...].astype(F32)
        vec_ref[...] = e_ref[...].astype(F32)

    return pl.pallas_call(
        kernel,
        grid=(steps,),
        in_specs=[
            pl.BlockSpec((part, d), lambda i: (i, 0)),
            pl.BlockSpec((part, d), lambda i: (steps + i, 0)),
            pl.BlockSpec((chunk, d), lambda i: (steps + i, 0)),
            pl.BlockSpec((EXTRA, d), lambda i: (2 * hidden // EXTRA, 0)),
        ],
        out_specs=[
            pl.BlockSpec((part, hidden), lambda i: (i, 0)),
            pl.BlockSpec((chunk, d), lambda i: (i, 0)),
            pl.BlockSpec((EXTRA, d), lambda i: (0, 0)),
        ],
        out_shape=[
            jax.ShapeDtypeStruct((d, hidden), F32),
            jax.ShapeDtypeStruct((hidden, d), F32),
            jax.ShapeDtypeStruct((EXTRA, d), F32),
        ],
        compiler_params=params(16),
        cost_estimate=pl.CostEstimate(
            flops=2 * d * hidden, bytes_accessed=12 * d * hidden, transcendentals=0
        ),
        name="unpack_front",
    )(packed, packed, packed, packed)


def attention_kernel(meta, q_ref, k_ref, v_ref, do_ref, tab_ref, *refs):
    ctx_ref, dq_ref, dk_ref, dv_ref, s_sc, e_sc, ds_sc, kt_sc, vt_sc, dk_sc, dv_sc = refs
    i = pl.program_id(1)
    qb = meta[3 + i]
    long = meta[0]
    rows = k_ref.shape[0]
    wide_cols, half_cols = 2 * BQ, 2 * BS
    ext = HD + 16

    @pl.when(i == 0)
    def _():
        dk_sc[...] = jnp.zeros_like(dk_sc)
        dv_sc[...] = jnp.zeros_like(dv_sc)
        kt_sc[...] = k_ref[...].T
        ones = jnp.ones((16, rows), BF)
        vt = v_ref[...].T
        for h in range(2):
            vt_sc[h * ext : h * ext + HD, :] = vt[h * HD : (h + 1) * HD]
            vt_sc[h * ext + HD : (h + 1) * ext, :] = ones

    def process(base, tiles):
        def keys(start, count):
            row = base + start * BS
            return pl.ds(row if isinstance(row, int) else pl.multiple_of(row, BS), count * BS)

        zeros_t = jnp.zeros((HD, BS), BF)
        zeros = jnp.zeros((BS, LANES), BF)
        lane = lax.broadcasted_iota(jnp.int32, (BS, LANES), 1)

        def wide(t):
            return jnp.concatenate(
                [
                    jnp.concatenate(pair, 0)
                    for a in range(0, BQ, BS)
                    for pair in ([t[:HD, a : a + BS], zeros_t], [zeros_t, t[HD:, a : a + BS]])
                ],
                1,
            )

        def tall(t):
            return jnp.concatenate(
                [
                    block
                    for a in range(0, BQ, BS)
                    for block in (
                        jnp.where(lane < HD, t[a : a + BS], zeros),
                        jnp.where(lane < HD, zeros, t[a : a + BS]),
                    )
                ],
                0,
            )

        queries = q_ref[...]
        q_wide, q_tall = wide(queries.T), tall(queries)
        key_index = lax.broadcasted_iota(jnp.int32, (BS, half_cols), 0)
        query_index = lax.broadcasted_iota(jnp.int32, (BS, half_cols), 1) % BS
        causal = key_index <= query_index
        first_col = lambda t: half_cols if t == tiles - 1 else 0
        top = jnp.full((8, wide_cols), NEG, F32)
        for t in range(tiles):
            lo = first_col(t)
            s = nn(k_ref[keys(t, 1), :], q_wide[:, lo:])
            if t == tiles - 1:
                s = jnp.where(causal, s, NEG)
            if t == tiles - 2:
                s = jnp.concatenate(
                    [jnp.where(causal, s[:, :half_cols], NEG), s[:, half_cols:]], 1
                )
            s_sc[t * BS : (t + 1) * BS, lo:] = s
            part = jnp.max(s.reshape(BS // 8, 8, wide_cols - lo), axis=0)
            if lo:
                top = jnp.concatenate([top[:, :lo], jnp.maximum(top[:, lo:], part)], 1)
            else:
                top = jnp.maximum(top, part)
        top = jnp.max(top, axis=0, keepdims=True)
        for t in range(tiles):
            lo = first_col(t)
            block = slice(t * BS, (t + 1) * BS)
            e_sc[block, lo:] = jnp.exp(s_sc[block, lo:] - top[:, lo:]).astype(BF)
        grad_t = do_ref[...].astype(F32).T
        ctx_parts, grad_parts, weighted = [[], []], [[], []], []
        for a in range(2):
            count = tiles - 1 + a
            for h in range(2):
                c = a * half_cols + h * BS
                r = nn(vt_sc[h * ext : (h + 1) * ext, keys(0, count)], e_sc[: count * BS, c : c + BS])
                over_total = 1.0 / r[HD : HD + 1]
                ctx = r[:HD] * over_total
                grad = (grad_t[h * HD : (h + 1) * HD, a * BS : (a + 1) * BS] * over_total).astype(BF)
                weighted.append(colsum(ctx * grad.astype(F32)))
                ctx_parts[a].append(ctx)
                grad_parts[a].append(grad)
        full = lambda parts: jnp.concatenate([jnp.concatenate(part, 0) for part in parts], 1)
        ctx_ref[...] = full(ctx_parts).T.astype(BF)
        grad_full = full(grad_parts)
        g_wide, g_tall = wide(grad_full), tall(grad_full.T)
        weighted = jnp.concatenate(weighted, 1)
        for t in range(tiles):
            lo = first_col(t)
            block = slice(t * BS, (t + 1) * BS)
            e = e_sc[block, lo:]
            gp = nn(v_ref[keys(t, 1), :], g_wide[:, lo:])
            ds = (e.astype(F32) * (gp - weighted[:, lo:])).astype(BF)
            ds_sc[block, lo:] = ds
            dv_sc[keys(t, 1), :] += nn(e, g_tall[lo:])
            dk_sc[keys(t, 1), :] += nn(ds, q_tall[lo:])
        dq_parts = [[], []]
        for a in range(2):
            count = tiles - 1 + a
            for h in range(2):
                c = a * half_cols + h * BS
                dq_parts[a].append(
                    nn(kt_sc[h * HD : (h + 1) * HD, keys(0, count)], ds_sc[: count * BS, c : c + BS])
                )
        at = pl.multiple_of(jnp.where(long == 1, qb, 0) * BQ, BQ)
        dq_ref[...] = rope(full(dq_parts).T * SCALE, tab_ref[pl.ds(at, BQ), :], True).astype(BF)

    for c in range(rows // BQ):

        @pl.when((long == 1) & (qb == c))
        def _(c=c):
            process(0, (c + 1) * (BQ // BS))

    @pl.when(long == 0)
    def _():
        process(qb * BQ, BQ // BS)

    @pl.when(i == pl.num_programs(1) - 1)
    def _():
        dv_ref[...] = dv_sc[...].astype(BF)

        def finish(b, _):
            block = pl.ds(pl.multiple_of(b * BQ, BQ), BQ)
            at = pl.multiple_of(jnp.where(long == 1, b, 0) * BQ, BQ)
            dk_ref[block, :] = rope(dk_sc[block, :], tab_ref[pl.ds(at, BQ), :], True).astype(BF)
            return 0

        lax.fori_loop(0, rows // BQ, finish, 0)


def attention(meta, qkv, grad_ctx, table):
    rows, cols = grad_ctx.shape
    pairs, blocks = cols // LANES, rows // BQ
    at_query = lambda p, i, m: (m[3 + i], p)
    whole = lambda part: lambda p, i, m: (0, part * pairs + p)
    kept = jax.ShapeDtypeStruct((rows, cols), BF)
    return pl.pallas_call(
        attention_kernel,
        grid_spec=pltpu.PrefetchScalarGridSpec(
            num_scalar_prefetch=1,
            grid=(pairs, blocks),
            in_specs=[
                pl.BlockSpec((BQ, LANES), at_query),
                pl.BlockSpec((rows, LANES), whole(1)),
                pl.BlockSpec((rows, LANES), whole(2)),
                pl.BlockSpec((BQ, LANES), at_query),
                pl.BlockSpec((rows, LANES), lambda p, i, m: (0, 0), pipeline_mode=pl.Buffered(1)),
            ],
            out_specs=[
                pl.BlockSpec((BQ, LANES), at_query),
                pl.BlockSpec((BQ, LANES), at_query),
                pl.BlockSpec((rows, LANES), whole(0)),
                pl.BlockSpec((rows, LANES), whole(0)),
            ],
            scratch_shapes=[
                pltpu.VMEM((rows, 2 * BQ), F32),
                pltpu.VMEM((rows, 2 * BQ), BF),
                pltpu.VMEM((rows, 2 * BQ), BF),
                pltpu.VMEM((LANES, rows), BF),
                pltpu.VMEM((2 * (HD + 16), rows), BF),
                pltpu.VMEM((rows, LANES), F32),
                pltpu.VMEM((rows, LANES), F32),
            ],
        ),
        out_shape=[kept] * 4,
        compiler_params=pltpu.CompilerParams(
            vmem_limit_bytes=32 << 20, dimension_semantics=("arbitrary", "arbitrary")
        ),
        cost_estimate=COST,
        name="attention",
    )(meta, qkv, qkv, qkv, grad_ctx, table)


def back_rows_kernel(meta, ctx_ref, gq_ref, gk_ref, gv_ref, ffn_ref, sf_ref, qkv_w, out_w, ag, part_ref, s_ref):
    part_ref[...] = (nn(ctx_ref[...], out_w[...]) + ffn_ref[...]).astype(part_ref.dtype)
    packed = jnp.concatenate([gq_ref[...], gk_ref[...], gv_ref[...]], axis=1)
    s_ref[...] = (nt(packed, qkv_w[...]) * ag[...].astype(F32) + sf_ref[...]).astype(s_ref.dtype)


def back_rows(meta, ctx, gq, gk, gv, ffn, sf, qkv_w, out_w, ag, kind):
    count, d = ffn.shape
    steps = count // ROWS
    cols = out_w.shape[0]
    here = pl.BlockSpec((ROWS, d), lambda i, m: (i, 0))
    there = pl.BlockSpec((ROWS, cols), lambda i, m: (m[1] * steps + i, 0))
    return pl.pallas_call(
        back_rows_kernel,
        grid_spec=pltpu.PrefetchScalarGridSpec(
            num_scalar_prefetch=1,
            grid=(steps,),
            in_specs=[there] * 4 + [here] * 2 + [once(qkv_w.shape), once(out_w.shape), once(ag.shape)],
            out_specs=[here, here],
        ),
        out_shape=[jax.ShapeDtypeStruct((count, d), kind)] * 2,
        compiler_params=params(24),
        cost_estimate=COST,
        name="back_rows",
    )(meta, ctx, gq, gk, gv, ffn, sf, qkv_w, out_w, ag)


def bit_of(me, bit):
    return lax.rem(lax.div(me, bit), 2)


def back_weights_kernel(meta, *refs):
    (x0_ref, x1_ref, g0_ref, g1_ref, ctx_ref, gq_ref, gk_ref, gv_ref, w_ref, ag, ash), refs = refs[:11], refs[11:]
    away_ref, kept_ref, qkv_acc, out_acc, bias_acc, all_sc = refs
    i = pl.program_id(0)
    steps = pl.num_programs(0)

    @pl.when(i == 0)
    def _():
        qkv_acc[...] = jnp.zeros_like(qkv_acc)
        out_acc[...] = jnp.zeros_like(out_acc)
        bias_acc[...] = jnp.zeros_like(bias_acc)

    own = i < steps // 2
    x = jnp.where(own, x0_ref[...].astype(F32), x1_ref[...].astype(F32))
    g = jnp.where(own, g0_ref[...], g1_ref[...])
    normed, _ = normalize(x)
    first = (normed * ag[...].astype(F32) + ash[...].astype(F32)).astype(BF)
    packed = jnp.concatenate([gq_ref[...], gk_ref[...], gv_ref[...]], axis=1)
    bias_acc[0:1, :] += colsum(packed.astype(F32))
    qkv_acc[...] += tn(first, packed)
    out_acc[...] += tn(ctx_ref[...], g)

    @pl.when(i == steps - 1)
    def _():
        d, width = qkv_acc.shape
        third = width // 3
        all_sc[:d, :width] = qkv_acc[...]
        all_sc[d:, :d] = out_acc[: 2 * third // 3, :]
        all_sc[d : d + third // 3, d:width] = out_acc[2 * third // 3 :, :third]
        all_sc[d + third // 3 :, d:width] = out_acc[2 * third // 3 :, third:]
        all_sc[:, width:] = jnp.zeros((all_sc.shape[0], LANES), F32)
        left = jnp.zeros((d, LANES), F32)
        right = jnp.zeros((d, LANES), F32)
        for c in range(0, width, LANES):
            w = w_ref[:, c : c + LANES].astype(F32)
            left += w * qkv_acc[:, c : c + LANES]
            right += w * bias_acc[0:1, c : c + LANES]
        shift_sum = colsum(right.T)
        gain_sum = (colsum(left.T) - ash[...].astype(F32) * shift_sum) / ag[...].astype(F32)
        quarter = all_sc.shape[0] // 4
        row = 0
        for vector in (bias_acc[0:1, :], gain_sum, shift_sum):
            for c in range(0, vector.shape[1], LANES):
                for base in (0, quarter):
                    all_sc[base + row : base + row + 1, width:] = vector[:, c : c + LANES]
                row += 1
        core = bit_of(meta[2], 1)
        for k in range(2):
            here = pl.multiple_of((2 * k + core) * quarter, quarter)
            there = pl.multiple_of((2 * k + 1 - core) * quarter, quarter)
            rows = slice(k * quarter, (k + 1) * quarter)
            kept_ref[rows, :] = all_sc[pl.ds(here, quarter), :]
            away_ref[rows, :] = all_sc[pl.ds(there, quarter), :].astype(BF)


def back_weights(meta, x_own, x_other, g_own, g_other, ctx, gq, gk, gv, qkv_w, ag, ash):
    half, d = x_own.shape
    steps = half // ROWS
    cols = ctx.shape[1]
    assert d == 2 * cols and cols % 3 == 0
    first = pl.BlockSpec((ROWS, d), lambda i, m: (jnp.minimum(i, steps - 1), 0))
    last = pl.BlockSpec((ROWS, d), lambda i, m: (jnp.maximum(i - steps, 0), 0))
    there = pl.BlockSpec(
        (ROWS, cols), lambda i, m: (lax.rem(m[1] * steps + i, 2 * steps), 0)
    )
    rows, width = d + 2 * cols // 3, 3 * cols + LANES
    return pl.pallas_call(
        back_weights_kernel,
        grid_spec=pltpu.PrefetchScalarGridSpec(
            num_scalar_prefetch=1,
            grid=(2 * steps,),
            in_specs=[first, last, first, last] + [there] * 4 + [once(a.shape) for a in (qkv_w, ag, ash)],
            out_specs=[once((rows // 2, width))] * 2,
            scratch_shapes=[
                pltpu.VMEM((d, 3 * cols), F32),
                pltpu.VMEM((cols, d), F32),
                pltpu.VMEM((8, 3 * cols), F32),
                pltpu.VMEM((rows, width), F32),
            ],
        ),
        out_shape=[
            jax.ShapeDtypeStruct((rows // 2, width), BF),
            jax.ShapeDtypeStruct((rows // 2, width), F32),
        ],
        compiler_params=params(32),
        cost_estimate=COST,
        name="back_weights",
    )(meta, x_own, x_other, g_own, g_other, ctx, gq, gk, gv, qkv_w, ag, ash)


def fold_kernel(bits, meta, *refs):
    if len(refs) == 6 and bits[0] is not None:
        rows = refs[0].shape[0] // 2
        ins = [r.at[pl.ds(k * rows, rows), :] for k in range(2) for r in refs[:2]]
        outs = refs[2:]
    else:
        ins, outs = refs[:4], refs[4:]
    for k, bit in enumerate(bits):
        kept, came = ins[2 * k], ins[2 * k + 1]
        if bit is None:
            outs[k][...] = (kept[...] + came[...].astype(F32)).astype(BF)
            continue
        away_ref, kept_ref = outs[2 * k], outs[2 * k + 1]
        half = kept_ref.shape[0]
        mine = bit_of(meta[2], bit)
        here = pl.ds(pl.multiple_of(mine * half, half), half)
        there = pl.ds(pl.multiple_of((1 - mine) * half, half), half)
        kept_ref[...] = kept[here, :] + came[here, :].astype(F32)
        away_ref[...] = (kept[there, :] + came[there, :].astype(F32)).astype(BF)


def spread_kernel(bits, join, meta, *refs):
    ins, outs = refs[:4], refs[4:]
    rows = ins[0].shape[0]
    for k, bit in enumerate(bits):
        out_ref, base = (outs[0], k * 2 * rows) if join else (outs[k], 0)
        mine = bit_of(meta[2], bit)
        out_ref[pl.ds(pl.multiple_of(base + mine * rows, rows), rows), :] = ins[2 * k][...]
        out_ref[pl.ds(pl.multiple_of(base + (1 - mine) * rows, rows), rows), :] = ins[2 * k + 1][...]
    if join:
        outs[1][...] = outs[0][:SMALLS, outs[0].shape[1] - LANES :].astype(F32)


def small_call(kernel, meta, ins, outs, name):
    size = sum(int(np.prod(shape)) for shape, _ in outs)
    held = pl.BlockSpec(memory_space=pltpu.VMEM)
    return pl.pallas_call(
        kernel,
        in_specs=[pl.BlockSpec(memory_space=pltpu.SMEM)] + [held] * len(ins),
        out_specs=[held] * len(outs),
        out_shape=[jax.ShapeDtypeStruct(*o) for o in outs],
        compiler_params=pltpu.CompilerParams(vmem_limit_bytes=SMALL_LIMIT),
        cost_estimate=pl.CostEstimate(flops=size, bytes_accessed=8 * size, transcendentals=0),
        name=name,
    )(meta, *ins)


def late_sum(meta, away, kept, orders, gates):
    gates = list(gates)

    def gated(step, values):
        if step < len(gates) and gates[step] is not None:
            values, gates[step] = lax.optimization_barrier((values, gates[step]))
        return values

    rows, width = kept.shape[0] // 2, kept.shape[1]
    came = swap_wide(away, 1)
    order_a, order_b = orders
    count = lax.axis_size("wide")
    if rows // (count // 2) < 16:
        parts = []
        for k, order in enumerate(orders):
            value = kept[k * rows : (k + 1) * rows] + came[k * rows : (k + 1) * rows].astype(F32)
            parts.append(gather_shares(scatter_sum(value, order[1:]), order[1:]))
        mine = jnp.concatenate(parts, 0)
        return mine, swap_wide(mine, 1), mine[:SMALLS, -LANES:].astype(F32), gates
    ins = [kept, came]
    steps = len(order_a)
    for step in range(1, steps):
        rows //= 2
        shapes = [((rows, width), BF), ((rows, width), F32)] * 2
        bits = (order_a[step], order_b[step])
        away_a, kept_a, away_b, kept_b = small_call(
            functools.partial(fold_kernel, bits), meta, ins, shapes, "fold"
        )
        ins = [kept_a, swap_wide(away_a, bits[0]), kept_b, swap_wide(away_b, bits[1])]
        ins = gated(step, ins)
    share_a, share_b = small_call(
        functools.partial(fold_kernel, (None, None)), meta, ins, [((rows, width), BF)] * 2, "fold"
    )
    for step in range(steps - 1, 0, -1):
        bits = (order_a[step], order_b[step])
        ins = [share_a, swap_wide(share_a, bits[0]), share_b, swap_wide(share_b, bits[1])]
        ins = gated(2 * steps - 1 - step, ins)
        last = step == 1
        shapes = [((4 * rows, width), BF)] if last else [((2 * rows, width), BF)] * 2
        if last:
            shapes.append(((SMALLS, LANES), F32))
        got = small_call(functools.partial(spread_kernel, bits, last), meta, ins, shapes, "spread")
        rows *= 2
        if not last:
            share_a, share_b = got
    return got[0], swap_wide(got[0], 1), got[1], gates


def unpack_late_kernel(meta, mine_ref, peer_ref, small_ref, came_ref, gqkv_ref, gout_ref, bias_ref, vec_ref, all_sc):
    d, width = gqkv_ref.shape
    third = width // 3
    quarter = mine_ref.shape[0] // 2
    core = bit_of(meta[2], 1)
    for k in range(2):
        rows = slice(k * quarter, (k + 1) * quarter)
        here = pl.multiple_of((2 * k + core) * quarter, quarter)
        there = pl.multiple_of((2 * k + 1 - core) * quarter, quarter)
        all_sc[pl.ds(here, quarter), :] = mine_ref[rows, :].astype(F32)
        all_sc[pl.ds(there, quarter), :] = peer_ref[rows, :].astype(F32)
    gout_ref[: 2 * third // 3, :] = all_sc[d:, :d]
    gout_ref[2 * third // 3 :, :third] = all_sc[d : d + third // 3, d:width]
    gout_ref[2 * third // 3 :, third:] = all_sc[d + third // 3 :, d:width]
    lane = lax.broadcasted_iota(jnp.int32, (1, LANES), 1)

    def pick(read, block, to):
        start = block % 3 * third + block // 3 * HD
        tile = read(start // LANES * LANES)
        return tile if start % LANES == to * HD else pltpu.roll(tile, HD, 1)

    count = width // LANES
    bias = jnp.concatenate([small_ref[c : c + 1, :] for c in range(count)], 1)
    bias8 = jnp.broadcast_to(bias, (8, width))
    for t in range(width // LANES):
        to = slice(t * LANES, (t + 1) * LANES)
        read = lambda c: all_sc[:d, c : c + LANES]
        gqkv_ref[:, to] = jnp.where(lane < HD, pick(read, 2 * t, 0), pick(read, 2 * t + 1, 1))
        read = lambda c: bias8[:, c : c + LANES]
        bias_ref[:, to] = jnp.where(lane < HD, pick(read, 2 * t, 0), pick(read, 2 * t + 1, 1))
    both = small_ref[...] + came_ref[...]
    per = d // LANES
    for k in range(2):
        start = count + k * per
        vec_ref[k : k + 1, :] = jnp.concatenate([both[c : c + 1, :] for c in range(start, start + per)], 1)
    vec_ref[2:, :] = jnp.zeros((vec_ref.shape[0] - 2, d), F32)


def unpack_late(meta, mine, peer, small, came, d, cols):
    width = 3 * cols
    whole = lambda shape: pl.BlockSpec(shape, lambda i, m: (0, 0))
    ins = [mine, peer, small, came]
    outs = [(d, width), (cols, d), (8, width), (8, d)]
    return pl.pallas_call(
        unpack_late_kernel,
        grid_spec=pltpu.PrefetchScalarGridSpec(
            num_scalar_prefetch=1,
            grid=(1,),
            in_specs=[whole(a.shape) for a in ins],
            out_specs=[whole(o) for o in outs],
            scratch_shapes=[pltpu.VMEM((2 * mine.shape[0], mine.shape[1]), F32)],
        ),
        out_shape=[jax.ShapeDtypeStruct(o, F32) for o in outs],
        compiler_params=params(24),
        cost_estimate=pl.CostEstimate(flops=4 * d * width, bytes_accessed=8 * d * width, transcendentals=0),
        name="unpack_late",
    )(meta, *ins)


def finish_kernel(meta, x_ref, g_ref, own_ref, came_ref, o_ref):
    normed, inverse = normalize(x_ref[...].astype(F32))
    s = own_ref[...] + came_ref[...].astype(F32)
    back_rows = inverse * (
        s
        - jnp.mean(s, axis=-1, keepdims=True)
        - normed * jnp.mean(s * normed, axis=-1, keepdims=True)
    )
    o_ref[...] = (g_ref[...].astype(F32) + back_rows).astype(BF)


def finish(meta, x, g, own, came):
    count, d = x.shape
    here = pl.BlockSpec((ROWS, d), lambda i, m: (i, 0))
    return pl.pallas_call(
        finish_kernel,
        grid_spec=pltpu.PrefetchScalarGridSpec(
            num_scalar_prefetch=1, grid=(count // ROWS,), in_specs=[here] * 4, out_specs=here
        ),
        out_shape=jax.ShapeDtypeStruct((count, d), BF),
        compiler_params=params(16),
        cost_estimate=pl.CostEstimate(flops=20 * count * d, bytes_accessed=14 * count * d, transcendentals=0),
        name="finish",
    )(meta, x, g, own, came)


def finish_out_kernel(x_ref, own_ref, came_ref, out_bias, down_bias, o_ref):
    bias = out_bias[...].astype(F32) + down_bias[...].astype(F32)
    o_ref[...] = (x_ref[...].astype(F32) + own_ref[...] + came_ref[...].astype(F32) + bias).astype(BF)


def finish_out(x, own, came, out_bias, down_bias):
    count, d = x.shape
    here = pl.BlockSpec((ROWS, d), lambda i: (i, 0))
    bias = pl.BlockSpec((1, d), lambda i: (0, 0))
    return pl.pallas_call(
        finish_out_kernel,
        grid=(count // ROWS,),
        in_specs=[here] * 3 + [bias] * 2,
        out_specs=here,
        out_shape=jax.ShapeDtypeStruct((count, d), BF),
        compiler_params=params(16),
        cost_estimate=pl.CostEstimate(flops=4 * count * d, bytes_accessed=10 * count * d, transcendentals=0),
        name="finish_out",
    )(x, own, came, out_bias, down_bias)


def regroup(w, heads):
    lead = w.shape[:-1]
    return jnp.swapaxes(w.reshape(*lead, heads, 3, HD), -3, -2).reshape(w.shape)


def wide_orders(count):
    bits = [1 << k for k in range(count.bit_length() - 1)]
    return bits, bits[:1] + bits[2:] + bits[1:2]


def swap_wide(value, bit):
    count = lax.axis_size("wide")
    return lax.ppermute(value, "wide", [(k, k ^ bit) for k in range(count)])


def scatter_sum(value, order):
    me = lax.axis_index("wide")
    for bit in order:
        half = value.shape[0] // 2
        mine = jnp.where((me & bit) == 0, 0, 1)
        away = lax.dynamic_slice_in_dim(value, (1 - mine) * half, half, 0).astype(BF)
        kept = lax.dynamic_slice_in_dim(value, mine * half, half, 0)
        value = kept.astype(F32) + swap_wide(away, bit).astype(F32)
    return value


def gather_shares(value, order):
    me = lax.axis_index("wide")
    value = value.astype(BF)
    for bit in reversed(order):
        came = swap_wide(value, bit)
        low = (me & bit) == 0
        value = jnp.concatenate([jnp.where(low, value, came), jnp.where(low, came, value)], 0)
    return value


def per_device(
    block_in,
    out_grad,
    seq_lens,
    qkv_weight,
    qkv_bias,
    out_weight,
    out_bias,
    up_weight,
    up_bias,
    down_weight,
    down_bias,
    attn_gain,
    attn_shift,
    ffn_gain,
    ffn_shift,
):
    swap = [(0, 1), (1, 0)]
    other_in = lax.ppermute(block_in, "narrow", swap)
    other_grad = lax.ppermute(out_grad, "narrow", swap)
    half = block_in.shape[0]
    group_rows = 2 * half
    heads = out_weight.shape[0] // HD
    own = lax.axis_index("narrow").astype(jnp.int32)
    long = (seq_lens[0, 0] == group_rows).astype(jnp.int32)
    row = lambda v: v.reshape(1, -1)
    order = jnp.arange(group_rows // BQ, dtype=jnp.int32)
    me = lax.axis_index("wide").astype(jnp.int32)
    meta_own = jnp.concatenate([jnp.stack([long, own, me]), order])
    meta_other = jnp.concatenate([jnp.stack([long, 1 - own, me]), order])
    table = jnp.asarray(rope_table(group_rows))
    qkv_w = regroup(qkv_weight, heads)
    weights = (
        qkv_w,
        row(regroup(qkv_bias, heads)),
        up_weight,
        row(up_bias),
        down_weight,
        out_weight,
        row(attn_gain),
        row(attn_shift),
        row(ffn_gain),
        row(ffn_shift),
    )
    qkv, gc, ffn_own, sf_own, *sums = front_own(
        meta_own, block_in, out_grad, weights, table, group_rows
    )
    qkv, ffn_other, act, slope = front_forward(meta_other, other_in, weights, table, qkv)
    gc, sf_other, early = front_backward(
        meta_other, other_in, other_grad, act, slope, weights, gc, sums
    )
    ag, ash = row(attn_gain), row(attn_shift)
    early = lax.psum(early, "wide")
    ctx, gq, gk, gv = attention(meta_own, qkv, gc, table)
    send_part, send_s = back_rows(
        meta_other, ctx, gq, gk, gv, ffn_other, sf_other, qkv_w, out_weight, ag, BF
    )
    came_s = lax.ppermute(send_s, "narrow", swap)
    came_part = lax.ppermute(send_part, "narrow", swap)
    ctx, send_s = lax.optimization_barrier((ctx, send_s))
    away, kept = back_weights(
        meta_own, block_in, other_in, out_grad, other_grad, ctx, gq, gk, gv, qkv_w, ag, ash
    )
    away, ffn_own = lax.optimization_barrier((away, ffn_own))
    own_part, own_s = back_rows(
        meta_own, ctx, gq, gk, gv, ffn_own, sf_own, qkv_w, out_weight, ag, F32
    )
    d, hidden = up_weight.shape
    in_grad = finish(meta_own, block_in, out_grad, own_s, came_s)
    block_out = finish_out(block_in, own_part, came_part, row(out_bias), row(down_bias))
    gup, gdown, early_vec = unpack_front(early, d, hidden)
    early_vec = early_vec[:3] + lax.ppermute(early_vec, "narrow", swap)[:3], early_vec[8 : 8 + hidden // d]
    gates = [None, None, own_part, came_s, (early, in_grad), (gup, gdown, early_vec), block_out]
    mine, peer, small, gates = late_sum(
        meta_own, away, kept, wide_orders(lax.axis_size("wide")), gates
    )
    _, _, _, _, (_, in_grad), (gup, gdown, early_vec), block_out = gates
    gqkv, gout, gqkv_b, late_vec = unpack_late(
        meta_own, mine, peer, small, lax.ppermute(small, "narrow", swap), d, out_weight.shape[0]
    )
    vec, gup_b = early_vec
    return (
        block_out,
        in_grad,
        gqkv,
        gqkv_b[0],
        gout,
        vec[2],
        gup,
        gup_b.reshape(-1),
        gdown,
        vec[2],
        late_vec[0],
        late_vec[1],
        vec[0],
        vec[1],
    )


def solution(mesh):
    rows = P(("wide", "narrow"), None)
    placed = (
        rows,
        rows,
        P("wide", None),
        P(None, "narrow"),
        P("narrow"),
        P("narrow", None),
        P(),
        P(None, "narrow"),
        P("narrow"),
        P("narrow", None),
        P(),
        P(),
        P(),
        P(),
        P(),
    )
    return jax.shard_map(
        per_device,
        mesh=mesh,
        in_specs=placed,
        out_specs=(
            rows,
            rows,
            P(None, "narrow"),
            P("narrow"),
            P("narrow", None),
            P(),
            P(None, "narrow"),
            P("narrow"),
            P("narrow", None),
            P(),
            P(),
            P(),
            P(),
            P(),
        ),
        check_vma=False,
    )
```

```python
import functools

import jax
import jax.numpy as jnp
import numpy as np
from jax import lax
from jax.experimental import pallas as pl
from jax.experimental.pallas import tpu as pltpu
from jax.sharding import PartitionSpec as P

HD = 64
ROT = 16
EPS = 1e-05
NEG = -1e30
SCALE = 0.125
SHORT_LEN = 512
F32 = jnp.float32
BF = jnp.bfloat16
LANES = 128
BQ = 512
BS = 256
ROWS = 512
SMALL_LIMIT = 8 << 20
COST = pl.CostEstimate(flops=1 << 20, bytes_accessed=1 << 12, transcendentals=0)


def nn(a, b):
    return lax.dot_general(a, b, (((1,), (0,)), ((), ())), preferred_element_type=F32)


def nt(a, b):
    return lax.dot_general(a, b, (((1,), (1,)), ((), ())), preferred_element_type=F32)


def tn(a, b):
    return lax.dot_general(a, b, (((0,), (0,)), ((), ())), preferred_element_type=F32)


def colsum(a):
    return jnp.sum(a, axis=0, keepdims=True)


def rope_table(rows):
    half = ROT // 2
    freq = np.float32(1.0) / np.float32(10000.0) ** (
        np.arange(half, dtype=np.float32) * np.float32(2.0) / np.float32(ROT)
    )
    angle = np.arange(rows, dtype=np.float32)[:, None] * freq.astype(np.float32)[None, :]
    table = np.zeros((rows, 2 * HD), np.float32)
    table[:, :HD] = 1.0
    table[:, :half] = table[:, half:ROT] = np.cos(angle)
    table[:, HD : HD + half] = -np.sin(angle)
    table[:, HD + half : HD + ROT] = np.sin(angle)
    return table


def rope(x, table, back):
    lane = lax.broadcasted_iota(jnp.int32, x.shape, 1)
    other = pltpu.roll(table, HD, 1)
    cosine = jnp.where(lane < HD, table, other)
    sine = jnp.where(lane < HD, other, table)
    partner = jnp.where(
        lane % HD < ROT // 2, pltpu.roll(x, LANES - ROT // 2, 1), pltpu.roll(x, ROT // 2, 1)
    )
    return x * cosine - partner * sine if back else x * cosine + partner * sine


def normalize(x):
    center = jnp.mean(x, axis=-1, keepdims=True)
    offset = x - center
    inverse = lax.rsqrt(jnp.mean(offset * offset, axis=-1, keepdims=True) + EPS)
    return offset * inverse, inverse


def once(shape):
    return pl.BlockSpec(shape, lambda i, m: (0,) * len(shape), pipeline_mode=pl.Buffered(1))


def params(mib):
    return pltpu.CompilerParams(vmem_limit_bytes=mib << 20, dimension_semantics=("arbitrary",))


EXTRA = 16
SMALLS = 32


def project(first, qkv_w, qkv_b, table, qkv_ref):
    packed = nn(first, qkv_w[...]) + qkv_b[...].astype(F32)
    third = packed.shape[1] // 3
    for c in range(0, third, LANES):
        q = rope(packed[:, c : c + LANES], table, False).astype(BF)
        qkv_ref[:, c : c + LANES] = (q.astype(F32) * SCALE).astype(BF)
        k = rope(packed[:, third + c : third + c + LANES], table, False)
        qkv_ref[:, third + c : third + c + LANES] = k.astype(BF)
    qkv_ref[:, 2 * third :] = packed[:, 2 * third :].astype(BF)


def gelu_parts(hidden):
    phi = 0.5 * (1.0 + lax.erf(hidden * np.float32(0.5**0.5)))
    density = jnp.exp(-0.5 * hidden * hidden) * np.float32(1.0 / np.sqrt(2.0 * np.pi))
    return hidden * phi, phi + hidden * density


def front_own_kernel(meta, *refs):
    (x_ref, g_ref, qkv_w, qkv_b, up_w, up_b, down_w, out_w, ag, ash, fg, fsh, tab_ref), refs = (
        refs[:13],
        refs[13:],
    )
    (qkv_ref, gc_ref, ffn_ref, s_ref, up_acc, down_acc, vec_ref, vech_ref) = refs
    normed, _ = normalize(x_ref[...].astype(F32))
    g = g_ref[...]
    first = (normed * ag[...].astype(F32) + ash[...].astype(F32)).astype(BF)
    second = (normed * fg[...].astype(F32) + fsh[...].astype(F32)).astype(BF)

    @pl.when(pl.program_id(0) == 0)
    def _():
        for ref in (up_acc, down_acc, vec_ref, vech_ref):
            ref[...] = jnp.zeros_like(ref)

    project(first, qkv_w, qkv_b, tab_ref[...], qkv_ref)
    gc_ref[...] = nt(g, out_w[...]).astype(BF)
    act, slope = gelu_parts(nn(second, up_w[...]) + up_b[...].astype(F32))
    act = act.astype(BF)
    ffn_ref[...] = nn(act, down_w[...])
    gh = (nt(g, down_w[...]) * slope).astype(BF)
    gs = nt(gh, up_w[...])
    s_ref[...] = gs * fg[...].astype(F32)
    vec_ref[0:1, :] += colsum(gs * normed)
    vec_ref[1:2, :] += colsum(gs)
    vec_ref[2:3, :] += colsum(g.astype(F32))
    vech_ref[0:1, :] += colsum(gh.astype(F32))
    up_acc[...] += tn(second, gh)
    down_acc[...] += tn(act, g)


def front_forward_kernel(meta, *refs):
    x_ref, qkv_w, qkv_b, up_w, up_b, down_w, ag, ash, fg, fsh, tab_ref, _ = refs[:12]
    qkv_ref, ffn_ref, act_ref, slope_ref = refs[12:]
    normed, _ = normalize(x_ref[...].astype(F32))
    first = (normed * ag[...].astype(F32) + ash[...].astype(F32)).astype(BF)
    second = (normed * fg[...].astype(F32) + fsh[...].astype(F32)).astype(BF)
    project(first, qkv_w, qkv_b, tab_ref[...], qkv_ref)
    act, slope = gelu_parts(nn(second, up_w[...]) + up_b[...].astype(F32))
    act = act.astype(BF)
    act_ref[...] = act
    slope_ref[...] = slope
    ffn_ref[...] = nn(act, down_w[...])


def front_backward_kernel(meta, *refs):
    x_ref, g_ref, act_ref, slope_ref, up_w, down_w, out_w, fg, fsh, _, *sums_in = refs[:14]
    gc_ref, s_ref, packed_ref, *rest = refs[14:]
    sums, befores, sems = rest[:4], rest[4:8], rest[8]
    up_acc, down_acc, vec_ref, vech_ref = sums
    i = pl.program_id(0)
    copies = [
        pltpu.make_async_copy(src, dst, sems.at[k])
        for k, (src, dst) in enumerate(zip(sums_in, befores))
    ]

    @pl.when(i == 0)
    def _():
        for copy in copies:
            copy.start()
        for ref in sums:
            ref[...] = jnp.zeros_like(ref)

    normed, _ = normalize(x_ref[...].astype(F32))
    second = (normed * fg[...].astype(F32) + fsh[...].astype(F32)).astype(BF)
    g = g_ref[...]
    gc_ref[...] = nt(g, out_w[...]).astype(BF)
    gh = (nt(g, down_w[...]) * slope_ref[...]).astype(BF)
    gs = nt(gh, up_w[...])
    s_ref[...] = gs * fg[...].astype(F32)
    vec_ref[0:1, :] += colsum(gs * normed)
    vec_ref[1:2, :] += colsum(gs)
    vech_ref[0:1, :] += colsum(gh.astype(F32))
    up_acc[...] += tn(second, gh)
    down_acc[...] += tn(act_ref[...], g)

    @pl.when(i == pl.num_programs(0) - 1)
    def _():
        for copy in copies:
            copy.wait()
        up_in, down_in, vec_in, vech_in = befores
        d = up_acc.shape[0]
        hidden_rows = down_acc.shape[0]
        spare = [vec_ref[...] + vec_in[...]]
        for c in range(0, hidden_rows, d):
            packed_ref[c : c + d, :] = (up_acc[:, c : c + d] + up_in[:, c : c + d]).astype(BF)
            spare.append(vech_ref[0:1, c : c + d] + vech_in[0:1, c : c + d])
        packed_ref[hidden_rows : 2 * hidden_rows, :] = (down_acc[...] + down_in[...]).astype(BF)
        pad = EXTRA - vec_ref.shape[0] - (len(spare) - 1)
        spare.append(jnp.zeros((pad, d), F32))
        packed_ref[2 * hidden_rows :, :] = jnp.concatenate(spare, 0).astype(BF)


def front_call(kernel, name, mib, meta, x, ins, outs, aliases, flops, scratch=()):
    count = x.shape[0]
    steps = count // ROWS
    per_short = SHORT_LEN // ROWS

    def spec(shape, kind):
        if kind == "here":
            return pl.BlockSpec((ROWS, shape[1]), lambda i, m: (i, 0))
        if kind == "there":
            return pl.BlockSpec((ROWS, shape[1]), lambda i, m: (m[1] * steps + i, 0))
        if kind == "table":
            block = lambda i, m: m[1] * steps + i
            return pl.BlockSpec(
                (ROWS, shape[1]),
                lambda i, m: (jnp.where(m[0] == 1, block(i, m), lax.rem(block(i, m), per_short)), 0),
            )
        return pl.BlockSpec(memory_space=pl.ANY) if kind == "any" else once(shape)

    return pl.pallas_call(
        kernel,
        grid_spec=pltpu.PrefetchScalarGridSpec(
            num_scalar_prefetch=1,
            grid=(steps,),
            in_specs=[spec(a.shape, kind) for a, kind in ins],
            out_specs=[spec(shape, kind) for (shape, _), kind in outs],
            scratch_shapes=list(scratch),
        ),
        out_shape=[jax.ShapeDtypeStruct(*o) for o, _ in outs],
        input_output_aliases=aliases,
        compiler_params=params(mib),
        cost_estimate=pl.CostEstimate(
            flops=flops, bytes_accessed=16 << 20, transcendentals=0
        ),
        name=name,
    )(meta, *[a for a, _ in ins])


def sums_of(d, hidden):
    return [(d, hidden), (hidden, d), (8, d), (8, hidden)]


def front_own(meta, x, g, weights, table, group_rows):
    (count, d), cols, hidden = x.shape, weights[5].shape[0], weights[2].shape[1]
    return front_call(
        front_own_kernel,
        "front_own",
        44,
        meta,
        x,
        [(x, "here"), (g, "here"), *[(w, "once") for w in weights], (table, "table")],
        [
            (((group_rows, 3 * cols), BF), "there"),
            (((group_rows, cols), BF), "there"),
            (((count, d), F32), "here"),
            (((count, d), F32), "here"),
            *[((shape, F32), "once") for shape in sums_of(d, hidden)],
        ],
        {},
        2 * count * d * (6 * hidden + 4 * cols),
    )


def front_forward(meta, x, weights, table, qkv):
    qkv_w, qkv_b, up_w, up_b, down_w, out_w, ag, ash, fg, fsh = weights
    (count, d), hidden = x.shape, up_w.shape[1]
    once_in = [(w, "once") for w in (qkv_w, qkv_b, up_w, up_b, down_w, ag, ash, fg, fsh)]
    return front_call(
        front_forward_kernel,
        "front_forward",
        32,
        meta,
        x,
        [(x, "here"), *once_in, (table, "table"), (qkv, "any")],
        [
            ((qkv.shape, BF), "there"),
            (((count, d), F32), "here"),
            (((count, hidden), BF), "here"),
            (((count, hidden), F32), "here"),
        ],
        {12: 0},
        2 * count * d * (2 * hidden + qkv.shape[1]),
    )


def front_backward(meta, x, g, act, slope, weights, gc, sums):
    _, _, up_w, _, down_w, out_w, _, _, fg, fsh = weights
    (count, d), hidden = x.shape, up_w.shape[1]
    return front_call(
        front_backward_kernel,
        "front_backward",
        44,
        meta,
        x,
        [
            *[(a, "here") for a in (x, g, act, slope)],
            *[(w, "once") for w in (up_w, down_w, out_w, fg, fsh)],
            (gc, "any"),
            *[(a, "any") for a in sums],
        ],
        [
            ((gc.shape, BF), "there"),
            (((count, d), F32), "here"),
            (((2 * hidden + EXTRA, d), BF), "once"),
        ],
        {10: 0},
        2 * count * d * (4 * hidden + out_w.shape[0]),
        [pltpu.VMEM(shape, F32) for shape in sums_of(d, hidden)] * 2 + [pltpu.SemaphoreType.DMA((4,))],
    )


def unpack_front(packed, d, hidden):
    assert hidden == 2 * d
    steps = 6
    part = d // steps
    chunk = hidden // steps

    def kernel(p0, p1, p2, e_ref, up_ref, down_ref, vec_ref):
        up_ref[:, :d] = p0[...].astype(F32)
        up_ref[:, d:] = p1[...].astype(F32)
        down_ref[...] = p2[...].astype(F32)
        vec_ref[...] = e_ref[...].astype(F32)

    return pl.pallas_call(
        kernel,
        grid=(steps,),
        in_specs=[
            pl.BlockSpec((part, d), lambda i: (i, 0)),
            pl.BlockSpec((part, d), lambda i: (steps + i, 0)),
            pl.BlockSpec((chunk, d), lambda i: (steps + i, 0)),
            pl.BlockSpec((EXTRA, d), lambda i: (2 * hidden // EXTRA, 0)),
        ],
        out_specs=[
            pl.BlockSpec((part, hidden), lambda i: (i, 0)),
            pl.BlockSpec((chunk, d), lambda i: (i, 0)),
            pl.BlockSpec((EXTRA, d), lambda i: (0, 0)),
        ],
        out_shape=[
            jax.ShapeDtypeStruct((d, hidden), F32),
            jax.ShapeDtypeStruct((hidden, d), F32),
            jax.ShapeDtypeStruct((EXTRA, d), F32),
        ],
        compiler_params=params(16),
        cost_estimate=pl.CostEstimate(
            flops=2 * d * hidden, bytes_accessed=12 * d * hidden, transcendentals=0
        ),
        name="unpack_front",
    )(packed, packed, packed, packed)


def attention_kernel(meta, q_ref, k_ref, v_ref, do_ref, tab_ref, *refs):
    ctx_ref, dq_ref, dk_ref, dv_ref, s_sc, e_sc, ds_sc, kt_sc, vt_sc, dk_sc, dv_sc = refs
    i = pl.program_id(1)
    qb = meta[3 + i]
    long = meta[0]
    rows = k_ref.shape[0]
    wide_cols, half_cols = 2 * BQ, 2 * BS
    ext = HD + 16

    @pl.when(i == 0)
    def _():
        dk_sc[...] = jnp.zeros_like(dk_sc)
        dv_sc[...] = jnp.zeros_like(dv_sc)
        kt_sc[...] = k_ref[...].T
        ones = jnp.ones((16, rows), BF)
        vt = v_ref[...].T
        for h in range(2):
            vt_sc[h * ext : h * ext + HD, :] = vt[h * HD : (h + 1) * HD]
            vt_sc[h * ext + HD : (h + 1) * ext, :] = ones

    def process(base, tiles):
        def keys(start, count):
            row = base + start * BS
            return pl.ds(row if isinstance(row, int) else pl.multiple_of(row, BS), count * BS)

        zeros_t = jnp.zeros((HD, BS), BF)
        zeros = jnp.zeros((BS, LANES), BF)
        lane = lax.broadcasted_iota(jnp.int32, (BS, LANES), 1)

        def wide(t):
            return jnp.concatenate(
                [
                    jnp.concatenate(pair, 0)
                    for a in range(0, BQ, BS)
                    for pair in ([t[:HD, a : a + BS], zeros_t], [zeros_t, t[HD:, a : a + BS]])
                ],
                1,
            )

        def tall(t):
            return jnp.concatenate(
                [
                    block
                    for a in range(0, BQ, BS)
                    for block in (
                        jnp.where(lane < HD, t[a : a + BS], zeros),
                        jnp.where(lane < HD, zeros, t[a : a + BS]),
                    )
                ],
                0,
            )

        queries = q_ref[...]
        q_wide, q_tall = wide(queries.T), tall(queries)
        key_index = lax.broadcasted_iota(jnp.int32, (BS, half_cols), 0)
        query_index = lax.broadcasted_iota(jnp.int32, (BS, half_cols), 1) % BS
        causal = key_index <= query_index
        first_col = lambda t: half_cols if t == tiles - 1 else 0
        top = jnp.full((8, wide_cols), NEG, F32)
        for t in range(tiles):
            lo = first_col(t)
            s = nn(k_ref[keys(t, 1), :], q_wide[:, lo:])
            if t == tiles - 1:
                s = jnp.where(causal, s, NEG)
            if t == tiles - 2:
                s = jnp.concatenate(
                    [jnp.where(causal, s[:, :half_cols], NEG), s[:, half_cols:]], 1
                )
            s_sc[t * BS : (t + 1) * BS, lo:] = s
            part = jnp.max(s.reshape(BS // 8, 8, wide_cols - lo), axis=0)
            if lo:
                top = jnp.concatenate([top[:, :lo], jnp.maximum(top[:, lo:], part)], 1)
            else:
                top = jnp.maximum(top, part)
        top = jnp.max(top, axis=0, keepdims=True)
        for t in range(tiles):
            lo = first_col(t)
            block = slice(t * BS, (t + 1) * BS)
            e_sc[block, lo:] = jnp.exp(s_sc[block, lo:] - top[:, lo:]).astype(BF)
        grad_t = do_ref[...].astype(F32).T
        ctx_parts, grad_parts, weighted = [[], []], [[], []], []
        for a in range(2):
            count = tiles - 1 + a
            for h in range(2):
                c = a * half_cols + h * BS
                r = nn(vt_sc[h * ext : (h + 1) * ext, keys(0, count)], e_sc[: count * BS, c : c + BS])
                over_total = 1.0 / r[HD : HD + 1]
                ctx = r[:HD] * over_total
                grad = (grad_t[h * HD : (h + 1) * HD, a * BS : (a + 1) * BS] * over_total).astype(BF)
                weighted.append(colsum(ctx * grad.astype(F32)))
                ctx_parts[a].append(ctx)
                grad_parts[a].append(grad)
        full = lambda parts: jnp.concatenate([jnp.concatenate(part, 0) for part in parts], 1)
        ctx_ref[...] = full(ctx_parts).T.astype(BF)
        grad_full = full(grad_parts)
        g_wide, g_tall = wide(grad_full), tall(grad_full.T)
        weighted = jnp.concatenate(weighted, 1)
        for t in range(tiles):
            lo = first_col(t)
            block = slice(t * BS, (t + 1) * BS)
            e = e_sc[block, lo:]
            gp = nn(v_ref[keys(t, 1), :], g_wide[:, lo:])
            ds = (e.astype(F32) * (gp - weighted[:, lo:])).astype(BF)
            ds_sc[block, lo:] = ds
            dv_sc[keys(t, 1), :] += nn(e, g_tall[lo:])
            dk_sc[keys(t, 1), :] += nn(ds, q_tall[lo:])
        dq_parts = [[], []]
        for a in range(2):
            count = tiles - 1 + a
            for h in range(2):
                c = a * half_cols + h * BS
                dq_parts[a].append(
                    nn(kt_sc[h * HD : (h + 1) * HD, keys(0, count)], ds_sc[: count * BS, c : c + BS])
                )
        at = pl.multiple_of(jnp.where(long == 1, qb, 0) * BQ, BQ)
        dq_ref[...] = rope(full(dq_parts).T * SCALE, tab_ref[pl.ds(at, BQ), :], True).astype(BF)

    for c in range(rows // BQ):

        @pl.when((long == 1) & (qb == c))
        def _(c=c):
            process(0, (c + 1) * (BQ // BS))

    @pl.when(long == 0)
    def _():
        process(qb * BQ, BQ // BS)

    @pl.when(i == pl.num_programs(1) - 1)
    def _():
        dv_ref[...] = dv_sc[...].astype(BF)

        def finish(b, _):
            block = pl.ds(pl.multiple_of(b * BQ, BQ), BQ)
            at = pl.multiple_of(jnp.where(long == 1, b, 0) * BQ, BQ)
            dk_ref[block, :] = rope(dk_sc[block, :], tab_ref[pl.ds(at, BQ), :], True).astype(BF)
            return 0

        lax.fori_loop(0, rows // BQ, finish, 0)


def attention(meta, qkv, grad_ctx, table):
    rows, cols = grad_ctx.shape
    pairs, blocks = cols // LANES, rows // BQ
    at_query = lambda p, i, m: (m[3 + i], p)
    whole = lambda part: lambda p, i, m: (0, part * pairs + p)
    kept = jax.ShapeDtypeStruct((rows, cols), BF)
    return pl.pallas_call(
        attention_kernel,
        grid_spec=pltpu.PrefetchScalarGridSpec(
            num_scalar_prefetch=1,
            grid=(pairs, blocks),
            in_specs=[
                pl.BlockSpec((BQ, LANES), at_query),
                pl.BlockSpec((rows, LANES), whole(1)),
                pl.BlockSpec((rows, LANES), whole(2)),
                pl.BlockSpec((BQ, LANES), at_query),
                pl.BlockSpec((rows, LANES), lambda p, i, m: (0, 0), pipeline_mode=pl.Buffered(1)),
            ],
            out_specs=[
                pl.BlockSpec((BQ, LANES), at_query),
                pl.BlockSpec((BQ, LANES), at_query),
                pl.BlockSpec((rows, LANES), whole(0)),
                pl.BlockSpec((rows, LANES), whole(0)),
            ],
            scratch_shapes=[
                pltpu.VMEM((rows, 2 * BQ), F32),
                pltpu.VMEM((rows, 2 * BQ), BF),
                pltpu.VMEM((rows, 2 * BQ), BF),
                pltpu.VMEM((LANES, rows), BF),
                pltpu.VMEM((2 * (HD + 16), rows), BF),
                pltpu.VMEM((rows, LANES), F32),
                pltpu.VMEM((rows, LANES), F32),
            ],
        ),
        out_shape=[kept] * 4,
        compiler_params=pltpu.CompilerParams(
            vmem_limit_bytes=32 << 20, dimension_semantics=("arbitrary", "arbitrary")
        ),
        cost_estimate=COST,
        name="attention",
    )(meta, qkv, qkv, qkv, grad_ctx, table)


def back_rows_kernel(meta, ctx_ref, gq_ref, gk_ref, gv_ref, ffn_ref, sf_ref, qkv_w, out_w, ag, part_ref, s_ref):
    part_ref[...] = (nn(ctx_ref[...], out_w[...]) + ffn_ref[...]).astype(part_ref.dtype)
    packed = jnp.concatenate([gq_ref[...], gk_ref[...], gv_ref[...]], axis=1)
    s_ref[...] = (nt(packed, qkv_w[...]) * ag[...].astype(F32) + sf_ref[...]).astype(s_ref.dtype)


def back_rows(meta, ctx, gq, gk, gv, ffn, sf, qkv_w, out_w, ag, kind):
    count, d = ffn.shape
    steps = count // ROWS
    cols = out_w.shape[0]
    here = pl.BlockSpec((ROWS, d), lambda i, m: (i, 0))
    there = pl.BlockSpec((ROWS, cols), lambda i, m: (m[1] * steps + i, 0))
    return pl.pallas_call(
        back_rows_kernel,
        grid_spec=pltpu.PrefetchScalarGridSpec(
            num_scalar_prefetch=1,
            grid=(steps,),
            in_specs=[there] * 4 + [here] * 2 + [once(qkv_w.shape), once(out_w.shape), once(ag.shape)],
            out_specs=[here, here],
        ),
        out_shape=[jax.ShapeDtypeStruct((count, d), kind)] * 2,
        compiler_params=params(24),
        cost_estimate=COST,
        name="back_rows",
    )(meta, ctx, gq, gk, gv, ffn, sf, qkv_w, out_w, ag)


def bit_of(me, bit):
    return lax.rem(lax.div(me, bit), 2)


def back_weights_kernel(meta, *refs):
    (x0_ref, x1_ref, g0_ref, g1_ref, ctx_ref, gq_ref, gk_ref, gv_ref, w_ref, ag, ash), refs = refs[:11], refs[11:]
    away_ref, kept_ref, qkv_acc, out_acc, bias_acc, all_sc = refs
    i = pl.program_id(0)
    steps = pl.num_programs(0)

    @pl.when(i == 0)
    def _():
        qkv_acc[...] = jnp.zeros_like(qkv_acc)
        out_acc[...] = jnp.zeros_like(out_acc)
        bias_acc[...] = jnp.zeros_like(bias_acc)

    own = i < steps // 2
    x = jnp.where(own, x0_ref[...].astype(F32), x1_ref[...].astype(F32))
    g = jnp.where(own, g0_ref[...], g1_ref[...])
    normed, _ = normalize(x)
    first = (normed * ag[...].astype(F32) + ash[...].astype(F32)).astype(BF)
    packed = jnp.concatenate([gq_ref[...], gk_ref[...], gv_ref[...]], axis=1)
    bias_acc[0:1, :] += colsum(packed.astype(F32))
    qkv_acc[...] += tn(first, packed)
    out_acc[...] += tn(ctx_ref[...], g)

    @pl.when(i == steps - 1)
    def _():
        d, width = qkv_acc.shape
        third = width // 3
        all_sc[:d, :width] = qkv_acc[...]
        all_sc[d:, :d] = out_acc[: 2 * third // 3, :]
        all_sc[d : d + third // 3, d:width] = out_acc[2 * third // 3 :, :third]
        all_sc[d + third // 3 :, d:width] = out_acc[2 * third // 3 :, third:]
        all_sc[:, width:] = jnp.zeros((all_sc.shape[0], LANES), F32)
        left = jnp.zeros((d, LANES), F32)
        right = jnp.zeros((d, LANES), F32)
        for c in range(0, width, LANES):
            w = w_ref[:, c : c + LANES].astype(F32)
            left += w * qkv_acc[:, c : c + LANES]
            right += w * bias_acc[0:1, c : c + LANES]
        shift_sum = colsum(right.T)
        gain_sum = (colsum(left.T) - ash[...].astype(F32) * shift_sum) / ag[...].astype(F32)
        quarter = all_sc.shape[0] // 4
        row = 0
        for vector in (bias_acc[0:1, :], gain_sum, shift_sum):
            for c in range(0, vector.shape[1], LANES):
                for base in (0, quarter):
                    all_sc[base + row : base + row + 1, width:] = vector[:, c : c + LANES]
                row += 1
        core = bit_of(meta[2], 1)
        for k in range(2):
            here = pl.multiple_of((2 * k + core) * quarter, quarter)
            there = pl.multiple_of((2 * k + 1 - core) * quarter, quarter)
            rows = slice(k * quarter, (k + 1) * quarter)
            kept_ref[rows, :] = all_sc[pl.ds(here, quarter), :]
            away_ref[rows, :] = all_sc[pl.ds(there, quarter), :].astype(BF)


def back_weights(meta, x_own, x_other, g_own, g_other, ctx, gq, gk, gv, qkv_w, ag, ash):
    half, d = x_own.shape
    steps = half // ROWS
    cols = ctx.shape[1]
    assert d == 2 * cols and cols % 3 == 0
    first = pl.BlockSpec((ROWS, d), lambda i, m: (jnp.minimum(i, steps - 1), 0))
    last = pl.BlockSpec((ROWS, d), lambda i, m: (jnp.maximum(i - steps, 0), 0))
    there = pl.BlockSpec(
        (ROWS, cols), lambda i, m: (lax.rem(m[1] * steps + i, 2 * steps), 0)
    )
    rows, width = d + 2 * cols // 3, 3 * cols + LANES
    return pl.pallas_call(
        back_weights_kernel,
        grid_spec=pltpu.PrefetchScalarGridSpec(
            num_scalar_prefetch=1,
            grid=(2 * steps,),
            in_specs=[first, last, first, last] + [there] * 4 + [once(a.shape) for a in (qkv_w, ag, ash)],
            out_specs=[once((rows // 2, width))] * 2,
            scratch_shapes=[
                pltpu.VMEM((d, 3 * cols), F32),
                pltpu.VMEM((cols, d), F32),
                pltpu.VMEM((8, 3 * cols), F32),
                pltpu.VMEM((rows, width), F32),
            ],
        ),
        out_shape=[
            jax.ShapeDtypeStruct((rows // 2, width), BF),
            jax.ShapeDtypeStruct((rows // 2, width), F32),
        ],
        compiler_params=params(32),
        cost_estimate=COST,
        name="back_weights",
    )(meta, x_own, x_other, g_own, g_other, ctx, gq, gk, gv, qkv_w, ag, ash)


def fold_kernel(bits, meta, *refs):
    if len(refs) == 6 and bits[0] is not None:
        rows = refs[0].shape[0] // 2
        ins = [r.at[pl.ds(k * rows, rows), :] for k in range(2) for r in refs[:2]]
        outs = refs[2:]
    else:
        ins, outs = refs[:4], refs[4:]
    for k, bit in enumerate(bits):
        kept, came = ins[2 * k], ins[2 * k + 1]
        if bit is None:
            outs[k][...] = (kept[...] + came[...].astype(F32)).astype(BF)
            continue
        away_ref, kept_ref = outs[2 * k], outs[2 * k + 1]
        half = kept_ref.shape[0]
        mine = bit_of(meta[2], bit)
        here = pl.ds(pl.multiple_of(mine * half, half), half)
        there = pl.ds(pl.multiple_of((1 - mine) * half, half), half)
        kept_ref[...] = kept[here, :] + came[here, :].astype(F32)
        away_ref[...] = (kept[there, :] + came[there, :].astype(F32)).astype(BF)


def spread_kernel(bits, join, meta, *refs):
    ins, outs = refs[:4], refs[4:]
    rows = ins[0].shape[0]
    for k, bit in enumerate(bits):
        out_ref, base = (outs[0], k * 2 * rows) if join else (outs[k], 0)
        mine = bit_of(meta[2], bit)
        out_ref[pl.ds(pl.multiple_of(base + mine * rows, rows), rows), :] = ins[2 * k][...]
        out_ref[pl.ds(pl.multiple_of(base + (1 - mine) * rows, rows), rows), :] = ins[2 * k + 1][...]
    if join:
        outs[1][...] = outs[0][:SMALLS, outs[0].shape[1] - LANES :].astype(F32)


def small_call(kernel, meta, ins, outs, name):
    size = sum(int(np.prod(shape)) for shape, _ in outs)
    held = pl.BlockSpec(memory_space=pltpu.VMEM)
    return pl.pallas_call(
        kernel,
        in_specs=[pl.BlockSpec(memory_space=pltpu.SMEM)] + [held] * len(ins),
        out_specs=[held] * len(outs),
        out_shape=[jax.ShapeDtypeStruct(*o) for o in outs],
        compiler_params=pltpu.CompilerParams(vmem_limit_bytes=SMALL_LIMIT),
        cost_estimate=pl.CostEstimate(flops=size, bytes_accessed=8 * size, transcendentals=0),
        name=name,
    )(meta, *ins)


def late_sum(meta, away, kept, orders, gates):
    gates = list(gates)

    def gated(step, values):
        if step < len(gates) and gates[step] is not None:
            values, gates[step] = lax.optimization_barrier((values, gates[step]))
        return values

    rows, width = kept.shape[0] // 2, kept.shape[1]
    came = swap_wide(away, 1)
    order_a, order_b = orders
    count = lax.axis_size("wide")
    if rows // (count // 2) < 16:
        parts = []
        for k, order in enumerate(orders):
            value = kept[k * rows : (k + 1) * rows] + came[k * rows : (k + 1) * rows].astype(F32)
            parts.append(gather_shares(scatter_sum(value, order[1:]), order[1:]))
        mine = jnp.concatenate(parts, 0)
        return mine, swap_wide(mine, 1), mine[:SMALLS, -LANES:].astype(F32), gates
    ins = [kept, came]
    steps = len(order_a)
    for step in range(1, steps):
        rows //= 2
        shapes = [((rows, width), BF), ((rows, width), F32)] * 2
        bits = (order_a[step], order_b[step])
        away_a, kept_a, away_b, kept_b = small_call(
            functools.partial(fold_kernel, bits), meta, ins, shapes, "fold"
        )
        ins = [kept_a, swap_wide(away_a, bits[0]), kept_b, swap_wide(away_b, bits[1])]
        ins = gated(step, ins)
    share_a, share_b = small_call(
        functools.partial(fold_kernel, (None, None)), meta, ins, [((rows, width), BF)] * 2, "fold"
    )
    for step in range(steps - 1, 0, -1):
        bits = (order_a[step], order_b[step])
        ins = [share_a, swap_wide(share_a, bits[0]), share_b, swap_wide(share_b, bits[1])]
        ins = gated(2 * steps - 1 - step, ins)
        last = step == 1
        shapes = [((4 * rows, width), BF)] if last else [((2 * rows, width), BF)] * 2
        if last:
            shapes.append(((SMALLS, LANES), F32))
        got = small_call(functools.partial(spread_kernel, bits, last), meta, ins, shapes, "spread")
        rows *= 2
        if not last:
            share_a, share_b = got
    return got[0], swap_wide(got[0], 1), got[1], gates


def unpack_late_kernel(meta, mine_ref, peer_ref, small_ref, came_ref, gqkv_ref, gout_ref, bias_ref, vec_ref, all_sc):
    d, width = gqkv_ref.shape
    third = width // 3
    quarter = mine_ref.shape[0] // 2
    core = bit_of(meta[2], 1)
    for k in range(2):
        rows = slice(k * quarter, (k + 1) * quarter)
        here = pl.multiple_of((2 * k + core) * quarter, quarter)
        there = pl.multiple_of((2 * k + 1 - core) * quarter, quarter)
        all_sc[pl.ds(here, quarter), :] = mine_ref[rows, :].astype(F32)
        all_sc[pl.ds(there, quarter), :] = peer_ref[rows, :].astype(F32)
    gout_ref[: 2 * third // 3, :] = all_sc[d:, :d]
    gout_ref[2 * third // 3 :, :third] = all_sc[d : d + third // 3, d:width]
    gout_ref[2 * third // 3 :, third:] = all_sc[d + third // 3 :, d:width]
    lane = lax.broadcasted_iota(jnp.int32, (1, LANES), 1)

    def pick(read, block, to):
        start = block % 3 * third + block // 3 * HD
        tile = read(start // LANES * LANES)
        return tile if start % LANES == to * HD else pltpu.roll(tile, HD, 1)

    count = width // LANES
    bias = jnp.concatenate([small_ref[c : c + 1, :] for c in range(count)], 1)
    bias8 = jnp.broadcast_to(bias, (8, width))
    for t in range(width // LANES):
        to = slice(t * LANES, (t + 1) * LANES)
        read = lambda c: all_sc[:d, c : c + LANES]
        gqkv_ref[:, to] = jnp.where(lane < HD, pick(read, 2 * t, 0), pick(read, 2 * t + 1, 1))
        read = lambda c: bias8[:, c : c + LANES]
        bias_ref[:, to] = jnp.where(lane < HD, pick(read, 2 * t, 0), pick(read, 2 * t + 1, 1))
    both = small_ref[...] + came_ref[...]
    per = d // LANES
    for k in range(2):
        start = count + k * per
        vec_ref[k : k + 1, :] = jnp.concatenate([both[c : c + 1, :] for c in range(start, start + per)], 1)
    vec_ref[2:, :] = jnp.zeros((vec_ref.shape[0] - 2, d), F32)


def unpack_late(meta, mine, peer, small, came, d, cols):
    width = 3 * cols
    whole = lambda shape: pl.BlockSpec(shape, lambda i, m: (0, 0))
    ins = [mine, peer, small, came]
    outs = [(d, width), (cols, d), (8, width), (8, d)]
    return pl.pallas_call(
        unpack_late_kernel,
        grid_spec=pltpu.PrefetchScalarGridSpec(
            num_scalar_prefetch=1,
            grid=(1,),
            in_specs=[whole(a.shape) for a in ins],
            out_specs=[whole(o) for o in outs],
            scratch_shapes=[pltpu.VMEM((2 * mine.shape[0], mine.shape[1]), F32)],
        ),
        out_shape=[jax.ShapeDtypeStruct(o, F32) for o in outs],
        compiler_params=params(24),
        cost_estimate=pl.CostEstimate(flops=4 * d * width, bytes_accessed=8 * d * width, transcendentals=0),
        name="unpack_late",
    )(meta, *ins)


def finish_kernel(meta, x_ref, g_ref, own_ref, came_ref, o_ref):
    normed, inverse = normalize(x_ref[...].astype(F32))
    s = own_ref[...] + came_ref[...].astype(F32)
    back_rows = inverse * (
        s
        - jnp.mean(s, axis=-1, keepdims=True)
        - normed * jnp.mean(s * normed, axis=-1, keepdims=True)
    )
    o_ref[...] = (g_ref[...].astype(F32) + back_rows).astype(BF)


def finish(meta, x, g, own, came):
    count, d = x.shape
    here = pl.BlockSpec((ROWS, d), lambda i, m: (i, 0))
    return pl.pallas_call(
        finish_kernel,
        grid_spec=pltpu.PrefetchScalarGridSpec(
            num_scalar_prefetch=1, grid=(count // ROWS,), in_specs=[here] * 4, out_specs=here
        ),
        out_shape=jax.ShapeDtypeStruct((count, d), BF),
        compiler_params=params(16),
        cost_estimate=pl.CostEstimate(flops=20 * count * d, bytes_accessed=14 * count * d, transcendentals=0),
        name="finish",
    )(meta, x, g, own, came)


def finish_out_kernel(x_ref, own_ref, came_ref, out_bias, down_bias, o_ref):
    bias = out_bias[...].astype(F32) + down_bias[...].astype(F32)
    o_ref[...] = (x_ref[...].astype(F32) + own_ref[...] + came_ref[...].astype(F32) + bias).astype(BF)


def finish_out(x, own, came, out_bias, down_bias):
    count, d = x.shape
    here = pl.BlockSpec((ROWS, d), lambda i: (i, 0))
    bias = pl.BlockSpec((1, d), lambda i: (0, 0))
    return pl.pallas_call(
        finish_out_kernel,
        grid=(count // ROWS,),
        in_specs=[here] * 3 + [bias] * 2,
        out_specs=here,
        out_shape=jax.ShapeDtypeStruct((count, d), BF),
        compiler_params=params(16),
        cost_estimate=pl.CostEstimate(flops=4 * count * d, bytes_accessed=10 * count * d, transcendentals=0),
        name="finish_out",
    )(x, own, came, out_bias, down_bias)


def regroup(w, heads):
    lead = w.shape[:-1]
    return jnp.swapaxes(w.reshape(*lead, heads, 3, HD), -3, -2).reshape(w.shape)


def wide_orders(count):
    bits = [1 << k for k in range(count.bit_length() - 1)]
    return bits, bits[:1] + bits[2:] + bits[1:2]


def swap_wide(value, bit):
    count = lax.axis_size("wide")
    return lax.ppermute(value, "wide", [(k, k ^ bit) for k in range(count)])


def scatter_sum(value, order):
    me = lax.axis_index("wide")
    for bit in order:
        half = value.shape[0] // 2
        mine = jnp.where((me & bit) == 0, 0, 1)
        away = lax.dynamic_slice_in_dim(value, (1 - mine) * half, half, 0).astype(BF)
        kept = lax.dynamic_slice_in_dim(value, mine * half, half, 0)
        value = kept.astype(F32) + swap_wide(away, bit).astype(F32)
    return value


def gather_shares(value, order):
    me = lax.axis_index("wide")
    value = value.astype(BF)
    for bit in reversed(order):
        came = swap_wide(value, bit)
        low = (me & bit) == 0
        value = jnp.concatenate([jnp.where(low, value, came), jnp.where(low, came, value)], 0)
    return value


def per_device(
    block_in,
    out_grad,
    seq_lens,
    qkv_weight,
    qkv_bias,
    out_weight,
    out_bias,
    up_weight,
    up_bias,
    down_weight,
    down_bias,
    attn_gain,
    attn_shift,
    ffn_gain,
    ffn_shift,
):
    swap = [(0, 1), (1, 0)]
    other_in = lax.ppermute(block_in, "narrow", swap)
    other_grad = lax.ppermute(out_grad, "narrow", swap)
    half = block_in.shape[0]
    group_rows = 2 * half
    heads = out_weight.shape[0] // HD
    own = lax.axis_index("narrow").astype(jnp.int32)
    long = (seq_lens[0, 0] == group_rows).astype(jnp.int32)
    row = lambda v: v.reshape(1, -1)
    order = jnp.arange(group_rows // BQ, dtype=jnp.int32)
    me = lax.axis_index("wide").astype(jnp.int32)
    meta_own = jnp.concatenate([jnp.stack([long, own, me]), order])
    meta_other = jnp.concatenate([jnp.stack([long, 1 - own, me]), order])
    table = jnp.asarray(rope_table(group_rows))
    qkv_w = regroup(qkv_weight, heads)
    weights = (
        qkv_w,
        row(regroup(qkv_bias, heads)),
        up_weight,
        row(up_bias),
        down_weight,
        out_weight,
        row(attn_gain),
        row(attn_shift),
        row(ffn_gain),
        row(ffn_shift),
    )
    qkv, gc, ffn_own, sf_own, *sums = front_own(
        meta_own, block_in, out_grad, weights, table, group_rows
    )
    qkv, ffn_other, act, slope = front_forward(meta_other, other_in, weights, table, qkv)
    gc, sf_other, early = front_backward(
        meta_other, other_in, other_grad, act, slope, weights, gc, sums
    )
    ag, ash = row(attn_gain), row(attn_shift)
    early = lax.psum(early, "wide")
    ctx, gq, gk, gv = attention(meta_own, qkv, gc, table)
    send_part, send_s = back_rows(
        meta_other, ctx, gq, gk, gv, ffn_other, sf_other, qkv_w, out_weight, ag, BF
    )
    came_s = lax.ppermute(send_s, "narrow", swap)
    came_part = lax.ppermute(send_part, "narrow", swap)
    ctx, send_s = lax.optimization_barrier((ctx, send_s))
    away, kept = back_weights(
        meta_own, block_in, other_in, out_grad, other_grad, ctx, gq, gk, gv, qkv_w, ag, ash
    )
    away, ffn_own = lax.optimization_barrier((away, ffn_own))
    own_part, own_s = back_rows(
        meta_own, ctx, gq, gk, gv, ffn_own, sf_own, qkv_w, out_weight, ag, F32
    )
    d, hidden = up_weight.shape
    in_grad = finish(meta_own, block_in, out_grad, own_s, came_s)
    block_out = finish_out(block_in, own_part, came_part, row(out_bias), row(down_bias))
    gup, gdown, early_vec = unpack_front(early, d, hidden)
    early_vec = early_vec[:3] + lax.ppermute(early_vec, "narrow", swap)[:3], early_vec[8 : 8 + hidden // d]
    gates = [None, None, own_part, came_s, (early, in_grad), (gup, gdown), (block_out, early_vec)]
    mine, peer, small, gates = late_sum(
        meta_own, away, kept, wide_orders(lax.axis_size("wide")), gates
    )
    _, _, _, _, (_, in_grad), (gup, gdown), (block_out, early_vec) = gates
    gqkv, gout, gqkv_b, late_vec = unpack_late(
        meta_own, mine, peer, small, lax.ppermute(small, "narrow", swap), d, out_weight.shape[0]
    )
    vec, gup_b = early_vec
    return (
        block_out,
        in_grad,
        gqkv,
        gqkv_b[0],
        gout,
        vec[2],
        gup,
        gup_b.reshape(-1),
        gdown,
        vec[2],
        late_vec[0],
        late_vec[1],
        vec[0],
        vec[1],
    )


def solution(mesh):
    rows = P(("wide", "narrow"), None)
    placed = (
        rows,
        rows,
        P("wide", None),
        P(None, "narrow"),
        P("narrow"),
        P("narrow", None),
        P(),
        P(None, "narrow"),
        P("narrow"),
        P("narrow", None),
        P(),
        P(),
        P(),
        P(),
        P(),
    )
    return jax.shard_map(
        per_device,
        mesh=mesh,
        in_specs=placed,
        out_specs=(
            rows,
            rows,
            P(None, "narrow"),
            P("narrow"),
            P("narrow", None),
            P(),
            P(None, "narrow"),
            P("narrow"),
            P("narrow", None),
            P(),
            P(),
            P(),
            P(),
            P(),
        ),
        check_vma=False,
    )
```

```python
import functools

import jax
import jax.numpy as jnp
import numpy as np
from jax import lax
from jax.experimental import pallas as pl
from jax.experimental.pallas import tpu as pltpu
from jax.sharding import PartitionSpec as P

HD = 64
ROT = 16
EPS = 1e-05
NEG = -1e30
SCALE = 0.125
SHORT_LEN = 512
F32 = jnp.float32
BF = jnp.bfloat16
LANES = 128
BQ = 512
BS = 256
ROWS = 512
SMALL_LIMIT = 8 << 20
COST = pl.CostEstimate(flops=1 << 20, bytes_accessed=1 << 12, transcendentals=0)


def nn(a, b):
    return lax.dot_general(a, b, (((1,), (0,)), ((), ())), preferred_element_type=F32)


def nt(a, b):
    return lax.dot_general(a, b, (((1,), (1,)), ((), ())), preferred_element_type=F32)


def tn(a, b):
    return lax.dot_general(a, b, (((0,), (0,)), ((), ())), preferred_element_type=F32)


def colsum(a):
    return jnp.sum(a, axis=0, keepdims=True)


def rope_table(rows):
    half = ROT // 2
    freq = np.float32(1.0) / np.float32(10000.0) ** (
        np.arange(half, dtype=np.float32) * np.float32(2.0) / np.float32(ROT)
    )
    angle = np.arange(rows, dtype=np.float32)[:, None] * freq.astype(np.float32)[None, :]
    table = np.zeros((rows, 2 * HD), np.float32)
    table[:, :HD] = 1.0
    table[:, :half] = table[:, half:ROT] = np.cos(angle)
    table[:, HD : HD + half] = -np.sin(angle)
    table[:, HD + half : HD + ROT] = np.sin(angle)
    return table


def rope(x, table, back):
    lane = lax.broadcasted_iota(jnp.int32, x.shape, 1)
    other = pltpu.roll(table, HD, 1)
    cosine = jnp.where(lane < HD, table, other)
    sine = jnp.where(lane < HD, other, table)
    partner = jnp.where(
        lane % HD < ROT // 2, pltpu.roll(x, LANES - ROT // 2, 1), pltpu.roll(x, ROT // 2, 1)
    )
    return x * cosine - partner * sine if back else x * cosine + partner * sine


def normalize(x):
    center = jnp.mean(x, axis=-1, keepdims=True)
    offset = x - center
    inverse = lax.rsqrt(jnp.mean(offset * offset, axis=-1, keepdims=True) + EPS)
    return offset * inverse, inverse


def once(shape):
    return pl.BlockSpec(shape, lambda i, m: (0,) * len(shape), pipeline_mode=pl.Buffered(1))


def params(mib):
    return pltpu.CompilerParams(vmem_limit_bytes=mib << 20, dimension_semantics=("arbitrary",))


EXTRA = 16
SMALLS = 32


def project(first, qkv_w, qkv_b, table, qkv_ref):
    packed = nn(first, qkv_w[...]) + qkv_b[...].astype(F32)
    third = packed.shape[1] // 3
    for c in range(0, third, LANES):
        q = rope(packed[:, c : c + LANES], table, False).astype(BF)
        qkv_ref[:, c : c + LANES] = (q.astype(F32) * SCALE).astype(BF)
        k = rope(packed[:, third + c : third + c + LANES], table, False)
        qkv_ref[:, third + c : third + c + LANES] = k.astype(BF)
    qkv_ref[:, 2 * third :] = packed[:, 2 * third :].astype(BF)


def gelu_parts(hidden):
    phi = 0.5 * (1.0 + lax.erf(hidden * np.float32(0.5**0.5)))
    density = jnp.exp(-0.5 * hidden * hidden) * np.float32(1.0 / np.sqrt(2.0 * np.pi))
    return hidden * phi, phi + hidden * density


def front_own_kernel(meta, *refs):
    (x_ref, g_ref, qkv_w, qkv_b, up_w, up_b, down_w, out_w, ag, ash, fg, fsh, tab_ref), refs = (
        refs[:13],
        refs[13:],
    )
    (qkv_ref, gc_ref, ffn_ref, s_ref, up_acc, down_acc, vec_ref, vech_ref) = refs
    normed, _ = normalize(x_ref[...].astype(F32))
    g = g_ref[...]
    first = (normed * ag[...].astype(F32) + ash[...].astype(F32)).astype(BF)
    second = (normed * fg[...].astype(F32) + fsh[...].astype(F32)).astype(BF)

    @pl.when(pl.program_id(0) == 0)
    def _():
        for ref in (up_acc, down_acc, vec_ref, vech_ref):
            ref[...] = jnp.zeros_like(ref)

    project(first, qkv_w, qkv_b, tab_ref[...], qkv_ref)
    gc_ref[...] = nt(g, out_w[...]).astype(BF)
    act, slope = gelu_parts(nn(second, up_w[...]) + up_b[...].astype(F32))
    act = act.astype(BF)
    ffn_ref[...] = nn(act, down_w[...])
    gh = (nt(g, down_w[...]) * slope).astype(BF)
    gs = nt(gh, up_w[...])
    s_ref[...] = gs * fg[...].astype(F32)
    vec_ref[0:1, :] += colsum(gs * normed)
    vec_ref[1:2, :] += colsum(gs)
    vec_ref[2:3, :] += colsum(g.astype(F32))
    vech_ref[0:1, :] += colsum(gh.astype(F32))
    up_acc[...] += tn(second, gh)
    down_acc[...] += tn(act, g)


def front_forward_kernel(meta, *refs):
    x_ref, qkv_w, qkv_b, up_w, up_b, down_w, ag, ash, fg, fsh, tab_ref, _ = refs[:12]
    qkv_ref, ffn_ref, act_ref, slope_ref = refs[12:]
    normed, _ = normalize(x_ref[...].astype(F32))
    first = (normed * ag[...].astype(F32) + ash[...].astype(F32)).astype(BF)
    second = (normed * fg[...].astype(F32) + fsh[...].astype(F32)).astype(BF)
    project(first, qkv_w, qkv_b, tab_ref[...], qkv_ref)
    act, slope = gelu_parts(nn(second, up_w[...]) + up_b[...].astype(F32))
    act = act.astype(BF)
    act_ref[...] = act
    slope_ref[...] = slope
    ffn_ref[...] = nn(act, down_w[...])


def front_backward_kernel(meta, *refs):
    x_ref, g_ref, act_ref, slope_ref, up_w, down_w, out_w, fg, fsh, _, *sums_in = refs[:14]
    gc_ref, s_ref, packed_ref, *rest = refs[14:]
    sums, befores, sems = rest[:4], rest[4:8], rest[8]
    up_acc, down_acc, vec_ref, vech_ref = sums
    i = pl.program_id(0)
    copies = [
        pltpu.make_async_copy(src, dst, sems.at[k])
        for k, (src, dst) in enumerate(zip(sums_in, befores))
    ]

    @pl.when(i == 0)
    def _():
        for copy in copies:
            copy.start()
        for ref in sums:
            ref[...] = jnp.zeros_like(ref)

    normed, _ = normalize(x_ref[...].astype(F32))
    second = (normed * fg[...].astype(F32) + fsh[...].astype(F32)).astype(BF)
    g = g_ref[...]
    gc_ref[...] = nt(g, out_w[...]).astype(BF)
    gh = (nt(g, down_w[...]) * slope_ref[...]).astype(BF)
    gs = nt(gh, up_w[...])
    s_ref[...] = gs * fg[...].astype(F32)
    vec_ref[0:1, :] += colsum(gs * normed)
    vec_ref[1:2, :] += colsum(gs)
    vech_ref[0:1, :] += colsum(gh.astype(F32))
    up_acc[...] += tn(second, gh)
    down_acc[...] += tn(act_ref[...], g)

    @pl.when(i == pl.num_programs(0) - 1)
    def _():
        for copy in copies:
            copy.wait()
        up_in, down_in, vec_in, vech_in = befores
        d = up_acc.shape[0]
        hidden_rows = down_acc.shape[0]
        spare = [vec_ref[...] + vec_in[...]]
        for c in range(0, hidden_rows, d):
            packed_ref[c : c + d, :] = (up_acc[:, c : c + d] + up_in[:, c : c + d]).astype(BF)
            spare.append(vech_ref[0:1, c : c + d] + vech_in[0:1, c : c + d])
        packed_ref[hidden_rows : 2 * hidden_rows, :] = (down_acc[...] + down_in[...]).astype(BF)
        pad = EXTRA - vec_ref.shape[0] - (len(spare) - 1)
        spare.append(jnp.zeros((pad, d), F32))
        packed_ref[2 * hidden_rows :, :] = jnp.concatenate(spare, 0).astype(BF)


def front_call(kernel, name, mib, meta, x, ins, outs, aliases, flops, scratch=()):
    count = x.shape[0]
    steps = count // ROWS
    per_short = SHORT_LEN // ROWS

    def spec(shape, kind):
        if kind == "here":
            return pl.BlockSpec((ROWS, shape[1]), lambda i, m: (i, 0))
        if kind == "there":
            return pl.BlockSpec((ROWS, shape[1]), lambda i, m: (m[1] * steps + i, 0))
        if kind == "table":
            block = lambda i, m: m[1] * steps + i
            return pl.BlockSpec(
                (ROWS, shape[1]),
                lambda i, m: (jnp.where(m[0] == 1, block(i, m), lax.rem(block(i, m), per_short)), 0),
            )
        return pl.BlockSpec(memory_space=pl.ANY) if kind == "any" else once(shape)

    return pl.pallas_call(
        kernel,
        grid_spec=pltpu.PrefetchScalarGridSpec(
            num_scalar_prefetch=1,
            grid=(steps,),
            in_specs=[spec(a.shape, kind) for a, kind in ins],
            out_specs=[spec(shape, kind) for (shape, _), kind in outs],
            scratch_shapes=list(scratch),
        ),
        out_shape=[jax.ShapeDtypeStruct(*o) for o, _ in outs],
        input_output_aliases=aliases,
        compiler_params=params(mib),
        cost_estimate=pl.CostEstimate(
            flops=flops, bytes_accessed=16 << 20, transcendentals=0
        ),
        name=name,
    )(meta, *[a for a, _ in ins])


def sums_of(d, hidden):
    return [(d, hidden), (hidden, d), (8, d), (8, hidden)]


def front_own(meta, x, g, weights, table, group_rows):
    (count, d), cols, hidden = x.shape, weights[5].shape[0], weights[2].shape[1]
    return front_call(
        front_own_kernel,
        "front_own",
        44,
        meta,
        x,
        [(x, "here"), (g, "here"), *[(w, "once") for w in weights], (table, "table")],
        [
            (((group_rows, 3 * cols), BF), "there"),
            (((group_rows, cols), BF), "there"),
            (((count, d), F32), "here"),
            (((count, d), F32), "here"),
            *[((shape, F32), "once") for shape in sums_of(d, hidden)],
        ],
        {},
        2 * count * d * (6 * hidden + 4 * cols),
    )


def front_forward(meta, x, weights, table, qkv):
    qkv_w, qkv_b, up_w, up_b, down_w, out_w, ag, ash, fg, fsh = weights
    (count, d), hidden = x.shape, up_w.shape[1]
    once_in = [(w, "once") for w in (qkv_w, qkv_b, up_w, up_b, down_w, ag, ash, fg, fsh)]
    return front_call(
        front_forward_kernel,
        "front_forward",
        32,
        meta,
        x,
        [(x, "here"), *once_in, (table, "table"), (qkv, "any")],
        [
            ((qkv.shape, BF), "there"),
            (((count, d), F32), "here"),
            (((count, hidden), BF), "here"),
            (((count, hidden), F32), "here"),
        ],
        {12: 0},
        2 * count * d * (2 * hidden + qkv.shape[1]),
    )


def front_backward(meta, x, g, act, slope, weights, gc, sums):
    _, _, up_w, _, down_w, out_w, _, _, fg, fsh = weights
    (count, d), hidden = x.shape, up_w.shape[1]
    return front_call(
        front_backward_kernel,
        "front_backward",
        44,
        meta,
        x,
        [
            *[(a, "here") for a in (x, g, act, slope)],
            *[(w, "once") for w in (up_w, down_w, out_w, fg, fsh)],
            (gc, "any"),
            *[(a, "any") for a in sums],
        ],
        [
            ((gc.shape, BF), "there"),
            (((count, d), F32), "here"),
            (((2 * hidden + EXTRA, d), BF), "once"),
        ],
        {10: 0},
        2 * count * d * (4 * hidden + out_w.shape[0]),
        [pltpu.VMEM(shape, F32) for shape in sums_of(d, hidden)] * 2 + [pltpu.SemaphoreType.DMA((4,))],
    )


def unpack_front(packed, d, hidden):
    assert hidden == 2 * d
    steps = 6
    part = d // steps
    chunk = hidden // steps

    def kernel(p0, p1, p2, e_ref, up_ref, down_ref, vec_ref):
        up_ref[:, :d] = p0[...].astype(F32)
        up_ref[:, d:] = p1[...].astype(F32)
        down_ref[...] = p2[...].astype(F32)
        vec_ref[...] = e_ref[...].astype(F32)

    return pl.pallas_call(
        kernel,
        grid=(steps,),
        in_specs=[
            pl.BlockSpec((part, d), lambda i: (i, 0)),
            pl.BlockSpec((part, d), lambda i: (steps + i, 0)),
            pl.BlockSpec((chunk, d), lambda i: (steps + i, 0)),
            pl.BlockSpec((EXTRA, d), lambda i: (2 * hidden // EXTRA, 0)),
        ],
        out_specs=[
            pl.BlockSpec((part, hidden), lambda i: (i, 0)),
            pl.BlockSpec((chunk, d), lambda i: (i, 0)),
            pl.BlockSpec((EXTRA, d), lambda i: (0, 0)),
        ],
        out_shape=[
            jax.ShapeDtypeStruct((d, hidden), F32),
            jax.ShapeDtypeStruct((hidden, d), F32),
            jax.ShapeDtypeStruct((EXTRA, d), F32),
        ],
        compiler_params=params(16),
        cost_estimate=pl.CostEstimate(
            flops=2 * d * hidden, bytes_accessed=12 * d * hidden, transcendentals=0
        ),
        name="unpack_front",
    )(packed, packed, packed, packed)


def attention_kernel(meta, q_ref, k_ref, v_ref, do_ref, tab_ref, *refs):
    ctx_ref, dq_ref, dk_ref, dv_ref, s_sc, e_sc, ds_sc, kt_sc, vt_sc, dk_sc, dv_sc, *parts = refs
    qw_sc, qt_sc, gw_sc, gt_sc, acc_sc = parts
    i = pl.program_id(1)
    qb = meta[3 + i]
    long = meta[0]
    rows = k_ref.shape[0]
    half_cols = 2 * BS
    ext = HD + 16

    @pl.when(i == 0)
    def _():
        dk_sc[...] = jnp.zeros_like(dk_sc)
        dv_sc[...] = jnp.zeros_like(dv_sc)
        kt_sc[...] = k_ref[...].T
        ones = jnp.ones((16, rows), BF)
        vt = v_ref[...].T
        for h in range(2):
            vt_sc[h * ext : h * ext + HD, :] = vt[h * HD : (h + 1) * HD]
            vt_sc[h * ext + HD : (h + 1) * ext, :] = ones

    first_block = jnp.where(long == 1, 0, qb)
    zeros_t = jnp.zeros((HD, BS), BF)
    zeros = jnp.zeros((BS, LANES), BF)
    lane = lax.broadcasted_iota(jnp.int32, (BS, LANES), 1)

    def wide(t):
        return jnp.concatenate(
            [
                jnp.concatenate(pair, 0)
                for a in range(0, BQ, BS)
                for pair in ([t[:HD, a : a + BS], zeros_t], [zeros_t, t[HD:, a : a + BS]])
            ],
            1,
        )

    def tall(t):
        return jnp.concatenate(
            [
                block
                for a in range(0, BQ, BS)
                for block in (
                    jnp.where(lane < HD, t[a : a + BS], zeros),
                    jnp.where(lane < HD, zeros, t[a : a + BS]),
                )
            ],
            0,
        )

    def keys(b, tile=0, count=2):
        return pl.ds(pl.multiple_of(b * BQ + tile * BS, BS), count * BS)

    queries = q_ref[...]
    qw_sc[...], qt_sc[...] = wide(queries.T), tall(queries)
    key_index = lax.broadcasted_iota(jnp.int32, (BS, half_cols), 0)
    query_index = lax.broadcasted_iota(jnp.int32, (BS, half_cols), 1) % BS
    causal = key_index <= query_index
    fold = lambda s: jnp.max(s.reshape(BS // 8, 8, s.shape[1]), axis=0)

    s = nn(k_ref[keys(qb, 0, 1), :], qw_sc[...])
    s = jnp.concatenate([jnp.where(causal, s[:, :half_cols], NEG), s[:, half_cols:]], 1)
    s_sc[keys(qb, 0, 1), :] = s
    low = jnp.where(causal, nn(k_ref[keys(qb, 1, 1), :], qw_sc[:, half_cols:]), NEG)
    s_sc[keys(qb, 1, 1), half_cols:] = low
    top = fold(s)
    top = jnp.concatenate([top[:, :half_cols], jnp.maximum(top[:, half_cols:], fold(low))], 1)

    def score(b, top):
        for t in range(2):
            s = nn(k_ref[keys(b, t, 1), :], qw_sc[...])
            s_sc[keys(b, t, 1), :] = s
            top = jnp.maximum(top, fold(s))
        return top

    top = jnp.max(lax.fori_loop(first_block, qb, score, top), axis=0, keepdims=True)

    def exponent(rows, lo):
        e = jnp.exp(s_sc[rows, lo:] - top[:, lo:]).astype(BF)
        e_sc[rows, lo:] = e
        return e

    sides = [(a, h, a * half_cols + h * BS) for a in range(2) for h in range(2)]
    exponent(keys(qb, 0, 1), 0)
    exponent(keys(qb, 1, 1), half_cols)
    for a, h, c in sides:
        rows_of = keys(qb, 0, 1 + a)
        acc_sc[:, c : c + BS] = nn(vt_sc[h * ext : (h + 1) * ext, rows_of], e_sc[rows_of, c : c + BS])

    def gather(b, _):
        e = exponent(keys(b), 0)
        for _, h, c in sides:
            acc_sc[:, c : c + BS] += nn(vt_sc[h * ext : (h + 1) * ext, keys(b)], e[:, c : c + BS])
        return 0

    lax.fori_loop(first_block, qb, gather, 0)
    grad_t = do_ref[...].astype(F32).T
    ctx_parts, grad_parts, weighted = [[], []], [[], []], []
    for a, h, c in sides:
        over_total = 1.0 / acc_sc[HD : HD + 1, c : c + BS]
        ctx = acc_sc[:HD, c : c + BS] * over_total
        grad = (grad_t[h * HD : (h + 1) * HD, a * BS : (a + 1) * BS] * over_total).astype(BF)
        weighted.append(colsum(ctx * grad.astype(F32)))
        ctx_parts[a].append(ctx)
        grad_parts[a].append(grad)
    full = lambda parts: jnp.concatenate([jnp.concatenate(part, 0) for part in parts], 1)
    ctx_ref[...] = full(ctx_parts).T.astype(BF)
    grad_full = full(grad_parts)
    gw_sc[...], gt_sc[...] = wide(grad_full), tall(grad_full.T)
    weighted = jnp.concatenate(weighted, 1)

    def backward(rows, lo):
        e = e_sc[rows, lo:]
        gp = nn(v_ref[rows, :], gw_sc[:, lo:])
        ds = (e.astype(F32) * (gp - weighted[:, lo:])).astype(BF)
        ds_sc[rows, lo:] = ds
        dv_sc[rows, :] += nn(e, gt_sc[lo:, :])
        dk_sc[rows, :] += nn(ds, qt_sc[lo:, :])

    backward(keys(qb, 0, 1), 0)
    backward(keys(qb, 1, 1), half_cols)
    for a, h, c in sides:
        rows_of = keys(qb, 0, 1 + a)
        acc_sc[:HD, c : c + BS] = nn(kt_sc[h * HD : (h + 1) * HD, rows_of], ds_sc[rows_of, c : c + BS])

    def before(b, _):
        for t in range(2):
            backward(keys(b, t, 1), 0)
        for _, h, c in sides:
            acc_sc[:HD, c : c + BS] += nn(kt_sc[h * HD : (h + 1) * HD, keys(b)], ds_sc[keys(b), c : c + BS])
        return 0

    lax.fori_loop(first_block, qb, before, 0)
    dq = jnp.concatenate(
        [
            jnp.concatenate([acc_sc[:HD, c : c + BS] for b, _, c in sides if b == a], 0)
            for a in range(2)
        ],
        1,
    )
    at = pl.multiple_of(jnp.where(long == 1, qb, 0) * BQ, BQ)
    dq_ref[...] = rope(dq.T * SCALE, tab_ref[pl.ds(at, BQ), :], True).astype(BF)

    @pl.when(i == pl.num_programs(1) - 1)
    def _():
        dv_ref[...] = dv_sc[...].astype(BF)

        def finish(b, _):
            block = pl.ds(pl.multiple_of(b * BQ, BQ), BQ)
            at = pl.multiple_of(jnp.where(long == 1, b, 0) * BQ, BQ)
            dk_ref[block, :] = rope(dk_sc[block, :], tab_ref[pl.ds(at, BQ), :], True).astype(BF)
            return 0

        lax.fori_loop(0, rows // BQ, finish, 0)


def attention(meta, qkv, grad_ctx, table):
    rows, cols = grad_ctx.shape
    pairs, blocks = cols // LANES, rows // BQ
    at_query = lambda p, i, m: (m[3 + i], p)
    whole = lambda part: lambda p, i, m: (0, part * pairs + p)
    kept = jax.ShapeDtypeStruct((rows, cols), BF)
    return pl.pallas_call(
        attention_kernel,
        grid_spec=pltpu.PrefetchScalarGridSpec(
            num_scalar_prefetch=1,
            grid=(pairs, blocks),
            in_specs=[
                pl.BlockSpec((BQ, LANES), at_query),
                pl.BlockSpec((rows, LANES), whole(1)),
                pl.BlockSpec((rows, LANES), whole(2)),
                pl.BlockSpec((BQ, LANES), at_query),
                pl.BlockSpec((rows, LANES), lambda p, i, m: (0, 0), pipeline_mode=pl.Buffered(1)),
            ],
            out_specs=[
                pl.BlockSpec((BQ, LANES), at_query),
                pl.BlockSpec((BQ, LANES), at_query),
                pl.BlockSpec((rows, LANES), whole(0)),
                pl.BlockSpec((rows, LANES), whole(0)),
            ],
            scratch_shapes=[
                pltpu.VMEM((rows, 2 * BQ), F32),
                pltpu.VMEM((rows, 2 * BQ), BF),
                pltpu.VMEM((rows, 2 * BQ), BF),
                pltpu.VMEM((LANES, rows), BF),
                pltpu.VMEM((2 * (HD + 16), rows), BF),
                pltpu.VMEM((rows, LANES), F32),
                pltpu.VMEM((rows, LANES), F32),
                *[pltpu.VMEM((LANES, 2 * BQ), BF), pltpu.VMEM((2 * BQ, LANES), BF)] * 2,
                pltpu.VMEM((HD + 16, 2 * BQ), F32),
            ],
        ),
        out_shape=[kept] * 4,
        compiler_params=pltpu.CompilerParams(
            vmem_limit_bytes=32 << 20, dimension_semantics=("arbitrary", "arbitrary")
        ),
        cost_estimate=COST,
        name="attention",
    )(meta, qkv, qkv, qkv, grad_ctx, table)


def back_rows_kernel(meta, ctx_ref, gq_ref, gk_ref, gv_ref, ffn_ref, sf_ref, qkv_w, out_w, ag, part_ref, s_ref):
    part_ref[...] = (nn(ctx_ref[...], out_w[...]) + ffn_ref[...]).astype(part_ref.dtype)
    packed = jnp.concatenate([gq_ref[...], gk_ref[...], gv_ref[...]], axis=1)
    s_ref[...] = (nt(packed, qkv_w[...]) * ag[...].astype(F32) + sf_ref[...]).astype(s_ref.dtype)


def back_rows(meta, ctx, gq, gk, gv, ffn, sf, qkv_w, out_w, ag, kind):
    count, d = ffn.shape
    steps = count // ROWS
    cols = out_w.shape[0]
    here = pl.BlockSpec((ROWS, d), lambda i, m: (i, 0))
    there = pl.BlockSpec((ROWS, cols), lambda i, m: (m[1] * steps + i, 0))
    return pl.pallas_call(
        back_rows_kernel,
        grid_spec=pltpu.PrefetchScalarGridSpec(
            num_scalar_prefetch=1,
            grid=(steps,),
            in_specs=[there] * 4 + [here] * 2 + [once(qkv_w.shape), once(out_w.shape), once(ag.shape)],
            out_specs=[here, here],
        ),
        out_shape=[jax.ShapeDtypeStruct((count, d), kind)] * 2,
        compiler_params=params(24),
        cost_estimate=COST,
        name="back_rows",
    )(meta, ctx, gq, gk, gv, ffn, sf, qkv_w, out_w, ag)


def bit_of(me, bit):
    return lax.rem(lax.div(me, bit), 2)


def back_weights_kernel(meta, *refs):
    (x0_ref, x1_ref, g0_ref, g1_ref, ctx_ref, gq_ref, gk_ref, gv_ref, w_ref, ag, ash), refs = refs[:11], refs[11:]
    away_ref, kept_ref, qkv_acc, out_acc, bias_acc, all_sc = refs
    i = pl.program_id(0)
    steps = pl.num_programs(0)

    @pl.when(i == 0)
    def _():
        qkv_acc[...] = jnp.zeros_like(qkv_acc)
        out_acc[...] = jnp.zeros_like(out_acc)
        bias_acc[...] = jnp.zeros_like(bias_acc)

    own = i < steps // 2
    x = jnp.where(own, x0_ref[...].astype(F32), x1_ref[...].astype(F32))
    g = jnp.where(own, g0_ref[...], g1_ref[...])
    normed, _ = normalize(x)
    first = (normed * ag[...].astype(F32) + ash[...].astype(F32)).astype(BF)
    packed = jnp.concatenate([gq_ref[...], gk_ref[...], gv_ref[...]], axis=1)
    bias_acc[0:1, :] += colsum(packed.astype(F32))
    qkv_acc[...] += tn(first, packed)
    out_acc[...] += tn(ctx_ref[...], g)

    @pl.when(i == steps - 1)
    def _():
        d, width = qkv_acc.shape
        third = width // 3
        all_sc[:d, :width] = qkv_acc[...]
        all_sc[d:, :d] = out_acc[: 2 * third // 3, :]
        all_sc[d : d + third // 3, d:width] = out_acc[2 * third // 3 :, :third]
        all_sc[d + third // 3 :, d:width] = out_acc[2 * third // 3 :, third:]
        all_sc[:, width:] = jnp.zeros((all_sc.shape[0], LANES), F32)
        left = jnp.zeros((d, LANES), F32)
        right = jnp.zeros((d, LANES), F32)
        for c in range(0, width, LANES):
            w = w_ref[:, c : c + LANES].astype(F32)
            left += w * qkv_acc[:, c : c + LANES]
            right += w * bias_acc[0:1, c : c + LANES]
        shift_sum = colsum(right.T)
        gain_sum = (colsum(left.T) - ash[...].astype(F32) * shift_sum) / ag[...].astype(F32)
        quarter = all_sc.shape[0] // 4
        row = 0
        for vector in (bias_acc[0:1, :], gain_sum, shift_sum):
            for c in range(0, vector.shape[1], LANES):
                for base in (0, quarter):
                    all_sc[base + row : base + row + 1, width:] = vector[:, c : c + LANES]
                row += 1
        core = bit_of(meta[2], 1)
        for k in range(2):
            here = pl.multiple_of((2 * k + core) * quarter, quarter)
            there = pl.multiple_of((2 * k + 1 - core) * quarter, quarter)
            rows = slice(k * quarter, (k + 1) * quarter)
            kept_ref[rows, :] = all_sc[pl.ds(here, quarter), :]
            away_ref[rows, :] = all_sc[pl.ds(there, quarter), :].astype(BF)


def back_weights(meta, x_own, x_other, g_own, g_other, ctx, gq, gk, gv, qkv_w, ag, ash):
    half, d = x_own.shape
    steps = half // ROWS
    cols = ctx.shape[1]
    assert d == 2 * cols and cols % 3 == 0
    first = pl.BlockSpec((ROWS, d), lambda i, m: (jnp.minimum(i, steps - 1), 0))
    last = pl.BlockSpec((ROWS, d), lambda i, m: (jnp.maximum(i - steps, 0), 0))
    there = pl.BlockSpec(
        (ROWS, cols), lambda i, m: (lax.rem(m[1] * steps + i, 2 * steps), 0)
    )
    rows, width = d + 2 * cols // 3, 3 * cols + LANES
    return pl.pallas_call(
        back_weights_kernel,
        grid_spec=pltpu.PrefetchScalarGridSpec(
            num_scalar_prefetch=1,
            grid=(2 * steps,),
            in_specs=[first, last, first, last] + [there] * 4 + [once(a.shape) for a in (qkv_w, ag, ash)],
            out_specs=[once((rows // 2, width))] * 2,
            scratch_shapes=[
                pltpu.VMEM((d, 3 * cols), F32),
                pltpu.VMEM((cols, d), F32),
                pltpu.VMEM((8, 3 * cols), F32),
                pltpu.VMEM((rows, width), F32),
            ],
        ),
        out_shape=[
            jax.ShapeDtypeStruct((rows // 2, width), BF),
            jax.ShapeDtypeStruct((rows // 2, width), F32),
        ],
        compiler_params=params(32),
        cost_estimate=COST,
        name="back_weights",
    )(meta, x_own, x_other, g_own, g_other, ctx, gq, gk, gv, qkv_w, ag, ash)


def fold_kernel(bits, meta, *refs):
    if len(refs) == 6 and bits[0] is not None:
        rows = refs[0].shape[0] // 2
        ins = [r.at[pl.ds(k * rows, rows), :] for k in range(2) for r in refs[:2]]
        outs = refs[2:]
    else:
        ins, outs = refs[:4], refs[4:]
    for k, bit in enumerate(bits):
        kept, came = ins[2 * k], ins[2 * k + 1]
        if bit is None:
            outs[k][...] = (kept[...] + came[...].astype(F32)).astype(BF)
            continue
        away_ref, kept_ref = outs[2 * k], outs[2 * k + 1]
        half = kept_ref.shape[0]
        mine = bit_of(meta[2], bit)
        here = pl.ds(pl.multiple_of(mine * half, half), half)
        there = pl.ds(pl.multiple_of((1 - mine) * half, half), half)
        kept_ref[...] = kept[here, :] + came[here, :].astype(F32)
        away_ref[...] = (kept[there, :] + came[there, :].astype(F32)).astype(BF)


def spread_kernel(bits, join, meta, *refs):
    ins, outs = refs[:4], refs[4:]
    rows = ins[0].shape[0]
    for k, bit in enumerate(bits):
        out_ref, base = (outs[0], k * 2 * rows) if join else (outs[k], 0)
        mine = bit_of(meta[2], bit)
        out_ref[pl.ds(pl.multiple_of(base + mine * rows, rows), rows), :] = ins[2 * k][...]
        out_ref[pl.ds(pl.multiple_of(base + (1 - mine) * rows, rows), rows), :] = ins[2 * k + 1][...]
    if join:
        outs[1][...] = outs[0][:SMALLS, outs[0].shape[1] - LANES :].astype(F32)


def small_call(kernel, meta, ins, outs, name):
    size = sum(int(np.prod(shape)) for shape, _ in outs)
    held = pl.BlockSpec(memory_space=pltpu.VMEM)
    return pl.pallas_call(
        kernel,
        in_specs=[pl.BlockSpec(memory_space=pltpu.SMEM)] + [held] * len(ins),
        out_specs=[held] * len(outs),
        out_shape=[jax.ShapeDtypeStruct(*o) for o in outs],
        compiler_params=pltpu.CompilerParams(vmem_limit_bytes=SMALL_LIMIT),
        cost_estimate=pl.CostEstimate(flops=size, bytes_accessed=8 * size, transcendentals=0),
        name=name,
    )(meta, *ins)


def late_sum(meta, away, kept, orders, gates):
    gates = list(gates)

    def gated(step, values):
        if step < len(gates) and gates[step] is not None:
            values, gates[step] = lax.optimization_barrier((values, gates[step]))
        return values

    rows, width = kept.shape[0] // 2, kept.shape[1]
    came = swap_wide(away, 1)
    order_a, order_b = orders
    count = lax.axis_size("wide")
    if rows // (count // 2) < 16:
        parts = []
        for k, order in enumerate(orders):
            value = kept[k * rows : (k + 1) * rows] + came[k * rows : (k + 1) * rows].astype(F32)
            parts.append(gather_shares(scatter_sum(value, order[1:]), order[1:]))
        mine = jnp.concatenate(parts, 0)
        return mine, swap_wide(mine, 1), mine[:SMALLS, -LANES:].astype(F32), gates
    ins = [kept, came]
    steps = len(order_a)
    for step in range(1, steps):
        rows //= 2
        shapes = [((rows, width), BF), ((rows, width), F32)] * 2
        bits = (order_a[step], order_b[step])
        away_a, kept_a, away_b, kept_b = small_call(
            functools.partial(fold_kernel, bits), meta, ins, shapes, "fold"
        )
        ins = [kept_a, swap_wide(away_a, bits[0]), kept_b, swap_wide(away_b, bits[1])]
        ins = gated(step, ins)
    share_a, share_b = small_call(
        functools.partial(fold_kernel, (None, None)), meta, ins, [((rows, width), BF)] * 2, "fold"
    )
    for step in range(steps - 1, 0, -1):
        bits = (order_a[step], order_b[step])
        ins = [share_a, swap_wide(share_a, bits[0]), share_b, swap_wide(share_b, bits[1])]
        ins = gated(2 * steps - 1 - step, ins)
        last = step == 1
        shapes = [((4 * rows, width), BF)] if last else [((2 * rows, width), BF)] * 2
        if last:
            shapes.append(((SMALLS, LANES), F32))
        got = small_call(functools.partial(spread_kernel, bits, last), meta, ins, shapes, "spread")
        rows *= 2
        if not last:
            share_a, share_b = got
    return got[0], swap_wide(got[0], 1), got[1], gates


def unpack_late_kernel(meta, mine_ref, peer_ref, small_ref, came_ref, gqkv_ref, gout_ref, bias_ref, vec_ref, all_sc):
    d, width = gqkv_ref.shape
    third = width // 3
    quarter = mine_ref.shape[0] // 2
    core = bit_of(meta[2], 1)
    for k in range(2):
        rows = slice(k * quarter, (k + 1) * quarter)
        here = pl.multiple_of((2 * k + core) * quarter, quarter)
        there = pl.multiple_of((2 * k + 1 - core) * quarter, quarter)
        all_sc[pl.ds(here, quarter), :] = mine_ref[rows, :].astype(F32)
        all_sc[pl.ds(there, quarter), :] = peer_ref[rows, :].astype(F32)
    gout_ref[: 2 * third // 3, :] = all_sc[d:, :d]
    gout_ref[2 * third // 3 :, :third] = all_sc[d : d + third // 3, d:width]
    gout_ref[2 * third // 3 :, third:] = all_sc[d + third // 3 :, d:width]
    lane = lax.broadcasted_iota(jnp.int32, (1, LANES), 1)

    def pick(read, block, to):
        start = block % 3 * third + block // 3 * HD
        tile = read(start // LANES * LANES)
        return tile if start % LANES == to * HD else pltpu.roll(tile, HD, 1)

    count = width // LANES
    bias = jnp.concatenate([small_ref[c : c + 1, :] for c in range(count)], 1)
    bias8 = jnp.broadcast_to(bias, (8, width))
    for t in range(width // LANES):
        to = slice(t * LANES, (t + 1) * LANES)
        read = lambda c: all_sc[:d, c : c + LANES]
        gqkv_ref[:, to] = jnp.where(lane < HD, pick(read, 2 * t, 0), pick(read, 2 * t + 1, 1))
        read = lambda c: bias8[:, c : c + LANES]
        bias_ref[:, to] = jnp.where(lane < HD, pick(read, 2 * t, 0), pick(read, 2 * t + 1, 1))
    both = small_ref[...] + came_ref[...]
    per = d // LANES
    for k in range(2):
        start = count + k * per
        vec_ref[k : k + 1, :] = jnp.concatenate([both[c : c + 1, :] for c in range(start, start + per)], 1)
    vec_ref[2:, :] = jnp.zeros((vec_ref.shape[0] - 2, d), F32)


def unpack_late(meta, mine, peer, small, came, d, cols):
    width = 3 * cols
    whole = lambda shape: pl.BlockSpec(shape, lambda i, m: (0, 0))
    ins = [mine, peer, small, came]
    outs = [(d, width), (cols, d), (8, width), (8, d)]
    return pl.pallas_call(
        unpack_late_kernel,
        grid_spec=pltpu.PrefetchScalarGridSpec(
            num_scalar_prefetch=1,
            grid=(1,),
            in_specs=[whole(a.shape) for a in ins],
            out_specs=[whole(o) for o in outs],
            scratch_shapes=[pltpu.VMEM((2 * mine.shape[0], mine.shape[1]), F32)],
        ),
        out_shape=[jax.ShapeDtypeStruct(o, F32) for o in outs],
        compiler_params=params(24),
        cost_estimate=pl.CostEstimate(flops=4 * d * width, bytes_accessed=8 * d * width, transcendentals=0),
        name="unpack_late",
    )(meta, *ins)


def finish_kernel(meta, x_ref, g_ref, own_ref, came_ref, o_ref):
    normed, inverse = normalize(x_ref[...].astype(F32))
    s = own_ref[...] + came_ref[...].astype(F32)
    back_rows = inverse * (
        s
        - jnp.mean(s, axis=-1, keepdims=True)
        - normed * jnp.mean(s * normed, axis=-1, keepdims=True)
    )
    o_ref[...] = (g_ref[...].astype(F32) + back_rows).astype(BF)


def finish(meta, x, g, own, came):
    count, d = x.shape
    here = pl.BlockSpec((ROWS, d), lambda i, m: (i, 0))
    return pl.pallas_call(
        finish_kernel,
        grid_spec=pltpu.PrefetchScalarGridSpec(
            num_scalar_prefetch=1, grid=(count // ROWS,), in_specs=[here] * 4, out_specs=here
        ),
        out_shape=jax.ShapeDtypeStruct((count, d), BF),
        compiler_params=params(16),
        cost_estimate=pl.CostEstimate(flops=20 * count * d, bytes_accessed=14 * count * d, transcendentals=0),
        name="finish",
    )(meta, x, g, own, came)


def finish_out_kernel(x_ref, own_ref, came_ref, out_bias, down_bias, o_ref):
    bias = out_bias[...].astype(F32) + down_bias[...].astype(F32)
    o_ref[...] = (x_ref[...].astype(F32) + own_ref[...] + came_ref[...].astype(F32) + bias).astype(BF)


def finish_out(x, own, came, out_bias, down_bias):
    count, d = x.shape
    here = pl.BlockSpec((ROWS, d), lambda i: (i, 0))
    bias = pl.BlockSpec((1, d), lambda i: (0, 0))
    return pl.pallas_call(
        finish_out_kernel,
        grid=(count // ROWS,),
        in_specs=[here] * 3 + [bias] * 2,
        out_specs=here,
        out_shape=jax.ShapeDtypeStruct((count, d), BF),
        compiler_params=params(16),
        cost_estimate=pl.CostEstimate(flops=4 * count * d, bytes_accessed=10 * count * d, transcendentals=0),
        name="finish_out",
    )(x, own, came, out_bias, down_bias)


def regroup(w, heads):
    lead = w.shape[:-1]
    return jnp.swapaxes(w.reshape(*lead, heads, 3, HD), -3, -2).reshape(w.shape)


def wide_orders(count):
    bits = [1 << k for k in range(count.bit_length() - 1)]
    return bits, bits[:1] + bits[2:] + bits[1:2]


def swap_wide(value, bit):
    count = lax.axis_size("wide")
    return lax.ppermute(value, "wide", [(k, k ^ bit) for k in range(count)])


def scatter_sum(value, order):
    me = lax.axis_index("wide")
    for bit in order:
        half = value.shape[0] // 2
        mine = jnp.where((me & bit) == 0, 0, 1)
        away = lax.dynamic_slice_in_dim(value, (1 - mine) * half, half, 0).astype(BF)
        kept = lax.dynamic_slice_in_dim(value, mine * half, half, 0)
        value = kept.astype(F32) + swap_wide(away, bit).astype(F32)
    return value


def gather_shares(value, order):
    me = lax.axis_index("wide")
    value = value.astype(BF)
    for bit in reversed(order):
        came = swap_wide(value, bit)
        low = (me & bit) == 0
        value = jnp.concatenate([jnp.where(low, value, came), jnp.where(low, came, value)], 0)
    return value


def per_device(
    block_in,
    out_grad,
    seq_lens,
    qkv_weight,
    qkv_bias,
    out_weight,
    out_bias,
    up_weight,
    up_bias,
    down_weight,
    down_bias,
    attn_gain,
    attn_shift,
    ffn_gain,
    ffn_shift,
):
    swap = [(0, 1), (1, 0)]
    other_in = lax.ppermute(block_in, "narrow", swap)
    other_grad = lax.ppermute(out_grad, "narrow", swap)
    half = block_in.shape[0]
    group_rows = 2 * half
    heads = out_weight.shape[0] // HD
    own = lax.axis_index("narrow").astype(jnp.int32)
    long = (seq_lens[0, 0] == group_rows).astype(jnp.int32)
    row = lambda v: v.reshape(1, -1)
    order = jnp.arange(group_rows // BQ, dtype=jnp.int32)
    me = lax.axis_index("wide").astype(jnp.int32)
    meta_own = jnp.concatenate([jnp.stack([long, own, me]), order])
    meta_other = jnp.concatenate([jnp.stack([long, 1 - own, me]), order])
    table = jnp.asarray(rope_table(group_rows))
    qkv_w = regroup(qkv_weight, heads)
    weights = (
        qkv_w,
        row(regroup(qkv_bias, heads)),
        up_weight,
        row(up_bias),
        down_weight,
        out_weight,
        row(attn_gain),
        row(attn_shift),
        row(ffn_gain),
        row(ffn_shift),
    )
    qkv, gc, ffn_own, sf_own, *sums = front_own(
        meta_own, block_in, out_grad, weights, table, group_rows
    )
    qkv, ffn_other, act, slope = front_forward(meta_other, other_in, weights, table, qkv)
    gc, sf_other, early = front_backward(
        meta_other, other_in, other_grad, act, slope, weights, gc, sums
    )
    ag, ash = row(attn_gain), row(attn_shift)
    early = lax.psum(early, "wide")
    ctx, gq, gk, gv = attention(meta_own, qkv, gc, table)
    send_part, send_s = back_rows(
        meta_other, ctx, gq, gk, gv, ffn_other, sf_other, qkv_w, out_weight, ag, BF
    )
    came_s = lax.ppermute(send_s, "narrow", swap)
    came_part = lax.ppermute(send_part, "narrow", swap)
    ctx, send_s = lax.optimization_barrier((ctx, send_s))
    away, kept = back_weights(
        meta_own, block_in, other_in, out_grad, other_grad, ctx, gq, gk, gv, qkv_w, ag, ash
    )
    away, ffn_own = lax.optimization_barrier((away, ffn_own))
    own_part, own_s = back_rows(
        meta_own, ctx, gq, gk, gv, ffn_own, sf_own, qkv_w, out_weight, ag, F32
    )
    d, hidden = up_weight.shape
    in_grad = finish(meta_own, block_in, out_grad, own_s, came_s)
    block_out = finish_out(block_in, own_part, came_part, row(out_bias), row(down_bias))
    gup, gdown, early_vec = unpack_front(early, d, hidden)
    early_vec = early_vec[:3] + lax.ppermute(early_vec, "narrow", swap)[:3], early_vec[8 : 8 + hidden // d]
    gates = [None, None, own_part, came_s, (early, in_grad), (gup, gdown), (block_out, early_vec)]
    mine, peer, small, gates = late_sum(
        meta_own, away, kept, wide_orders(lax.axis_size("wide")), gates
    )
    _, _, _, _, (_, in_grad), (gup, gdown), (block_out, early_vec) = gates
    gqkv, gout, gqkv_b, late_vec = unpack_late(
        meta_own, mine, peer, small, lax.ppermute(small, "narrow", swap), d, out_weight.shape[0]
    )
    vec, gup_b = early_vec
    return (
        block_out,
        in_grad,
        gqkv,
        gqkv_b[0],
        gout,
        vec[2],
        gup,
        gup_b.reshape(-1),
        gdown,
        vec[2],
        late_vec[0],
        late_vec[1],
        vec[0],
        vec[1],
    )


def solution(mesh):
    rows = P(("wide", "narrow"), None)
    placed = (
        rows,
        rows,
        P("wide", None),
        P(None, "narrow"),
        P("narrow"),
        P("narrow", None),
        P(),
        P(None, "narrow"),
        P("narrow"),
        P("narrow", None),
        P(),
        P(),
        P(),
        P(),
        P(),
    )
    return jax.shard_map(
        per_device,
        mesh=mesh,
        in_specs=placed,
        out_specs=(
            rows,
            rows,
            P(None, "narrow"),
            P("narrow"),
            P("narrow", None),
            P(),
            P(None, "narrow"),
            P("narrow"),
            P("narrow", None),
            P(),
            P(),
            P(),
            P(),
            P(),
        ),
        check_vma=False,
    )
```

```python
import functools

import jax
import jax.numpy as jnp
import numpy as np
from jax import lax
from jax.experimental import pallas as pl
from jax.experimental.pallas import tpu as pltpu
from jax.sharding import PartitionSpec as P

HD = 64
ROT = 16
EPS = 1e-05
NEG = -1e30
SCALE = 0.125
SHORT_LEN = 512
F32 = jnp.float32
BF = jnp.bfloat16
LANES = 128
BQ = 512
BS = 256
ROWS = 512
SMALL_LIMIT = 8 << 20
COST = pl.CostEstimate(flops=1 << 20, bytes_accessed=1 << 12, transcendentals=0)


def nn(a, b):
    return lax.dot_general(a, b, (((1,), (0,)), ((), ())), preferred_element_type=F32)


def nt(a, b):
    return lax.dot_general(a, b, (((1,), (1,)), ((), ())), preferred_element_type=F32)


def tn(a, b):
    return lax.dot_general(a, b, (((0,), (0,)), ((), ())), preferred_element_type=F32)


def colsum(a):
    return jnp.sum(a, axis=0, keepdims=True)


def rope_table(rows):
    half = ROT // 2
    freq = np.float32(1.0) / np.float32(10000.0) ** (
        np.arange(half, dtype=np.float32) * np.float32(2.0) / np.float32(ROT)
    )
    angle = np.arange(rows, dtype=np.float32)[:, None] * freq.astype(np.float32)[None, :]
    table = np.zeros((rows, 2 * HD), np.float32)
    table[:, :HD] = 1.0
    table[:, :half] = table[:, half:ROT] = np.cos(angle)
    table[:, HD : HD + half] = -np.sin(angle)
    table[:, HD + half : HD + ROT] = np.sin(angle)
    return table


def rope(x, table, back):
    lane = lax.broadcasted_iota(jnp.int32, x.shape, 1)
    other = pltpu.roll(table, HD, 1)
    cosine = jnp.where(lane < HD, table, other)
    sine = jnp.where(lane < HD, other, table)
    partner = jnp.where(
        lane % HD < ROT // 2, pltpu.roll(x, LANES - ROT // 2, 1), pltpu.roll(x, ROT // 2, 1)
    )
    return x * cosine - partner * sine if back else x * cosine + partner * sine


def normalize(x):
    center = jnp.mean(x, axis=-1, keepdims=True)
    offset = x - center
    inverse = lax.rsqrt(jnp.mean(offset * offset, axis=-1, keepdims=True) + EPS)
    return offset * inverse, inverse


def once(shape):
    return pl.BlockSpec(shape, lambda i, m: (0,) * len(shape), pipeline_mode=pl.Buffered(1))


def params(mib):
    return pltpu.CompilerParams(vmem_limit_bytes=mib << 20, dimension_semantics=("arbitrary",))


EXTRA = 16
SMALLS = 32


def project(first, qkv_w, qkv_b, table, qkv_ref):
    packed = nn(first, qkv_w[...]) + qkv_b[...].astype(F32)
    third = packed.shape[1] // 3
    for c in range(0, third, LANES):
        q = rope(packed[:, c : c + LANES], table, False).astype(BF)
        qkv_ref[:, c : c + LANES] = (q.astype(F32) * SCALE).astype(BF)
        k = rope(packed[:, third + c : third + c + LANES], table, False)
        qkv_ref[:, third + c : third + c + LANES] = k.astype(BF)
    qkv_ref[:, 2 * third :] = packed[:, 2 * third :].astype(BF)


def gelu_parts(hidden):
    phi = 0.5 * (1.0 + lax.erf(hidden * np.float32(0.5**0.5)))
    density = jnp.exp(-0.5 * hidden * hidden) * np.float32(1.0 / np.sqrt(2.0 * np.pi))
    return hidden * phi, phi + hidden * density


def front_own_kernel(meta, *refs):
    (x_ref, g_ref, qkv_w, qkv_b, up_w, up_b, down_w, out_w, ag, ash, fg, fsh, tab_ref), refs = (
        refs[:13],
        refs[13:],
    )
    (qkv_ref, gc_ref, ffn_ref, s_ref, up_acc, down_acc, vec_ref, vech_ref) = refs
    normed, _ = normalize(x_ref[...].astype(F32))
    g = g_ref[...]
    first = (normed * ag[...].astype(F32) + ash[...].astype(F32)).astype(BF)
    second = (normed * fg[...].astype(F32) + fsh[...].astype(F32)).astype(BF)

    @pl.when(pl.program_id(0) == 0)
    def _():
        for ref in (up_acc, down_acc, vec_ref, vech_ref):
            ref[...] = jnp.zeros_like(ref)

    project(first, qkv_w, qkv_b, tab_ref[...], qkv_ref)
    gc_ref[...] = nt(g, out_w[...]).astype(BF)
    act, slope = gelu_parts(nn(second, up_w[...]) + up_b[...].astype(F32))
    act = act.astype(BF)
    ffn_ref[...] = nn(act, down_w[...])
    gh = (nt(g, down_w[...]) * slope).astype(BF)
    gs = nt(gh, up_w[...])
    s_ref[...] = gs * fg[...].astype(F32)
    vec_ref[0:1, :] += colsum(gs * normed)
    vec_ref[1:2, :] += colsum(gs)
    vec_ref[2:3, :] += colsum(g.astype(F32))
    vech_ref[0:1, :] += colsum(gh.astype(F32))
    up_acc[...] += tn(second, gh)
    down_acc[...] += tn(act, g)


def front_forward_kernel(meta, *refs):
    x_ref, qkv_w, qkv_b, up_w, up_b, down_w, ag, ash, fg, fsh, tab_ref, _ = refs[:12]
    qkv_ref, ffn_ref, act_ref, slope_ref = refs[12:]
    normed, _ = normalize(x_ref[...].astype(F32))
    first = (normed * ag[...].astype(F32) + ash[...].astype(F32)).astype(BF)
    second = (normed * fg[...].astype(F32) + fsh[...].astype(F32)).astype(BF)
    project(first, qkv_w, qkv_b, tab_ref[...], qkv_ref)
    act, slope = gelu_parts(nn(second, up_w[...]) + up_b[...].astype(F32))
    act = act.astype(BF)
    act_ref[...] = act
    slope_ref[...] = slope
    ffn_ref[...] = nn(act, down_w[...])


def front_backward_kernel(meta, *refs):
    x_ref, g_ref, act_ref, slope_ref, up_w, down_w, out_w, fg, fsh, _, *sums_in = refs[:14]
    gc_ref, s_ref, packed_ref, *rest = refs[14:]
    sums, befores, sems = rest[:4], rest[4:8], rest[8]
    up_acc, down_acc, vec_ref, vech_ref = sums
    i = pl.program_id(0)
    copies = [
        pltpu.make_async_copy(src, dst, sems.at[k])
        for k, (src, dst) in enumerate(zip(sums_in, befores))
    ]

    @pl.when(i == 0)
    def _():
        for copy in copies:
            copy.start()
        for ref in sums:
            ref[...] = jnp.zeros_like(ref)

    normed, _ = normalize(x_ref[...].astype(F32))
    second = (normed * fg[...].astype(F32) + fsh[...].astype(F32)).astype(BF)
    g = g_ref[...]
    gc_ref[...] = nt(g, out_w[...]).astype(BF)
    gh = (nt(g, down_w[...]) * slope_ref[...]).astype(BF)
    gs = nt(gh, up_w[...])
    s_ref[...] = gs * fg[...].astype(F32)
    vec_ref[0:1, :] += colsum(gs * normed)
    vec_ref[1:2, :] += colsum(gs)
    vech_ref[0:1, :] += colsum(gh.astype(F32))
    up_acc[...] += tn(second, gh)
    down_acc[...] += tn(act_ref[...], g)

    @pl.when(i == pl.num_programs(0) - 1)
    def _():
        for copy in copies:
            copy.wait()
        up_in, down_in, vec_in, vech_in = befores
        d = up_acc.shape[0]
        hidden_rows = down_acc.shape[0]
        spare = [vec_ref[...] + vec_in[...]]
        for c in range(0, hidden_rows, d):
            packed_ref[c : c + d, :] = (up_acc[:, c : c + d] + up_in[:, c : c + d]).astype(BF)
            spare.append(vech_ref[0:1, c : c + d] + vech_in[0:1, c : c + d])
        packed_ref[hidden_rows : 2 * hidden_rows, :] = (down_acc[...] + down_in[...]).astype(BF)
        pad = EXTRA - vec_ref.shape[0] - (len(spare) - 1)
        spare.append(jnp.zeros((pad, d), F32))
        packed_ref[2 * hidden_rows :, :] = jnp.concatenate(spare, 0).astype(BF)


def front_call(kernel, name, mib, meta, x, ins, outs, aliases, flops, scratch=()):
    count = x.shape[0]
    steps = count // ROWS
    per_short = SHORT_LEN // ROWS

    def spec(shape, kind):
        if kind == "here":
            return pl.BlockSpec((ROWS, shape[1]), lambda i, m: (i, 0))
        if kind == "there":
            return pl.BlockSpec((ROWS, shape[1]), lambda i, m: (m[1] * steps + i, 0))
        if kind == "table":
            block = lambda i, m: m[1] * steps + i
            return pl.BlockSpec(
                (ROWS, shape[1]),
                lambda i, m: (jnp.where(m[0] == 1, block(i, m), lax.rem(block(i, m), per_short)), 0),
            )
        return pl.BlockSpec(memory_space=pl.ANY) if kind == "any" else once(shape)

    return pl.pallas_call(
        kernel,
        grid_spec=pltpu.PrefetchScalarGridSpec(
            num_scalar_prefetch=1,
            grid=(steps,),
            in_specs=[spec(a.shape, kind) for a, kind in ins],
            out_specs=[spec(shape, kind) for (shape, _), kind in outs],
            scratch_shapes=list(scratch),
        ),
        out_shape=[jax.ShapeDtypeStruct(*o) for o, _ in outs],
        input_output_aliases=aliases,
        compiler_params=params(mib),
        cost_estimate=pl.CostEstimate(
            flops=flops, bytes_accessed=16 << 20, transcendentals=0
        ),
        name=name,
    )(meta, *[a for a, _ in ins])


def sums_of(d, hidden):
    return [(d, hidden), (hidden, d), (8, d), (8, hidden)]


def front_own(meta, x, g, weights, table, group_rows):
    (count, d), cols, hidden = x.shape, weights[5].shape[0], weights[2].shape[1]
    return front_call(
        front_own_kernel,
        "front_own",
        44,
        meta,
        x,
        [(x, "here"), (g, "here"), *[(w, "once") for w in weights], (table, "table")],
        [
            (((group_rows, 3 * cols), BF), "there"),
            (((group_rows, cols), BF), "there"),
            (((count, d), F32), "here"),
            (((count, d), F32), "here"),
            *[((shape, F32), "once") for shape in sums_of(d, hidden)],
        ],
        {},
        2 * count * d * (6 * hidden + 4 * cols),
    )


def front_forward(meta, x, weights, table, qkv):
    qkv_w, qkv_b, up_w, up_b, down_w, out_w, ag, ash, fg, fsh = weights
    (count, d), hidden = x.shape, up_w.shape[1]
    once_in = [(w, "once") for w in (qkv_w, qkv_b, up_w, up_b, down_w, ag, ash, fg, fsh)]
    return front_call(
        front_forward_kernel,
        "front_forward",
        32,
        meta,
        x,
        [(x, "here"), *once_in, (table, "table"), (qkv, "any")],
        [
            ((qkv.shape, BF), "there"),
            (((count, d), F32), "here"),
            (((count, hidden), BF), "here"),
            (((count, hidden), F32), "here"),
        ],
        {12: 0},
        2 * count * d * (2 * hidden + qkv.shape[1]),
    )


def front_backward(meta, x, g, act, slope, weights, gc, sums):
    _, _, up_w, _, down_w, out_w, _, _, fg, fsh = weights
    (count, d), hidden = x.shape, up_w.shape[1]
    return front_call(
        front_backward_kernel,
        "front_backward",
        44,
        meta,
        x,
        [
            *[(a, "here") for a in (x, g, act, slope)],
            *[(w, "once") for w in (up_w, down_w, out_w, fg, fsh)],
            (gc, "any"),
            *[(a, "any") for a in sums],
        ],
        [
            ((gc.shape, BF), "there"),
            (((count, d), F32), "here"),
            (((2 * hidden + EXTRA, d), BF), "once"),
        ],
        {10: 0},
        2 * count * d * (4 * hidden + out_w.shape[0]),
        [pltpu.VMEM(shape, F32) for shape in sums_of(d, hidden)] * 2 + [pltpu.SemaphoreType.DMA((4,))],
    )


def unpack_front(packed, d, hidden):
    assert hidden == 2 * d
    steps = 6
    part = d // steps
    chunk = hidden // steps

    def kernel(p0, p1, p2, e_ref, up_ref, down_ref, vec_ref):
        up_ref[:, :d] = p0[...].astype(F32)
        up_ref[:, d:] = p1[...].astype(F32)
        down_ref[...] = p2[...].astype(F32)
        vec_ref[...] = e_ref[...].astype(F32)

    return pl.pallas_call(
        kernel,
        grid=(steps,),
        in_specs=[
            pl.BlockSpec((part, d), lambda i: (i, 0)),
            pl.BlockSpec((part, d), lambda i: (steps + i, 0)),
            pl.BlockSpec((chunk, d), lambda i: (steps + i, 0)),
            pl.BlockSpec((EXTRA, d), lambda i: (2 * hidden // EXTRA, 0)),
        ],
        out_specs=[
            pl.BlockSpec((part, hidden), lambda i: (i, 0)),
            pl.BlockSpec((chunk, d), lambda i: (i, 0)),
            pl.BlockSpec((EXTRA, d), lambda i: (0, 0)),
        ],
        out_shape=[
            jax.ShapeDtypeStruct((d, hidden), F32),
            jax.ShapeDtypeStruct((hidden, d), F32),
            jax.ShapeDtypeStruct((EXTRA, d), F32),
        ],
        compiler_params=params(16),
        cost_estimate=pl.CostEstimate(
            flops=2 * d * hidden, bytes_accessed=12 * d * hidden, transcendentals=0
        ),
        name="unpack_front",
    )(packed, packed, packed, packed)


def attention_kernel(meta, q_ref, k_ref, v_ref, do_ref, tab_ref, *refs):
    ctx_ref, dq_ref, dk_ref, dv_ref, s_sc, e_sc, ds_sc, kt_sc, vt_sc, dk_sc, dv_sc, *parts = refs
    qw_sc, qt_sc, gw_sc, gt_sc, acc_sc = parts
    i = pl.program_id(1)
    qb = meta[3 + i]
    long = meta[0]
    rows = k_ref.shape[0]
    half_cols = 2 * BS
    ext = HD + 16

    @pl.when(i == 0)
    def _():
        dk_sc[...] = jnp.zeros_like(dk_sc)
        dv_sc[...] = jnp.zeros_like(dv_sc)
        kt_sc[...] = k_ref[...].T
        ones = jnp.ones((16, rows), BF)
        vt = v_ref[...].T
        for h in range(2):
            vt_sc[h * ext : h * ext + HD, :] = vt[h * HD : (h + 1) * HD]
            vt_sc[h * ext + HD : (h + 1) * ext, :] = ones

    first_block = jnp.where(long == 1, 0, qb)
    zeros_t = jnp.zeros((HD, BS), BF)
    zeros = jnp.zeros((BS, LANES), BF)
    lane = lax.broadcasted_iota(jnp.int32, (BS, LANES), 1)

    def wide(t):
        return jnp.concatenate(
            [
                jnp.concatenate(pair, 0)
                for a in range(0, BQ, BS)
                for pair in ([t[:HD, a : a + BS], zeros_t], [zeros_t, t[HD:, a : a + BS]])
            ],
            1,
        )

    def tall(t):
        return jnp.concatenate(
            [
                block
                for a in range(0, BQ, BS)
                for block in (
                    jnp.where(lane < HD, t[a : a + BS], zeros),
                    jnp.where(lane < HD, zeros, t[a : a + BS]),
                )
            ],
            0,
        )

    def keys(b, tile=0, count=2):
        return pl.ds(pl.multiple_of(b * BQ + tile * BS, BS), count * BS)

    queries = q_ref[...]
    qw_sc[...], qt_sc[...] = wide(queries.T), tall(queries)
    key_index = lax.broadcasted_iota(jnp.int32, (BS, half_cols), 0)
    query_index = lax.broadcasted_iota(jnp.int32, (BS, half_cols), 1) % BS
    causal = key_index <= query_index
    fold = lambda s: jnp.max(s.reshape(BS // 8, 8, s.shape[1]), axis=0)

    s = nn(k_ref[keys(qb, 0, 1), :], qw_sc[...])
    s = jnp.concatenate([jnp.where(causal, s[:, :half_cols], NEG), s[:, half_cols:]], 1)
    s_sc[keys(qb, 0, 1), :] = s
    low = jnp.where(causal, nn(k_ref[keys(qb, 1, 1), :], qw_sc[:, half_cols:]), NEG)
    s_sc[keys(qb, 1, 1), half_cols:] = low
    top = fold(s)
    top = jnp.concatenate([top[:, :half_cols], jnp.maximum(top[:, half_cols:], fold(low))], 1)

    def score(b, top):
        for t in range(2):
            s = nn(k_ref[keys(b, t, 1), :], qw_sc[...])
            s_sc[keys(b, t, 1), :] = s
            top = jnp.maximum(top, fold(s))
        return top

    top = jnp.max(lax.fori_loop(first_block, qb, score, top), axis=0, keepdims=True)

    def exponent(rows, lo):
        e = jnp.exp(s_sc[rows, lo:] - top[:, lo:]).astype(BF)
        e_sc[rows, lo:] = e
        return e

    sides = [(a, h, a * half_cols + h * BS) for a in range(2) for h in range(2)]
    exponent(keys(qb, 0, 1), 0)
    exponent(keys(qb, 1, 1), half_cols)
    for a, h, c in sides:
        rows_of = keys(qb, 0, 1 + a)
        acc_sc[:, c : c + BS] = nn(vt_sc[h * ext : (h + 1) * ext, rows_of], e_sc[rows_of, c : c + BS])

    def gather(b, _):
        e = exponent(keys(b), 0)
        for _, h, c in sides:
            acc_sc[:, c : c + BS] += nn(vt_sc[h * ext : (h + 1) * ext, keys(b)], e[:, c : c + BS])
        return 0

    lax.fori_loop(first_block, qb, gather, 0)
    grad_t = do_ref[...].astype(F32).T
    ctx_parts, grad_parts, weighted = [[], []], [[], []], []
    for a, h, c in sides:
        over_total = 1.0 / acc_sc[HD : HD + 1, c : c + BS]
        ctx = acc_sc[:HD, c : c + BS] * over_total
        grad = (grad_t[h * HD : (h + 1) * HD, a * BS : (a + 1) * BS] * over_total).astype(BF)
        weighted.append(colsum(ctx * grad.astype(F32)))
        ctx_parts[a].append(ctx)
        grad_parts[a].append(grad)
    full = lambda parts: jnp.concatenate([jnp.concatenate(part, 0) for part in parts], 1)
    ctx_ref[...] = full(ctx_parts).T.astype(BF)
    grad_full = full(grad_parts)
    gw_sc[...], gt_sc[...] = wide(grad_full), tall(grad_full.T)
    weighted = jnp.concatenate(weighted, 1)

    def backward(rows, lo):
        e = e_sc[rows, lo:]
        gp = nn(v_ref[rows, :], gw_sc[:, lo:])
        ds = (e.astype(F32) * (gp - weighted[:, lo:])).astype(BF)
        ds_sc[rows, lo:] = ds
        dv_sc[rows, :] += nn(e, gt_sc[lo:, :])
        dk_sc[rows, :] += nn(ds, qt_sc[lo:, :])

    backward(keys(qb, 0, 1), 0)
    backward(keys(qb, 1, 1), half_cols)
    for a, h, c in sides:
        rows_of = keys(qb, 0, 1 + a)
        acc_sc[:HD, c : c + BS] = nn(kt_sc[h * HD : (h + 1) * HD, rows_of], ds_sc[rows_of, c : c + BS])

    def before(b, _):
        for t in range(2):
            backward(keys(b, t, 1), 0)
        for _, h, c in sides:
            acc_sc[:HD, c : c + BS] += nn(kt_sc[h * HD : (h + 1) * HD, keys(b)], ds_sc[keys(b), c : c + BS])
        return 0

    lax.fori_loop(first_block, qb, before, 0)
    dq = jnp.concatenate(
        [
            jnp.concatenate([acc_sc[:HD, c : c + BS] for b, _, c in sides if b == a], 0)
            for a in range(2)
        ],
        1,
    )
    at = pl.multiple_of(jnp.where(long == 1, qb, 0) * BQ, BQ)
    dq_ref[...] = rope(dq.T * SCALE, tab_ref[pl.ds(at, BQ), :], True).astype(BF)

    @pl.when(i == pl.num_programs(1) - 1)
    def _():
        dv_ref[...] = dv_sc[...].astype(BF)

        def finish(b, _):
            block = pl.ds(pl.multiple_of(b * BQ, BQ), BQ)
            at = pl.multiple_of(jnp.where(long == 1, b, 0) * BQ, BQ)
            dk_ref[block, :] = rope(dk_sc[block, :], tab_ref[pl.ds(at, BQ), :], True).astype(BF)
            return 0

        lax.fori_loop(0, rows // BQ, finish, 0)


def attention(meta, qkv, grad_ctx, table):
    rows, cols = grad_ctx.shape
    pairs, blocks = cols // LANES, rows // BQ
    at_query = lambda p, i, m: (m[3 + i], p)
    whole = lambda part: lambda p, i, m: (0, part * pairs + p)
    kept = jax.ShapeDtypeStruct((rows, cols), BF)
    return pl.pallas_call(
        attention_kernel,
        grid_spec=pltpu.PrefetchScalarGridSpec(
            num_scalar_prefetch=1,
            grid=(pairs, blocks),
            in_specs=[
                pl.BlockSpec((BQ, LANES), at_query),
                pl.BlockSpec((rows, LANES), whole(1)),
                pl.BlockSpec((rows, LANES), whole(2)),
                pl.BlockSpec((BQ, LANES), at_query),
                pl.BlockSpec((rows, LANES), lambda p, i, m: (0, 0), pipeline_mode=pl.Buffered(1)),
            ],
            out_specs=[
                pl.BlockSpec((BQ, LANES), at_query),
                pl.BlockSpec((BQ, LANES), at_query),
                pl.BlockSpec((rows, LANES), whole(0)),
                pl.BlockSpec((rows, LANES), whole(0)),
            ],
            scratch_shapes=[
                pltpu.VMEM((rows, 2 * BQ), F32),
                pltpu.VMEM((rows, 2 * BQ), BF),
                pltpu.VMEM((rows, 2 * BQ), BF),
                pltpu.VMEM((LANES, rows), BF),
                pltpu.VMEM((2 * (HD + 16), rows), BF),
                pltpu.VMEM((rows, LANES), F32),
                pltpu.VMEM((rows, LANES), F32),
                *[pltpu.VMEM((LANES, 2 * BQ), BF), pltpu.VMEM((2 * BQ, LANES), BF)] * 2,
                pltpu.VMEM((HD + 16, 2 * BQ), F32),
            ],
        ),
        out_shape=[kept] * 4,
        compiler_params=pltpu.CompilerParams(
            vmem_limit_bytes=32 << 20, dimension_semantics=("arbitrary", "arbitrary")
        ),
        cost_estimate=COST,
        name="attention",
    )(meta, qkv, qkv, qkv, grad_ctx, table)


def back_rows_kernel(meta, ctx_ref, gq_ref, gk_ref, gv_ref, ffn_ref, sf_ref, qkv_w, out_w, ag, part_ref, s_ref):
    part_ref[...] = (nn(ctx_ref[...], out_w[...]) + ffn_ref[...]).astype(part_ref.dtype)
    packed = jnp.concatenate([gq_ref[...], gk_ref[...], gv_ref[...]], axis=1)
    s_ref[...] = (nt(packed, qkv_w[...]) * ag[...].astype(F32) + sf_ref[...]).astype(s_ref.dtype)


def back_rows(meta, ctx, gq, gk, gv, ffn, sf, qkv_w, out_w, ag, kind):
    count, d = ffn.shape
    steps = count // ROWS
    cols = out_w.shape[0]
    here = pl.BlockSpec((ROWS, d), lambda i, m: (i, 0))
    there = pl.BlockSpec((ROWS, cols), lambda i, m: (m[1] * steps + i, 0))
    return pl.pallas_call(
        back_rows_kernel,
        grid_spec=pltpu.PrefetchScalarGridSpec(
            num_scalar_prefetch=1,
            grid=(steps,),
            in_specs=[there] * 4 + [here] * 2 + [once(qkv_w.shape), once(out_w.shape), once(ag.shape)],
            out_specs=[here, here],
        ),
        out_shape=[jax.ShapeDtypeStruct((count, d), kind)] * 2,
        compiler_params=params(24),
        cost_estimate=COST,
        name="back_rows",
    )(meta, ctx, gq, gk, gv, ffn, sf, qkv_w, out_w, ag)


def bit_of(me, bit):
    return lax.rem(lax.div(me, bit), 2)


def back_weights_kernel(meta, *refs):
    (x0_ref, x1_ref, g0_ref, g1_ref, ctx_ref, gq_ref, gk_ref, gv_ref, w_ref, ag, ash), refs = refs[:11], refs[11:]
    away_ref, kept_ref, qkv_acc, out_acc, bias_acc, all_sc = refs
    i = pl.program_id(0)
    steps = pl.num_programs(0)

    @pl.when(i == 0)
    def _():
        qkv_acc[...] = jnp.zeros_like(qkv_acc)
        out_acc[...] = jnp.zeros_like(out_acc)
        bias_acc[...] = jnp.zeros_like(bias_acc)

    own = i < steps // 2
    x = jnp.where(own, x0_ref[...].astype(F32), x1_ref[...].astype(F32))
    g = jnp.where(own, g0_ref[...], g1_ref[...])
    normed, _ = normalize(x)
    first = (normed * ag[...].astype(F32) + ash[...].astype(F32)).astype(BF)
    packed = jnp.concatenate([gq_ref[...], gk_ref[...], gv_ref[...]], axis=1)
    bias_acc[0:1, :] += colsum(packed.astype(F32))
    qkv_acc[...] += tn(first, packed)
    out_acc[...] += tn(ctx_ref[...], g)

    @pl.when(i == steps - 1)
    def _():
        d, width = qkv_acc.shape
        third = width // 3
        all_sc[:d, :width] = qkv_acc[...]
        all_sc[d:, :d] = out_acc[: 2 * third // 3, :]
        all_sc[d : d + third // 3, d:width] = out_acc[2 * third // 3 :, :third]
        all_sc[d + third // 3 :, d:width] = out_acc[2 * third // 3 :, third:]
        all_sc[:, width:] = jnp.zeros((all_sc.shape[0], LANES), F32)
        left = jnp.zeros((d, LANES), F32)
        right = jnp.zeros((d, LANES), F32)
        for c in range(0, width, LANES):
            w = w_ref[:, c : c + LANES].astype(F32)
            left += w * qkv_acc[:, c : c + LANES]
            right += w * bias_acc[0:1, c : c + LANES]
        shift_sum = colsum(right.T)
        gain_sum = (colsum(left.T) - ash[...].astype(F32) * shift_sum) / ag[...].astype(F32)
        quarter = all_sc.shape[0] // 4
        row = 0
        for vector in (bias_acc[0:1, :], gain_sum, shift_sum):
            for c in range(0, vector.shape[1], LANES):
                for base in (0, quarter):
                    all_sc[base + row : base + row + 1, width:] = vector[:, c : c + LANES]
                row += 1
        core = bit_of(meta[2], 1)
        for k in range(2):
            here = pl.multiple_of((2 * k + core) * quarter, quarter)
            there = pl.multiple_of((2 * k + 1 - core) * quarter, quarter)
            rows = slice(k * quarter, (k + 1) * quarter)
            kept_ref[rows, :] = all_sc[pl.ds(here, quarter), :]
            away_ref[rows, :] = all_sc[pl.ds(there, quarter), :].astype(BF)


def back_weights(meta, x_own, x_other, g_own, g_other, ctx, gq, gk, gv, qkv_w, ag, ash):
    half, d = x_own.shape
    steps = half // ROWS
    cols = ctx.shape[1]
    assert d == 2 * cols and cols % 3 == 0
    first = pl.BlockSpec((ROWS, d), lambda i, m: (jnp.minimum(i, steps - 1), 0))
    last = pl.BlockSpec((ROWS, d), lambda i, m: (jnp.maximum(i - steps, 0), 0))
    there = pl.BlockSpec(
        (ROWS, cols), lambda i, m: (lax.rem(m[1] * steps + i, 2 * steps), 0)
    )
    rows, width = d + 2 * cols // 3, 3 * cols + LANES
    return pl.pallas_call(
        back_weights_kernel,
        grid_spec=pltpu.PrefetchScalarGridSpec(
            num_scalar_prefetch=1,
            grid=(2 * steps,),
            in_specs=[first, last, first, last] + [there] * 4 + [once(a.shape) for a in (qkv_w, ag, ash)],
            out_specs=[once((rows // 2, width))] * 2,
            scratch_shapes=[
                pltpu.VMEM((d, 3 * cols), F32),
                pltpu.VMEM((cols, d), F32),
                pltpu.VMEM((8, 3 * cols), F32),
                pltpu.VMEM((rows, width), F32),
            ],
        ),
        out_shape=[
            jax.ShapeDtypeStruct((rows // 2, width), BF),
            jax.ShapeDtypeStruct((rows // 2, width), F32),
        ],
        compiler_params=params(32),
        cost_estimate=COST,
        name="back_weights",
    )(meta, x_own, x_other, g_own, g_other, ctx, gq, gk, gv, qkv_w, ag, ash)


def fold_kernel(bits, meta, *refs):
    if len(refs) == 6 and bits[0] is not None:
        rows = refs[0].shape[0] // 2
        ins = [r.at[pl.ds(k * rows, rows), :] for k in range(2) for r in refs[:2]]
        outs = refs[2:]
    else:
        ins, outs = refs[:4], refs[4:]
    for k, bit in enumerate(bits):
        kept, came = ins[2 * k], ins[2 * k + 1]
        if bit is None:
            outs[k][...] = (kept[...] + came[...].astype(F32)).astype(BF)
            continue
        away_ref, kept_ref = outs[2 * k], outs[2 * k + 1]
        half = kept_ref.shape[0]
        mine = bit_of(meta[2], bit)
        here = pl.ds(pl.multiple_of(mine * half, half), half)
        there = pl.ds(pl.multiple_of((1 - mine) * half, half), half)
        kept_ref[...] = kept[here, :] + came[here, :].astype(F32)
        away_ref[...] = (kept[there, :] + came[there, :].astype(F32)).astype(BF)


def spread_kernel(bits, join, meta, *refs):
    ins, outs = refs[:4], refs[4:]
    rows = ins[0].shape[0]
    for k, bit in enumerate(bits):
        out_ref, base = (outs[0], k * 2 * rows) if join else (outs[k], 0)
        mine = bit_of(meta[2], bit)
        out_ref[pl.ds(pl.multiple_of(base + mine * rows, rows), rows), :] = ins[2 * k][...]
        out_ref[pl.ds(pl.multiple_of(base + (1 - mine) * rows, rows), rows), :] = ins[2 * k + 1][...]
    if join:
        outs[1][...] = outs[0][:SMALLS, outs[0].shape[1] - LANES :].astype(F32)


def small_call(kernel, meta, ins, outs, name):
    size = sum(int(np.prod(shape)) for shape, _ in outs)
    held = pl.BlockSpec(memory_space=pltpu.VMEM)
    return pl.pallas_call(
        kernel,
        in_specs=[pl.BlockSpec(memory_space=pltpu.SMEM)] + [held] * len(ins),
        out_specs=[held] * len(outs),
        out_shape=[jax.ShapeDtypeStruct(*o) for o in outs],
        compiler_params=pltpu.CompilerParams(vmem_limit_bytes=SMALL_LIMIT),
        cost_estimate=pl.CostEstimate(flops=size, bytes_accessed=8 * size, transcendentals=0),
        name=name,
    )(meta, *ins)


def late_sum(meta, away, kept, orders, gates):
    gates = list(gates)

    def gated(step, values):
        if step < len(gates) and gates[step] is not None:
            values, gates[step] = lax.optimization_barrier((values, gates[step]))
        return values

    rows, width = kept.shape[0] // 2, kept.shape[1]
    came = swap_wide(away, 1)
    order_a, order_b = orders
    count = lax.axis_size("wide")
    if rows // (count // 2) < 16:
        parts = []
        for k, order in enumerate(orders):
            value = kept[k * rows : (k + 1) * rows] + came[k * rows : (k + 1) * rows].astype(F32)
            parts.append(gather_shares(scatter_sum(value, order[1:]), order[1:]))
        mine = jnp.concatenate(parts, 0)
        return mine, swap_wide(mine, 1), mine[:SMALLS, -LANES:].astype(F32), gates
    ins = [kept, came]
    steps = len(order_a)
    for step in range(1, steps):
        rows //= 2
        shapes = [((rows, width), BF), ((rows, width), F32)] * 2
        bits = (order_a[step], order_b[step])
        away_a, kept_a, away_b, kept_b = small_call(
            functools.partial(fold_kernel, bits), meta, ins, shapes, "fold"
        )
        ins = [kept_a, swap_wide(away_a, bits[0]), kept_b, swap_wide(away_b, bits[1])]
        ins = gated(step, ins)
    share_a, share_b = small_call(
        functools.partial(fold_kernel, (None, None)), meta, ins, [((rows, width), BF)] * 2, "fold"
    )
    for step in range(steps - 1, 0, -1):
        bits = (order_a[step], order_b[step])
        ins = [share_a, swap_wide(share_a, bits[0]), share_b, swap_wide(share_b, bits[1])]
        ins = gated(2 * steps - 1 - step, ins)
        last = step == 1
        shapes = [((4 * rows, width), BF)] if last else [((2 * rows, width), BF)] * 2
        if last:
            shapes.append(((SMALLS, LANES), F32))
        got = small_call(functools.partial(spread_kernel, bits, last), meta, ins, shapes, "spread")
        rows *= 2
        if not last:
            share_a, share_b = got
    return got[0], swap_wide(got[0], 1), got[1], gates


def unpack_late_kernel(meta, mine_ref, peer_ref, small_ref, came_ref, gqkv_ref, gout_ref, bias_ref, vec_ref, all_sc):
    d, width = gqkv_ref.shape
    third = width // 3
    quarter = mine_ref.shape[0] // 2
    core = bit_of(meta[2], 1)
    for k in range(2):
        rows = slice(k * quarter, (k + 1) * quarter)
        here = pl.multiple_of((2 * k + core) * quarter, quarter)
        there = pl.multiple_of((2 * k + 1 - core) * quarter, quarter)
        all_sc[pl.ds(here, quarter), :] = mine_ref[rows, :].astype(F32)
        all_sc[pl.ds(there, quarter), :] = peer_ref[rows, :].astype(F32)
    gout_ref[: 2 * third // 3, :] = all_sc[d:, :d]
    gout_ref[2 * third // 3 :, :third] = all_sc[d : d + third // 3, d:width]
    gout_ref[2 * third // 3 :, third:] = all_sc[d + third // 3 :, d:width]
    lane = lax.broadcasted_iota(jnp.int32, (1, LANES), 1)

    def pick(read, block, to):
        start = block % 3 * third + block // 3 * HD
        tile = read(start // LANES * LANES)
        return tile if start % LANES == to * HD else pltpu.roll(tile, HD, 1)

    count = width // LANES
    bias = jnp.concatenate([small_ref[c : c + 1, :] for c in range(count)], 1)
    bias8 = jnp.broadcast_to(bias, (8, width))
    for t in range(width // LANES):
        to = slice(t * LANES, (t + 1) * LANES)
        read = lambda c: all_sc[:d, c : c + LANES]
        gqkv_ref[:, to] = jnp.where(lane < HD, pick(read, 2 * t, 0), pick(read, 2 * t + 1, 1))
        read = lambda c: bias8[:, c : c + LANES]
        bias_ref[:, to] = jnp.where(lane < HD, pick(read, 2 * t, 0), pick(read, 2 * t + 1, 1))
    both = small_ref[...] + came_ref[...]
    per = d // LANES
    for k in range(2):
        start = count + k * per
        vec_ref[k : k + 1, :] = jnp.concatenate([both[c : c + 1, :] for c in range(start, start + per)], 1)
    vec_ref[2:, :] = jnp.zeros((vec_ref.shape[0] - 2, d), F32)


def unpack_late(meta, mine, peer, small, came, d, cols):
    width = 3 * cols
    whole = lambda shape: pl.BlockSpec(shape, lambda i, m: (0, 0))
    ins = [mine, peer, small, came]
    outs = [(d, width), (cols, d), (8, width), (8, d)]
    return pl.pallas_call(
        unpack_late_kernel,
        grid_spec=pltpu.PrefetchScalarGridSpec(
            num_scalar_prefetch=1,
            grid=(1,),
            in_specs=[whole(a.shape) for a in ins],
            out_specs=[whole(o) for o in outs],
            scratch_shapes=[pltpu.VMEM((2 * mine.shape[0], mine.shape[1]), F32)],
        ),
        out_shape=[jax.ShapeDtypeStruct(o, F32) for o in outs],
        compiler_params=params(24),
        cost_estimate=pl.CostEstimate(flops=4 * d * width, bytes_accessed=8 * d * width, transcendentals=0),
        name="unpack_late",
    )(meta, *ins)


def finish_kernel(meta, x_ref, g_ref, own_ref, came_ref, o_ref):
    normed, inverse = normalize(x_ref[...].astype(F32))
    s = own_ref[...] + came_ref[...].astype(F32)
    back_rows = inverse * (
        s
        - jnp.mean(s, axis=-1, keepdims=True)
        - normed * jnp.mean(s * normed, axis=-1, keepdims=True)
    )
    o_ref[...] = (g_ref[...].astype(F32) + back_rows).astype(BF)


def finish(meta, x, g, own, came):
    count, d = x.shape
    here = pl.BlockSpec((ROWS, d), lambda i, m: (i, 0))
    return pl.pallas_call(
        finish_kernel,
        grid_spec=pltpu.PrefetchScalarGridSpec(
            num_scalar_prefetch=1, grid=(count // ROWS,), in_specs=[here] * 4, out_specs=here
        ),
        out_shape=jax.ShapeDtypeStruct((count, d), BF),
        compiler_params=params(16),
        cost_estimate=pl.CostEstimate(flops=20 * count * d, bytes_accessed=14 * count * d, transcendentals=0),
        name="finish",
    )(meta, x, g, own, came)


def finish_out_kernel(x_ref, own_ref, came_ref, out_bias, down_bias, o_ref):
    bias = out_bias[...].astype(F32) + down_bias[...].astype(F32)
    o_ref[...] = (x_ref[...].astype(F32) + own_ref[...] + came_ref[...].astype(F32) + bias).astype(BF)


def finish_out(x, own, came, out_bias, down_bias):
    count, d = x.shape
    here = pl.BlockSpec((ROWS, d), lambda i: (i, 0))
    bias = pl.BlockSpec((1, d), lambda i: (0, 0))
    return pl.pallas_call(
        finish_out_kernel,
        grid=(count // ROWS,),
        in_specs=[here] * 3 + [bias] * 2,
        out_specs=here,
        out_shape=jax.ShapeDtypeStruct((count, d), BF),
        compiler_params=params(16),
        cost_estimate=pl.CostEstimate(flops=4 * count * d, bytes_accessed=10 * count * d, transcendentals=0),
        name="finish_out",
    )(x, own, came, out_bias, down_bias)


def regroup(w, heads):
    lead = w.shape[:-1]
    return jnp.swapaxes(w.reshape(*lead, heads, 3, HD), -3, -2).reshape(w.shape)


def wide_orders(count):
    bits = [1 << k for k in range(count.bit_length() - 1)]
    return bits, bits[:1] + bits[2:] + bits[1:2]


def swap_wide(value, bit):
    count = lax.axis_size("wide")
    return lax.ppermute(value, "wide", [(k, k ^ bit) for k in range(count)])


def scatter_sum(value, order):
    me = lax.axis_index("wide")
    for bit in order:
        half = value.shape[0] // 2
        mine = jnp.where((me & bit) == 0, 0, 1)
        away = lax.dynamic_slice_in_dim(value, (1 - mine) * half, half, 0).astype(BF)
        kept = lax.dynamic_slice_in_dim(value, mine * half, half, 0)
        value = kept.astype(F32) + swap_wide(away, bit).astype(F32)
    return value


def gather_shares(value, order):
    me = lax.axis_index("wide")
    value = value.astype(BF)
    for bit in reversed(order):
        came = swap_wide(value, bit)
        low = (me & bit) == 0
        value = jnp.concatenate([jnp.where(low, value, came), jnp.where(low, came, value)], 0)
    return value


def per_device(
    block_in,
    out_grad,
    seq_lens,
    qkv_weight,
    qkv_bias,
    out_weight,
    out_bias,
    up_weight,
    up_bias,
    down_weight,
    down_bias,
    attn_gain,
    attn_shift,
    ffn_gain,
    ffn_shift,
):
    swap = [(0, 1), (1, 0)]
    stay = lambda value: pltpu.with_memory_space_constraint(value, pltpu.HBM)
    other_in = lax.ppermute(block_in, "narrow", swap)
    other_grad = lax.ppermute(out_grad, "narrow", swap)
    half = block_in.shape[0]
    group_rows = 2 * half
    heads = out_weight.shape[0] // HD
    own = lax.axis_index("narrow").astype(jnp.int32)
    long = (seq_lens[0, 0] == group_rows).astype(jnp.int32)
    row = lambda v: v.reshape(1, -1)
    order = jnp.arange(group_rows // BQ, dtype=jnp.int32)
    me = lax.axis_index("wide").astype(jnp.int32)
    meta_own = jnp.concatenate([jnp.stack([long, own, me]), order])
    meta_other = jnp.concatenate([jnp.stack([long, 1 - own, me]), order])
    table = jnp.asarray(rope_table(group_rows))
    qkv_w = regroup(qkv_weight, heads)
    weights = (
        qkv_w,
        row(regroup(qkv_bias, heads)),
        up_weight,
        row(up_bias),
        down_weight,
        out_weight,
        row(attn_gain),
        row(attn_shift),
        row(ffn_gain),
        row(ffn_shift),
    )
    qkv, gc, ffn_own, sf_own, *sums = front_own(
        meta_own, block_in, out_grad, weights, table, group_rows
    )
    qkv, ffn_other, act, slope = front_forward(meta_other, other_in, weights, table, qkv)
    gc, sf_other, early = front_backward(
        meta_other, other_in, other_grad, act, slope, weights, gc, sums
    )
    ag, ash = row(attn_gain), row(attn_shift)
    early = lax.psum(early, "wide")
    ctx, gq, gk, gv = attention(meta_own, stay(qkv), stay(gc), stay(table))
    away, kept = back_weights(
        meta_own, block_in, other_in, out_grad, other_grad, ctx, gq, gk, gv, qkv_w, ag, ash
    )
    away, ffn_other = lax.optimization_barrier((away, ffn_other))
    send_part, send_s = back_rows(
        meta_other, ctx, gq, gk, gv, ffn_other, sf_other, qkv_w, out_weight, ag, BF
    )
    came_s = lax.ppermute(send_s, "narrow", swap)
    came_part = lax.ppermute(send_part, "narrow", swap)
    send_s, ffn_own = lax.optimization_barrier((send_s, ffn_own))
    own_part, own_s = back_rows(
        meta_own, ctx, gq, gk, gv, stay(ffn_own), stay(sf_own), qkv_w, out_weight, ag, F32
    )
    d, hidden = up_weight.shape
    in_grad = finish(meta_own, block_in, out_grad, own_s, came_s)
    block_out = finish_out(block_in, own_part, came_part, row(out_bias), row(down_bias))
    gup, gdown, early_vec = unpack_front(stay(early), d, hidden)
    early_vec = early_vec[:3] + lax.ppermute(early_vec, "narrow", swap)[:3], early_vec[8 : 8 + hidden // d]
    gates = [None, None, (own_part, came_s), in_grad, early, (gup, gdown), (block_out, early_vec)]
    mine, peer, small, gates = late_sum(
        meta_own, away, kept, wide_orders(lax.axis_size("wide")), gates
    )
    _, _, _, in_grad, _, (gup, gdown), (block_out, early_vec) = gates
    gqkv, gout, gqkv_b, late_vec = unpack_late(
        meta_own, mine, peer, small, lax.ppermute(small, "narrow", swap), d, out_weight.shape[0]
    )
    vec, gup_b = early_vec
    return (
        block_out,
        in_grad,
        gqkv,
        gqkv_b[0],
        gout,
        vec[2],
        gup,
        gup_b.reshape(-1),
        gdown,
        vec[2],
        late_vec[0],
        late_vec[1],
        vec[0],
        vec[1],
    )


def solution(mesh):
    rows = P(("wide", "narrow"), None)
    placed = (
        rows,
        rows,
        P("wide", None),
        P(None, "narrow"),
        P("narrow"),
        P("narrow", None),
        P(),
        P(None, "narrow"),
        P("narrow"),
        P("narrow", None),
        P(),
        P(),
        P(),
        P(),
        P(),
    )
    return jax.shard_map(
        per_device,
        mesh=mesh,
        in_specs=placed,
        out_specs=(
            rows,
            rows,
            P(None, "narrow"),
            P("narrow"),
            P("narrow", None),
            P(),
            P(None, "narrow"),
            P("narrow"),
            P("narrow", None),
            P(),
            P(),
            P(),
            P(),
            P(),
        ),
        check_vma=False,
    )
```

```python
import functools

import jax
import jax.numpy as jnp
import numpy as np
from jax import lax
from jax.experimental import pallas as pl
from jax.experimental.pallas import tpu as pltpu
from jax.sharding import PartitionSpec as P

HD = 64
ROT = 16
EPS = 1e-05
NEG = -1e30
SCALE = 0.125
SHORT_LEN = 512
F32 = jnp.float32
BF = jnp.bfloat16
LANES = 128
BQ = 512
BS = 256
ROWS = 512
SMALL_LIMIT = 8 << 20
COST = pl.CostEstimate(flops=1 << 20, bytes_accessed=1 << 12, transcendentals=0)


def nn(a, b):
    return lax.dot_general(a, b, (((1,), (0,)), ((), ())), preferred_element_type=F32)


def nt(a, b):
    return lax.dot_general(a, b, (((1,), (1,)), ((), ())), preferred_element_type=F32)


def tn(a, b):
    return lax.dot_general(a, b, (((0,), (0,)), ((), ())), preferred_element_type=F32)


def colsum(a):
    return jnp.sum(a, axis=0, keepdims=True)


def rope_table(rows):
    half = ROT // 2
    freq = np.float32(1.0) / np.float32(10000.0) ** (
        np.arange(half, dtype=np.float32) * np.float32(2.0) / np.float32(ROT)
    )
    angle = np.arange(rows, dtype=np.float32)[:, None] * freq.astype(np.float32)[None, :]
    table = np.zeros((rows, 2 * HD), np.float32)
    table[:, :HD] = 1.0
    table[:, :half] = table[:, half:ROT] = np.cos(angle)
    table[:, HD : HD + half] = -np.sin(angle)
    table[:, HD + half : HD + ROT] = np.sin(angle)
    return table


def rope(x, table, back):
    lane = lax.broadcasted_iota(jnp.int32, x.shape, 1)
    other = pltpu.roll(table, HD, 1)
    cosine = jnp.where(lane < HD, table, other)
    sine = jnp.where(lane < HD, other, table)
    partner = jnp.where(
        lane % HD < ROT // 2, pltpu.roll(x, LANES - ROT // 2, 1), pltpu.roll(x, ROT // 2, 1)
    )
    return x * cosine - partner * sine if back else x * cosine + partner * sine


def normalize(x):
    center = jnp.mean(x, axis=-1, keepdims=True)
    offset = x - center
    inverse = lax.rsqrt(jnp.mean(offset * offset, axis=-1, keepdims=True) + EPS)
    return offset * inverse, inverse


def once(shape):
    return pl.BlockSpec(shape, lambda i, m: (0,) * len(shape), pipeline_mode=pl.Buffered(1))


def params(mib):
    return pltpu.CompilerParams(vmem_limit_bytes=mib << 20, dimension_semantics=("arbitrary",))


EXTRA = 16
SMALLS = 32


def project(first, qkv_w, qkv_b, table, qkv_ref):
    packed = nn(first, qkv_w[...]) + qkv_b[...].astype(F32)
    third = packed.shape[1] // 3
    for c in range(0, third, LANES):
        q = rope(packed[:, c : c + LANES], table, False).astype(BF)
        qkv_ref[:, c : c + LANES] = (q.astype(F32) * SCALE).astype(BF)
        k = rope(packed[:, third + c : third + c + LANES], table, False)
        qkv_ref[:, third + c : third + c + LANES] = k.astype(BF)
    qkv_ref[:, 2 * third :] = packed[:, 2 * third :].astype(BF)


def gelu_parts(hidden):
    phi = 0.5 * (1.0 + lax.erf(hidden * np.float32(0.5**0.5)))
    density = jnp.exp(-0.5 * hidden * hidden) * np.float32(1.0 / np.sqrt(2.0 * np.pi))
    return hidden * phi, phi + hidden * density


def front_own_kernel(meta, *refs):
    (x_ref, g_ref, qkv_w, qkv_b, up_w, up_b, down_w, out_w, ag, ash, fg, fsh, tab_ref), refs = (
        refs[:13],
        refs[13:],
    )
    (qkv_ref, gc_ref, ffn_ref, s_ref, up_acc, down_acc, vec_ref, vech_ref) = refs
    normed, _ = normalize(x_ref[...].astype(F32))
    g = g_ref[...]
    first = (normed * ag[...].astype(F32) + ash[...].astype(F32)).astype(BF)
    second = (normed * fg[...].astype(F32) + fsh[...].astype(F32)).astype(BF)

    @pl.when(pl.program_id(0) == 0)
    def _():
        for ref in (up_acc, down_acc, vec_ref, vech_ref):
            ref[...] = jnp.zeros_like(ref)

    project(first, qkv_w, qkv_b, tab_ref[...], qkv_ref)
    gc_ref[...] = nt(g, out_w[...]).astype(BF)
    act, slope = gelu_parts(nn(second, up_w[...]) + up_b[...].astype(F32))
    act = act.astype(BF)
    ffn_ref[...] = nn(act, down_w[...])
    gh = (nt(g, down_w[...]) * slope).astype(BF)
    gs = nt(gh, up_w[...])
    s_ref[...] = gs * fg[...].astype(F32)
    vec_ref[0:1, :] += colsum(gs * normed)
    vec_ref[1:2, :] += colsum(gs)
    vec_ref[2:3, :] += colsum(g.astype(F32))
    vech_ref[0:1, :] += colsum(gh.astype(F32))
    up_acc[...] += tn(second, gh)
    down_acc[...] += tn(act, g)


def front_forward_kernel(meta, *refs):
    x_ref, qkv_w, qkv_b, up_w, up_b, down_w, ag, ash, fg, fsh, tab_ref, _ = refs[:12]
    qkv_ref, ffn_ref, act_ref, slope_ref = refs[12:]
    normed, _ = normalize(x_ref[...].astype(F32))
    first = (normed * ag[...].astype(F32) + ash[...].astype(F32)).astype(BF)
    second = (normed * fg[...].astype(F32) + fsh[...].astype(F32)).astype(BF)
    project(first, qkv_w, qkv_b, tab_ref[...], qkv_ref)
    act, slope = gelu_parts(nn(second, up_w[...]) + up_b[...].astype(F32))
    act = act.astype(BF)
    act_ref[...] = act
    slope_ref[...] = slope
    ffn_ref[...] = nn(act, down_w[...])


def front_backward_kernel(meta, *refs):
    x_ref, g_ref, act_ref, slope_ref, up_w, down_w, out_w, fg, fsh, _, *sums_in = refs[:14]
    gc_ref, s_ref, packed_ref, *rest = refs[14:]
    sums, befores, sems = rest[:4], rest[4:8], rest[8]
    up_acc, down_acc, vec_ref, vech_ref = sums
    i = pl.program_id(0)
    copies = [
        pltpu.make_async_copy(src, dst, sems.at[k])
        for k, (src, dst) in enumerate(zip(sums_in, befores))
    ]

    @pl.when(i == 0)
    def _():
        for copy in copies:
            copy.start()
        for ref in sums:
            ref[...] = jnp.zeros_like(ref)

    normed, _ = normalize(x_ref[...].astype(F32))
    second = (normed * fg[...].astype(F32) + fsh[...].astype(F32)).astype(BF)
    g = g_ref[...]
    gc_ref[...] = nt(g, out_w[...]).astype(BF)
    gh = (nt(g, down_w[...]) * slope_ref[...]).astype(BF)
    gs = nt(gh, up_w[...])
    s_ref[...] = gs * fg[...].astype(F32)
    vec_ref[0:1, :] += colsum(gs * normed)
    vec_ref[1:2, :] += colsum(gs)
    vech_ref[0:1, :] += colsum(gh.astype(F32))
    up_acc[...] += tn(second, gh)
    down_acc[...] += tn(act_ref[...], g)

    @pl.when(i == pl.num_programs(0) - 1)
    def _():
        for copy in copies:
            copy.wait()
        up_in, down_in, vec_in, vech_in = befores
        d = up_acc.shape[0]
        hidden_rows = down_acc.shape[0]
        spare = [vec_ref[...] + vec_in[...]]
        for c in range(0, hidden_rows, d):
            packed_ref[c : c + d, :] = (up_acc[:, c : c + d] + up_in[:, c : c + d]).astype(BF)
            spare.append(vech_ref[0:1, c : c + d] + vech_in[0:1, c : c + d])
        packed_ref[hidden_rows : 2 * hidden_rows, :] = (down_acc[...] + down_in[...]).astype(BF)
        pad = EXTRA - vec_ref.shape[0] - (len(spare) - 1)
        spare.append(jnp.zeros((pad, d), F32))
        packed_ref[2 * hidden_rows :, :] = jnp.concatenate(spare, 0).astype(BF)


def front_call(kernel, name, mib, meta, x, ins, outs, aliases, flops, scratch=()):
    count = x.shape[0]
    steps = count // ROWS
    per_short = SHORT_LEN // ROWS

    def spec(shape, kind):
        if kind == "here":
            return pl.BlockSpec((ROWS, shape[1]), lambda i, m: (i, 0))
        if kind == "there":
            return pl.BlockSpec((ROWS, shape[1]), lambda i, m: (m[1] * steps + i, 0))
        if kind == "table":
            block = lambda i, m: m[1] * steps + i
            return pl.BlockSpec(
                (ROWS, shape[1]),
                lambda i, m: (jnp.where(m[0] == 1, block(i, m), lax.rem(block(i, m), per_short)), 0),
            )
        return pl.BlockSpec(memory_space=pl.ANY) if kind == "any" else once(shape)

    return pl.pallas_call(
        kernel,
        grid_spec=pltpu.PrefetchScalarGridSpec(
            num_scalar_prefetch=1,
            grid=(steps,),
            in_specs=[spec(a.shape, kind) for a, kind in ins],
            out_specs=[spec(shape, kind) for (shape, _), kind in outs],
            scratch_shapes=list(scratch),
        ),
        out_shape=[jax.ShapeDtypeStruct(*o) for o, _ in outs],
        input_output_aliases=aliases,
        compiler_params=params(mib),
        cost_estimate=pl.CostEstimate(
            flops=flops, bytes_accessed=16 << 20, transcendentals=0
        ),
        name=name,
    )(meta, *[a for a, _ in ins])


def sums_of(d, hidden):
    return [(d, hidden), (hidden, d), (8, d), (8, hidden)]


def front_own(meta, x, g, weights, table, group_rows):
    (count, d), cols, hidden = x.shape, weights[5].shape[0], weights[2].shape[1]
    return front_call(
        front_own_kernel,
        "front_own",
        44,
        meta,
        x,
        [(x, "here"), (g, "here"), *[(w, "once") for w in weights], (table, "table")],
        [
            (((group_rows, 3 * cols), BF), "there"),
            (((group_rows, cols), BF), "there"),
            (((count, d), F32), "here"),
            (((count, d), F32), "here"),
            *[((shape, F32), "once") for shape in sums_of(d, hidden)],
        ],
        {},
        2 * count * d * (6 * hidden + 4 * cols),
    )


def front_forward(meta, x, weights, table, qkv):
    qkv_w, qkv_b, up_w, up_b, down_w, out_w, ag, ash, fg, fsh = weights
    (count, d), hidden = x.shape, up_w.shape[1]
    once_in = [(w, "once") for w in (qkv_w, qkv_b, up_w, up_b, down_w, ag, ash, fg, fsh)]
    return front_call(
        front_forward_kernel,
        "front_forward",
        32,
        meta,
        x,
        [(x, "here"), *once_in, (table, "table"), (qkv, "any")],
        [
            ((qkv.shape, BF), "there"),
            (((count, d), F32), "here"),
            (((count, hidden), BF), "here"),
            (((count, hidden), F32), "here"),
        ],
        {12: 0},
        2 * count * d * (2 * hidden + qkv.shape[1]),
    )


def front_backward(meta, x, g, act, slope, weights, gc, sums):
    _, _, up_w, _, down_w, out_w, _, _, fg, fsh = weights
    (count, d), hidden = x.shape, up_w.shape[1]
    return front_call(
        front_backward_kernel,
        "front_backward",
        44,
        meta,
        x,
        [
            *[(a, "here") for a in (x, g, act, slope)],
            *[(w, "once") for w in (up_w, down_w, out_w, fg, fsh)],
            (gc, "any"),
            *[(a, "any") for a in sums],
        ],
        [
            ((gc.shape, BF), "there"),
            (((count, d), F32), "here"),
            (((2 * hidden + EXTRA, d), BF), "once"),
        ],
        {10: 0},
        2 * count * d * (4 * hidden + out_w.shape[0]),
        [pltpu.VMEM(shape, F32) for shape in sums_of(d, hidden)] * 2 + [pltpu.SemaphoreType.DMA((4,))],
    )


def unpack_front(packed, d, hidden):
    assert hidden == 2 * d
    steps = 6
    part = d // steps
    chunk = hidden // steps

    def kernel(p0, p1, p2, e_ref, up_ref, down_ref, vec_ref):
        up_ref[:, :d] = p0[...].astype(F32)
        up_ref[:, d:] = p1[...].astype(F32)
        down_ref[...] = p2[...].astype(F32)
        vec_ref[...] = e_ref[...].astype(F32)

    return pl.pallas_call(
        kernel,
        grid=(steps,),
        in_specs=[
            pl.BlockSpec((part, d), lambda i: (i, 0)),
            pl.BlockSpec((part, d), lambda i: (steps + i, 0)),
            pl.BlockSpec((chunk, d), lambda i: (steps + i, 0)),
            pl.BlockSpec((EXTRA, d), lambda i: (2 * hidden // EXTRA, 0)),
        ],
        out_specs=[
            pl.BlockSpec((part, hidden), lambda i: (i, 0)),
            pl.BlockSpec((chunk, d), lambda i: (i, 0)),
            pl.BlockSpec((EXTRA, d), lambda i: (0, 0)),
        ],
        out_shape=[
            jax.ShapeDtypeStruct((d, hidden), F32),
            jax.ShapeDtypeStruct((hidden, d), F32),
            jax.ShapeDtypeStruct((EXTRA, d), F32),
        ],
        compiler_params=params(16),
        cost_estimate=pl.CostEstimate(
            flops=2 * d * hidden, bytes_accessed=12 * d * hidden, transcendentals=0
        ),
        name="unpack_front",
    )(packed, packed, packed, packed)


def attention_kernel(meta, q_ref, k_ref, v_ref, do_ref, tab_ref, *refs):
    ctx_ref, dq_ref, dk_ref, dv_ref, s_sc, e_sc, ds_sc, kt_sc, vt_sc, dk_sc, dv_sc, *parts = refs
    qw_sc, qt_sc, gw_sc, gt_sc, acc_sc = parts
    i = pl.program_id(1)
    qb = meta[3 + i]
    long = meta[0]
    rows = k_ref.shape[0]
    half_cols = 2 * BS
    ext = HD + 16

    @pl.when(i == 0)
    def _():
        dk_sc[...] = jnp.zeros_like(dk_sc)
        dv_sc[...] = jnp.zeros_like(dv_sc)
        kt_sc[...] = k_ref[...].T
        ones = jnp.ones((16, rows), BF)
        vt = v_ref[...].T
        for h in range(2):
            vt_sc[h * ext : h * ext + HD, :] = vt[h * HD : (h + 1) * HD]
            vt_sc[h * ext + HD : (h + 1) * ext, :] = ones

    first_block = jnp.where(long == 1, 0, qb)
    zeros_t = jnp.zeros((HD, BS), BF)
    zeros = jnp.zeros((BS, LANES), BF)
    lane = lax.broadcasted_iota(jnp.int32, (BS, LANES), 1)

    def wide(t):
        return jnp.concatenate(
            [
                jnp.concatenate(pair, 0)
                for a in range(0, BQ, BS)
                for pair in ([t[:HD, a : a + BS], zeros_t], [zeros_t, t[HD:, a : a + BS]])
            ],
            1,
        )

    def tall(t):
        return jnp.concatenate(
            [
                block
                for a in range(0, BQ, BS)
                for block in (
                    jnp.where(lane < HD, t[a : a + BS], zeros),
                    jnp.where(lane < HD, zeros, t[a : a + BS]),
                )
            ],
            0,
        )

    def keys(b, tile=0, count=2):
        return pl.ds(pl.multiple_of(b * BQ + tile * BS, BS), count * BS)

    queries = q_ref[...]
    qw_sc[...], qt_sc[...] = wide(queries.T), tall(queries)
    key_index = lax.broadcasted_iota(jnp.int32, (BS, half_cols), 0)
    query_index = lax.broadcasted_iota(jnp.int32, (BS, half_cols), 1) % BS
    causal = key_index <= query_index
    fold = lambda s: jnp.max(s.reshape(BS // 8, 8, s.shape[1]), axis=0)

    s = nn(k_ref[keys(qb, 0, 1), :], qw_sc[...])
    s = jnp.concatenate([jnp.where(causal, s[:, :half_cols], NEG), s[:, half_cols:]], 1)
    s_sc[keys(qb, 0, 1), :] = s
    low = jnp.where(causal, nn(k_ref[keys(qb, 1, 1), :], qw_sc[:, half_cols:]), NEG)
    s_sc[keys(qb, 1, 1), half_cols:] = low
    top = fold(s)
    top = jnp.concatenate([top[:, :half_cols], jnp.maximum(top[:, half_cols:], fold(low))], 1)

    def score(b, top):
        for t in range(2):
            s = nn(k_ref[keys(b, t, 1), :], qw_sc[...])
            s_sc[keys(b, t, 1), :] = s
            top = jnp.maximum(top, fold(s))
        return top

    top = jnp.max(lax.fori_loop(first_block, qb, score, top), axis=0, keepdims=True)

    def exponent(rows, lo):
        e = jnp.exp(s_sc[rows, lo:] - top[:, lo:]).astype(BF)
        e_sc[rows, lo:] = e
        return e

    sides = [(a, h, a * half_cols + h * BS) for a in range(2) for h in range(2)]
    exponent(keys(qb, 0, 1), 0)
    exponent(keys(qb, 1, 1), half_cols)
    for a, h, c in sides:
        rows_of = keys(qb, 0, 1 + a)
        acc_sc[:, c : c + BS] = nn(vt_sc[h * ext : (h + 1) * ext, rows_of], e_sc[rows_of, c : c + BS])

    def gather(b, _):
        e = exponent(keys(b), 0)
        for _, h, c in sides:
            acc_sc[:, c : c + BS] += nn(vt_sc[h * ext : (h + 1) * ext, keys(b)], e[:, c : c + BS])
        return 0

    lax.fori_loop(first_block, qb, gather, 0)
    grad_t = do_ref[...].astype(F32).T
    ctx_parts, grad_parts, weighted = [[], []], [[], []], []
    for a, h, c in sides:
        over_total = 1.0 / acc_sc[HD : HD + 1, c : c + BS]
        ctx = acc_sc[:HD, c : c + BS] * over_total
        grad = (grad_t[h * HD : (h + 1) * HD, a * BS : (a + 1) * BS] * over_total).astype(BF)
        weighted.append(colsum(ctx * grad.astype(F32)))
        ctx_parts[a].append(ctx)
        grad_parts[a].append(grad)
    full = lambda parts: jnp.concatenate([jnp.concatenate(part, 0) for part in parts], 1)
    ctx_ref[...] = full(ctx_parts).T.astype(BF)
    grad_full = full(grad_parts)
    gw_sc[...], gt_sc[...] = wide(grad_full), tall(grad_full.T)
    weighted = jnp.concatenate(weighted, 1)

    def backward(rows, lo):
        e = e_sc[rows, lo:]
        gp = nn(v_ref[rows, :], gw_sc[:, lo:])
        ds = (e.astype(F32) * (gp - weighted[:, lo:])).astype(BF)
        ds_sc[rows, lo:] = ds
        dv_sc[rows, :] += nn(e, gt_sc[lo:, :])
        dk_sc[rows, :] += nn(ds, qt_sc[lo:, :])

    backward(keys(qb, 0, 1), 0)
    backward(keys(qb, 1, 1), half_cols)
    for a, h, c in sides:
        rows_of = keys(qb, 0, 1 + a)
        acc_sc[:HD, c : c + BS] = nn(kt_sc[h * HD : (h + 1) * HD, rows_of], ds_sc[rows_of, c : c + BS])

    def before(b, _):
        for t in range(2):
            backward(keys(b, t, 1), 0)
        for _, h, c in sides:
            acc_sc[:HD, c : c + BS] += nn(kt_sc[h * HD : (h + 1) * HD, keys(b)], ds_sc[keys(b), c : c + BS])
        return 0

    lax.fori_loop(first_block, qb, before, 0)
    dq = jnp.concatenate(
        [
            jnp.concatenate([acc_sc[:HD, c : c + BS] for b, _, c in sides if b == a], 0)
            for a in range(2)
        ],
        1,
    )
    at = pl.multiple_of(jnp.where(long == 1, qb, 0) * BQ, BQ)
    dq_ref[...] = rope(dq.T * SCALE, tab_ref[pl.ds(at, BQ), :], True).astype(BF)

    @pl.when(i == pl.num_programs(1) - 1)
    def _():
        dv_ref[...] = dv_sc[...].astype(BF)

        def finish(b, _):
            block = pl.ds(pl.multiple_of(b * BQ, BQ), BQ)
            at = pl.multiple_of(jnp.where(long == 1, b, 0) * BQ, BQ)
            dk_ref[block, :] = rope(dk_sc[block, :], tab_ref[pl.ds(at, BQ), :], True).astype(BF)
            return 0

        lax.fori_loop(0, rows // BQ, finish, 0)


def attention(meta, qkv, grad_ctx, table):
    rows, cols = grad_ctx.shape
    pairs, blocks = cols // LANES, rows // BQ
    at_query = lambda p, i, m: (m[3 + i], p)
    whole = lambda part: lambda p, i, m: (0, part * pairs + p)
    kept = jax.ShapeDtypeStruct((rows, cols), BF)
    return pl.pallas_call(
        attention_kernel,
        grid_spec=pltpu.PrefetchScalarGridSpec(
            num_scalar_prefetch=1,
            grid=(pairs, blocks),
            in_specs=[
                pl.BlockSpec((BQ, LANES), at_query),
                pl.BlockSpec((rows, LANES), whole(1)),
                pl.BlockSpec((rows, LANES), whole(2)),
                pl.BlockSpec((BQ, LANES), at_query),
                pl.BlockSpec((rows, LANES), lambda p, i, m: (0, 0), pipeline_mode=pl.Buffered(1)),
            ],
            out_specs=[
                pl.BlockSpec((BQ, LANES), at_query),
                pl.BlockSpec((BQ, LANES), at_query),
                pl.BlockSpec((rows, LANES), whole(0)),
                pl.BlockSpec((rows, LANES), whole(0)),
            ],
            scratch_shapes=[
                pltpu.VMEM((rows, 2 * BQ), F32),
                pltpu.VMEM((rows, 2 * BQ), BF),
                pltpu.VMEM((rows, 2 * BQ), BF),
                pltpu.VMEM((LANES, rows), BF),
                pltpu.VMEM((2 * (HD + 16), rows), BF),
                pltpu.VMEM((rows, LANES), F32),
                pltpu.VMEM((rows, LANES), F32),
                *[pltpu.VMEM((LANES, 2 * BQ), BF), pltpu.VMEM((2 * BQ, LANES), BF)] * 2,
                pltpu.VMEM((HD + 16, 2 * BQ), F32),
            ],
        ),
        out_shape=[kept] * 4,
        compiler_params=pltpu.CompilerParams(
            vmem_limit_bytes=32 << 20, dimension_semantics=("arbitrary", "arbitrary")
        ),
        cost_estimate=COST,
        name="attention",
    )(meta, qkv, qkv, qkv, grad_ctx, table)


def back_rows_kernel(meta, ctx_ref, gq_ref, gk_ref, gv_ref, ffn_ref, sf_ref, qkv_w, out_w, ag, part_ref, s_ref):
    part_ref[...] = (nn(ctx_ref[...], out_w[...]) + ffn_ref[...]).astype(part_ref.dtype)
    packed = jnp.concatenate([gq_ref[...], gk_ref[...], gv_ref[...]], axis=1)
    s_ref[...] = (nt(packed, qkv_w[...]) * ag[...].astype(F32) + sf_ref[...]).astype(s_ref.dtype)


def back_rows(meta, ctx, gq, gk, gv, ffn, sf, qkv_w, out_w, ag, kind):
    count, d = ffn.shape
    steps = count // ROWS
    cols = out_w.shape[0]
    here = pl.BlockSpec((ROWS, d), lambda i, m: (i, 0))
    there = pl.BlockSpec((ROWS, cols), lambda i, m: (m[1] * steps + i, 0))
    return pl.pallas_call(
        back_rows_kernel,
        grid_spec=pltpu.PrefetchScalarGridSpec(
            num_scalar_prefetch=1,
            grid=(steps,),
            in_specs=[there] * 4 + [here] * 2 + [once(qkv_w.shape), once(out_w.shape), once(ag.shape)],
            out_specs=[here, here],
        ),
        out_shape=[jax.ShapeDtypeStruct((count, d), kind)] * 2,
        compiler_params=params(24),
        cost_estimate=COST,
        name="back_rows",
    )(meta, ctx, gq, gk, gv, ffn, sf, qkv_w, out_w, ag)


def bit_of(me, bit):
    return lax.rem(lax.div(me, bit), 2)


def back_weights_kernel(meta, *refs):
    (x0_ref, x1_ref, g0_ref, g1_ref, ctx_ref, gq_ref, gk_ref, gv_ref, w_ref, ag, ash), refs = refs[:11], refs[11:]
    away_ref, kept_ref, qkv_acc, out_acc, bias_acc, all_sc = refs
    i = pl.program_id(0)
    steps = pl.num_programs(0)

    @pl.when(i == 0)
    def _():
        qkv_acc[...] = jnp.zeros_like(qkv_acc)
        out_acc[...] = jnp.zeros_like(out_acc)
        bias_acc[...] = jnp.zeros_like(bias_acc)

    own = i < steps // 2
    x = jnp.where(own, x0_ref[...].astype(F32), x1_ref[...].astype(F32))
    g = jnp.where(own, g0_ref[...], g1_ref[...])
    normed, _ = normalize(x)
    first = (normed * ag[...].astype(F32) + ash[...].astype(F32)).astype(BF)
    packed = jnp.concatenate([gq_ref[...], gk_ref[...], gv_ref[...]], axis=1)
    bias_acc[0:1, :] += colsum(packed.astype(F32))
    qkv_acc[...] += tn(first, packed)
    out_acc[...] += tn(ctx_ref[...], g)

    @pl.when(i == steps - 1)
    def _():
        d, width = qkv_acc.shape
        third = width // 3
        all_sc[:d, :width] = qkv_acc[...]
        all_sc[d:, :d] = out_acc[: 2 * third // 3, :]
        all_sc[d : d + third // 3, d:width] = out_acc[2 * third // 3 :, :third]
        all_sc[d + third // 3 :, d:width] = out_acc[2 * third // 3 :, third:]
        all_sc[:, width:] = jnp.zeros((all_sc.shape[0], LANES), F32)
        left = jnp.zeros((d, LANES), F32)
        right = jnp.zeros((d, LANES), F32)
        for c in range(0, width, LANES):
            w = w_ref[:, c : c + LANES].astype(F32)
            left += w * qkv_acc[:, c : c + LANES]
            right += w * bias_acc[0:1, c : c + LANES]
        shift_sum = colsum(right.T)
        gain_sum = (colsum(left.T) - ash[...].astype(F32) * shift_sum) / ag[...].astype(F32)
        quarter = all_sc.shape[0] // 4
        row = 0
        for vector in (bias_acc[0:1, :], gain_sum, shift_sum):
            for c in range(0, vector.shape[1], LANES):
                for base in (0, quarter):
                    all_sc[base + row : base + row + 1, width:] = vector[:, c : c + LANES]
                row += 1
        core = bit_of(meta[2], 1)
        for k in range(2):
            here = pl.multiple_of((2 * k + core) * quarter, quarter)
            there = pl.multiple_of((2 * k + 1 - core) * quarter, quarter)
            rows = slice(k * quarter, (k + 1) * quarter)
            kept_ref[rows, :] = all_sc[pl.ds(here, quarter), :]
            away_ref[rows, :] = all_sc[pl.ds(there, quarter), :].astype(BF)


def back_weights(meta, x_own, x_other, g_own, g_other, ctx, gq, gk, gv, qkv_w, ag, ash):
    half, d = x_own.shape
    steps = half // ROWS
    cols = ctx.shape[1]
    assert d == 2 * cols and cols % 3 == 0
    first = pl.BlockSpec((ROWS, d), lambda i, m: (jnp.minimum(i, steps - 1), 0))
    last = pl.BlockSpec((ROWS, d), lambda i, m: (jnp.maximum(i - steps, 0), 0))
    there = pl.BlockSpec(
        (ROWS, cols), lambda i, m: (lax.rem(m[1] * steps + i, 2 * steps), 0)
    )
    rows, width = d + 2 * cols // 3, 3 * cols + LANES
    return pl.pallas_call(
        back_weights_kernel,
        grid_spec=pltpu.PrefetchScalarGridSpec(
            num_scalar_prefetch=1,
            grid=(2 * steps,),
            in_specs=[first, last, first, last] + [there] * 4 + [once(a.shape) for a in (qkv_w, ag, ash)],
            out_specs=[once((rows // 2, width))] * 2,
            scratch_shapes=[
                pltpu.VMEM((d, 3 * cols), F32),
                pltpu.VMEM((cols, d), F32),
                pltpu.VMEM((8, 3 * cols), F32),
                pltpu.VMEM((rows, width), F32),
            ],
        ),
        out_shape=[
            jax.ShapeDtypeStruct((rows // 2, width), BF),
            jax.ShapeDtypeStruct((rows // 2, width), F32),
        ],
        compiler_params=params(32),
        cost_estimate=COST,
        name="back_weights",
    )(meta, x_own, x_other, g_own, g_other, ctx, gq, gk, gv, qkv_w, ag, ash)


def fold_kernel(bits, meta, *refs):
    if len(refs) == 6 and bits[0] is not None:
        rows = refs[0].shape[0] // 2
        ins = [r.at[pl.ds(k * rows, rows), :] for k in range(2) for r in refs[:2]]
        outs = refs[2:]
    else:
        ins, outs = refs[:4], refs[4:]
    for k, bit in enumerate(bits):
        kept, came = ins[2 * k], ins[2 * k + 1]
        if bit is None:
            outs[k][...] = (kept[...] + came[...].astype(F32)).astype(BF)
            continue
        away_ref, kept_ref = outs[2 * k], outs[2 * k + 1]
        half = kept_ref.shape[0]
        mine = bit_of(meta[2], bit)
        here = pl.ds(pl.multiple_of(mine * half, half), half)
        there = pl.ds(pl.multiple_of((1 - mine) * half, half), half)
        kept_ref[...] = kept[here, :] + came[here, :].astype(F32)
        away_ref[...] = (kept[there, :] + came[there, :].astype(F32)).astype(BF)


def spread_kernel(bits, join, meta, *refs):
    ins, outs = refs[:4], refs[4:]
    rows = ins[0].shape[0]
    for k, bit in enumerate(bits):
        out_ref, base = (outs[0], k * 2 * rows) if join else (outs[k], 0)
        mine = bit_of(meta[2], bit)
        out_ref[pl.ds(pl.multiple_of(base + mine * rows, rows), rows), :] = ins[2 * k][...]
        out_ref[pl.ds(pl.multiple_of(base + (1 - mine) * rows, rows), rows), :] = ins[2 * k + 1][...]
    if join:
        outs[1][...] = outs[0][:SMALLS, outs[0].shape[1] - LANES :].astype(F32)


def small_call(kernel, meta, ins, outs, name):
    size = sum(int(np.prod(shape)) for shape, _ in outs)
    held = pl.BlockSpec(memory_space=pltpu.VMEM)
    return pl.pallas_call(
        kernel,
        in_specs=[pl.BlockSpec(memory_space=pltpu.SMEM)] + [held] * len(ins),
        out_specs=[held] * len(outs),
        out_shape=[jax.ShapeDtypeStruct(*o) for o in outs],
        compiler_params=pltpu.CompilerParams(vmem_limit_bytes=SMALL_LIMIT),
        cost_estimate=pl.CostEstimate(flops=size, bytes_accessed=8 * size, transcendentals=0),
        name=name,
    )(meta, *ins)


def late_sum(meta, away, kept, orders, gates):
    gates = list(gates)

    def gated(step, values):
        if step < len(gates) and gates[step] is not None:
            values, gates[step] = lax.optimization_barrier((values, gates[step]))
        return values

    rows, width = kept.shape[0] // 2, kept.shape[1]
    came = swap_wide(away, 1)
    order_a, order_b = orders
    count = lax.axis_size("wide")
    if rows // (count // 2) < 16:
        parts = []
        for k, order in enumerate(orders):
            value = kept[k * rows : (k + 1) * rows] + came[k * rows : (k + 1) * rows].astype(F32)
            parts.append(gather_shares(scatter_sum(value, order[1:]), order[1:]))
        mine = jnp.concatenate(parts, 0)
        return mine, swap_wide(mine, 1), mine[:SMALLS, -LANES:].astype(F32), gates
    ins = [kept, came]
    steps = len(order_a)
    for step in range(1, steps):
        rows //= 2
        shapes = [((rows, width), BF), ((rows, width), F32)] * 2
        bits = (order_a[step], order_b[step])
        away_a, kept_a, away_b, kept_b = small_call(
            functools.partial(fold_kernel, bits), meta, ins, shapes, "fold"
        )
        ins = [kept_a, swap_wide(away_a, bits[0]), kept_b, swap_wide(away_b, bits[1])]
        ins = gated(step, ins)
    share_a, share_b = small_call(
        functools.partial(fold_kernel, (None, None)), meta, ins, [((rows, width), BF)] * 2, "fold"
    )
    for step in range(steps - 1, 0, -1):
        bits = (order_a[step], order_b[step])
        ins = [share_a, swap_wide(share_a, bits[0]), share_b, swap_wide(share_b, bits[1])]
        ins = gated(2 * steps - 1 - step, ins)
        last = step == 1
        shapes = [((4 * rows, width), BF)] if last else [((2 * rows, width), BF)] * 2
        if last:
            shapes.append(((SMALLS, LANES), F32))
        got = small_call(functools.partial(spread_kernel, bits, last), meta, ins, shapes, "spread")
        rows *= 2
        if not last:
            share_a, share_b = got
    return got[0], swap_wide(got[0], 1), got[1], gates


def unpack_late_kernel(meta, mine_ref, peer_ref, small_ref, came_ref, gqkv_ref, gout_ref, bias_ref, vec_ref, all_sc):
    d, width = gqkv_ref.shape
    third = width // 3
    quarter = mine_ref.shape[0] // 2
    core = bit_of(meta[2], 1)
    for k in range(2):
        rows = slice(k * quarter, (k + 1) * quarter)
        here = pl.multiple_of((2 * k + core) * quarter, quarter)
        there = pl.multiple_of((2 * k + 1 - core) * quarter, quarter)
        all_sc[pl.ds(here, quarter), :] = mine_ref[rows, :].astype(F32)
        all_sc[pl.ds(there, quarter), :] = peer_ref[rows, :].astype(F32)
    gout_ref[: 2 * third // 3, :] = all_sc[d:, :d]
    gout_ref[2 * third // 3 :, :third] = all_sc[d : d + third // 3, d:width]
    gout_ref[2 * third // 3 :, third:] = all_sc[d + third // 3 :, d:width]
    lane = lax.broadcasted_iota(jnp.int32, (1, LANES), 1)

    def pick(read, block, to):
        start = block % 3 * third + block // 3 * HD
        tile = read(start // LANES * LANES)
        return tile if start % LANES == to * HD else pltpu.roll(tile, HD, 1)

    count = width // LANES
    bias = jnp.concatenate([small_ref[c : c + 1, :] for c in range(count)], 1)
    bias8 = jnp.broadcast_to(bias, (8, width))
    for t in range(width // LANES):
        to = slice(t * LANES, (t + 1) * LANES)
        read = lambda c: all_sc[:d, c : c + LANES]
        gqkv_ref[:, to] = jnp.where(lane < HD, pick(read, 2 * t, 0), pick(read, 2 * t + 1, 1))
        read = lambda c: bias8[:, c : c + LANES]
        bias_ref[:, to] = jnp.where(lane < HD, pick(read, 2 * t, 0), pick(read, 2 * t + 1, 1))
    both = small_ref[...] + came_ref[...]
    per = d // LANES
    for k in range(2):
        start = count + k * per
        vec_ref[k : k + 1, :] = jnp.concatenate([both[c : c + 1, :] for c in range(start, start + per)], 1)
    vec_ref[2:, :] = jnp.zeros((vec_ref.shape[0] - 2, d), F32)


def unpack_late(meta, mine, peer, small, came, d, cols):
    width = 3 * cols
    whole = lambda shape: pl.BlockSpec(shape, lambda i, m: (0, 0))
    ins = [mine, peer, small, came]
    outs = [(d, width), (cols, d), (8, width), (8, d)]
    return pl.pallas_call(
        unpack_late_kernel,
        grid_spec=pltpu.PrefetchScalarGridSpec(
            num_scalar_prefetch=1,
            grid=(1,),
            in_specs=[whole(a.shape) for a in ins],
            out_specs=[whole(o) for o in outs],
            scratch_shapes=[pltpu.VMEM((2 * mine.shape[0], mine.shape[1]), F32)],
        ),
        out_shape=[jax.ShapeDtypeStruct(o, F32) for o in outs],
        compiler_params=params(24),
        cost_estimate=pl.CostEstimate(flops=4 * d * width, bytes_accessed=8 * d * width, transcendentals=0),
        name="unpack_late",
    )(meta, *ins)


def finish_kernel(meta, x_ref, g_ref, own_ref, came_ref, o_ref):
    normed, inverse = normalize(x_ref[...].astype(F32))
    s = own_ref[...] + came_ref[...].astype(F32)
    back_rows = inverse * (
        s
        - jnp.mean(s, axis=-1, keepdims=True)
        - normed * jnp.mean(s * normed, axis=-1, keepdims=True)
    )
    o_ref[...] = (g_ref[...].astype(F32) + back_rows).astype(BF)


def finish(meta, x, g, own, came):
    count, d = x.shape
    here = pl.BlockSpec((ROWS, d), lambda i, m: (i, 0))
    return pl.pallas_call(
        finish_kernel,
        grid_spec=pltpu.PrefetchScalarGridSpec(
            num_scalar_prefetch=1, grid=(count // ROWS,), in_specs=[here] * 4, out_specs=here
        ),
        out_shape=jax.ShapeDtypeStruct((count, d), BF),
        compiler_params=params(16),
        cost_estimate=pl.CostEstimate(flops=20 * count * d, bytes_accessed=14 * count * d, transcendentals=0),
        name="finish",
    )(meta, x, g, own, came)


def finish_out_kernel(x_ref, own_ref, came_ref, out_bias, down_bias, o_ref):
    bias = out_bias[...].astype(F32) + down_bias[...].astype(F32)
    o_ref[...] = (x_ref[...].astype(F32) + own_ref[...] + came_ref[...].astype(F32) + bias).astype(BF)


def finish_out(x, own, came, out_bias, down_bias):
    count, d = x.shape
    here = pl.BlockSpec((ROWS, d), lambda i: (i, 0))
    bias = pl.BlockSpec((1, d), lambda i: (0, 0))
    return pl.pallas_call(
        finish_out_kernel,
        grid=(count // ROWS,),
        in_specs=[here] * 3 + [bias] * 2,
        out_specs=here,
        out_shape=jax.ShapeDtypeStruct((count, d), BF),
        compiler_params=params(16),
        cost_estimate=pl.CostEstimate(flops=4 * count * d, bytes_accessed=10 * count * d, transcendentals=0),
        name="finish_out",
    )(x, own, came, out_bias, down_bias)


def regroup(w, heads):
    lead = w.shape[:-1]
    return jnp.swapaxes(w.reshape(*lead, heads, 3, HD), -3, -2).reshape(w.shape)


def wide_orders(count):
    bits = [1 << k for k in range(count.bit_length() - 1)]
    return bits, bits[:1] + bits[2:] + bits[1:2]


def swap_wide(value, bit):
    count = lax.axis_size("wide")
    return lax.ppermute(value, "wide", [(k, k ^ bit) for k in range(count)])


def scatter_sum(value, order):
    me = lax.axis_index("wide")
    for bit in order:
        half = value.shape[0] // 2
        mine = jnp.where((me & bit) == 0, 0, 1)
        away = lax.dynamic_slice_in_dim(value, (1 - mine) * half, half, 0).astype(BF)
        kept = lax.dynamic_slice_in_dim(value, mine * half, half, 0)
        value = kept.astype(F32) + swap_wide(away, bit).astype(F32)
    return value


def gather_shares(value, order):
    me = lax.axis_index("wide")
    value = value.astype(BF)
    for bit in reversed(order):
        came = swap_wide(value, bit)
        low = (me & bit) == 0
        value = jnp.concatenate([jnp.where(low, value, came), jnp.where(low, came, value)], 0)
    return value


def per_device(
    block_in,
    out_grad,
    seq_lens,
    qkv_weight,
    qkv_bias,
    out_weight,
    out_bias,
    up_weight,
    up_bias,
    down_weight,
    down_bias,
    attn_gain,
    attn_shift,
    ffn_gain,
    ffn_shift,
):
    swap = [(0, 1), (1, 0)]
    stay = lambda value: pltpu.with_memory_space_constraint(value, pltpu.HBM)
    other_in = lax.ppermute(block_in, "narrow", swap)
    other_grad = lax.ppermute(out_grad, "narrow", swap)
    half = block_in.shape[0]
    group_rows = 2 * half
    heads = out_weight.shape[0] // HD
    own = lax.axis_index("narrow").astype(jnp.int32)
    long = (seq_lens[0, 0] == group_rows).astype(jnp.int32)
    row = lambda v: v.reshape(1, -1)
    order = jnp.arange(group_rows // BQ, dtype=jnp.int32)
    me = lax.axis_index("wide").astype(jnp.int32)
    meta_own = jnp.concatenate([jnp.stack([long, own, me]), order])
    meta_other = jnp.concatenate([jnp.stack([long, 1 - own, me]), order])
    table = jnp.asarray(rope_table(group_rows))
    qkv_w = regroup(qkv_weight, heads)
    weights = (
        qkv_w,
        row(regroup(qkv_bias, heads)),
        up_weight,
        row(up_bias),
        down_weight,
        out_weight,
        row(attn_gain),
        row(attn_shift),
        row(ffn_gain),
        row(ffn_shift),
    )
    qkv, gc, ffn_own, sf_own, *sums = front_own(
        meta_own, block_in, out_grad, weights, table, group_rows
    )
    qkv, ffn_other, act, slope = front_forward(meta_other, other_in, weights, table, qkv)
    gc, sf_other, early = front_backward(
        meta_other, other_in, other_grad, act, slope, weights, gc, sums
    )
    ag, ash = row(attn_gain), row(attn_shift)
    early = lax.psum(early, "wide")
    ctx, gq, gk, gv = attention(meta_own, stay(qkv), stay(gc), stay(table))
    away, kept = back_weights(
        meta_own, block_in, other_in, out_grad, other_grad, ctx, gq, gk, gv, qkv_w, ag, ash
    )
    away, ffn_other = lax.optimization_barrier((away, ffn_other))
    send_part, send_s = back_rows(
        meta_other, ctx, gq, gk, gv, ffn_other, sf_other, qkv_w, out_weight, ag, BF
    )
    came_s = lax.ppermute(send_s, "narrow", swap)
    came_part = lax.ppermute(send_part, "narrow", swap)
    send_s, ffn_own = lax.optimization_barrier((send_s, ffn_own))
    own_part, own_s = back_rows(
        meta_own, ctx, gq, gk, gv, stay(ffn_own), stay(sf_own), qkv_w, out_weight, ag, F32
    )
    d, hidden = up_weight.shape
    in_grad = finish(meta_own, block_in, out_grad, own_s, came_s)
    block_out = finish_out(block_in, own_part, came_part, row(out_bias), row(down_bias))
    gup, gdown, early_vec = unpack_front(early, d, hidden)
    early_vec = early_vec[:3] + lax.ppermute(early_vec, "narrow", swap)[:3], early_vec[8 : 8 + hidden // d]
    gates = [None, None, own_part, came_s, (early, in_grad), (gup, gdown), (block_out, early_vec)]
    mine, peer, small, gates = late_sum(
        meta_own, away, kept, wide_orders(lax.axis_size("wide")), gates
    )
    _, _, _, _, (_, in_grad), (gup, gdown), (block_out, early_vec) = gates
    gqkv, gout, gqkv_b, late_vec = unpack_late(
        meta_own, mine, peer, small, lax.ppermute(small, "narrow", swap), d, out_weight.shape[0]
    )
    vec, gup_b = early_vec
    return (
        block_out,
        in_grad,
        gqkv,
        gqkv_b[0],
        gout,
        vec[2],
        gup,
        gup_b.reshape(-1),
        gdown,
        vec[2],
        late_vec[0],
        late_vec[1],
        vec[0],
        vec[1],
    )


def solution(mesh):
    rows = P(("wide", "narrow"), None)
    placed = (
        rows,
        rows,
        P("wide", None),
        P(None, "narrow"),
        P("narrow"),
        P("narrow", None),
        P(),
        P(None, "narrow"),
        P("narrow"),
        P("narrow", None),
        P(),
        P(),
        P(),
        P(),
        P(),
    )
    return jax.shard_map(
        per_device,
        mesh=mesh,
        in_specs=placed,
        out_specs=(
            rows,
            rows,
            P(None, "narrow"),
            P("narrow"),
            P("narrow", None),
            P(),
            P(None, "narrow"),
            P("narrow"),
            P("narrow", None),
            P(),
            P(),
            P(),
            P(),
            P(),
        ),
        check_vma=False,
    )
```
